32 devices in a mesh: grp: 2 (over y), seq: 4 (over z), head: 4 (over x, core).
Axes of the slice: x: 2, y: 2, z: 4, core: 2. Of those that a mesh axis runs over, the one named last changes fastest.
Arguments:
- encoder: bfloat16 [8, 256, 4096], P('grp', 'seq'), parts along dimension 0, may hold values from -6 to 6
- key_weight: bfloat16 [4096, 4096], P('seq', 'head'), may hold values from -0.09375 to 0.09375
- value_weight: bfloat16 [4096, 4096], P('seq', 'head'), may hold values from -0.09375 to 0.09375
- tile_mask: int32 [2, 64, 64], P(None, 'seq', 'head'), may hold values 0 or 1
- lengths: int32 [8], P('grp'), parts along dimension 0, may hold values from 64 to 256, as said below
- queries: bfloat16 [8, 64, 4096], P('grp', 'seq', 'head'), parts along dimension 0, may hold values from -240 to 240
- cotangent: bfloat16 [8, 64, 4096], P('grp', 'seq', 'head'), parts along dimension 0, may hold values from -6 to 6
Outputs:
- attention: bfloat16 [8, 64, 4096], P('grp', 'seq', 'head'), parts along dimension 0
- query_grad: bfloat16 [8, 64, 4096], P('grp', 'seq', 'head'), parts along dimension 0
- encoder_grad: bfloat16 [8, 256, 4096], P('grp', 'seq', 'head'), parts along dimension 0
The draws below stay inside these ranges and needn't reach their ends.
There are 2 independent parts, one for each index of `grp`. The reference program is written for one: setup_inputs(seed, part) draws one part's arguments, and reference() takes and returns one part's arrays. A program takes and returns all parts, laid end to end along the dimension named above; an argument that names none is the same for every part. Nothing has to cross between parts.
Inputs may be any that keep to these rules, and one draw needn't show every extreme that they name: `lengths`: one document of each group has all 256 positions valid.
All inputs are finite; a program needn't handle non-finite values. No bound on the sum of `tile_mask` on one device may be relied on, other than what follows from the above.
Results may differ from the reference program's by a relative error of at most 0.0096.
Values may be sent and summed in bfloat16 or wider, within the bound.
No kernel may reach another device: no remote copies, remote signals or barrier semaphores. Data moves between devices by JAX's collectives and lax.ppermute only.
A program may use at most 128 MiB of HBM per device.

```python
import jax
import jax.numpy as jnp
from jax import lax

D = 4096
HEADS = 64
DH = 64
TILE = 64
DOCS = 4
ENC_LEN = 256
DEC_LEN = 64
HD = 4096


def draw_lengths(key, part):
    drawn = jax.random.randint(key, (DOCS,), ENC_LEN // 4, ENC_LEN + 1)
    longest = jax.random.randint(jax.random.fold_in(key, 3), (), 0, DOCS)
    return jnp.where(jnp.arange(DOCS) == longest, ENC_LEN, drawn).astype(jnp.int32)


def draw_queries(key, part):
    normal_draw = jax.random.normal(key, (DOCS, DEC_LEN, HEADS * DH), jnp.float32)
    normal_draw = jnp.clip(normal_draw, -6.0, 6.0)
    return normal_draw.astype(jnp.bfloat16)


def touch_ends(values, own_key, smallest, top_value):
    spot = [jax.random.randint(jax.random.fold_in(own_key, axis), (), 0, length) for axis, length in enumerate(values.shape)]
    main_axis = values.shape.index(max(values.shape))
    next_to = spot[:main_axis] + [(spot[main_axis] + 1) % values.shape[main_axis]] + spot[main_axis + 1:]
    return values.at[tuple(spot)].set(smallest).at[tuple(next_to)].set(top_value)


def levels(rng, shape, pieces, smallest, high):
    def one(axis_at, shards_of):
        draws = jax.random.uniform(jax.random.fold_in(jax.random.fold_in(rng, 6), axis_at), (shards_of,), jnp.float32, smallest / len(pieces), high / len(pieces))
        return jnp.repeat(jnp.exp(draws), shape[axis_at] // shards_of).reshape((-1,) + (1,) * (len(shape) - axis_at - 1))

    loudness = one(*pieces[0])
    for cut in pieces[1:]:
        loudness = loudness * one(*cut)
    return loudness


def normal_values(key, shape, deviation, reach, split=(), held_as=jnp.bfloat16):
    array = deviation * jax.random.normal(key, shape, jnp.float32)
    if split:
        array = array * levels(key, shape, split, -0.22, 0.18)
    return jnp.clip(array, -reach, reach).astype(held_as)


def setup_inputs(seed: int = 0, part: int = 0) -> dict:
    splits = jax.random.split(jax.random.key(seed), 8)
    part_splits = jax.random.split(jax.random.fold_in(splits[7], part), 8)
    encoder = normal_values(part_splits[0], (DOCS, ENC_LEN, D), 1.0, 6.0, ((1, 4),))
    key_weight = normal_values(splits[1], (D, HD), D ** -0.5, 0.09375, ((0, 4), (1, 4)))
    value_weight = normal_values(splits[2], (D, HD), D ** -0.5, 0.09375, ((0, 4), (1, 4)))
    tile_mask = touch_ends((jax.random.randint(splits[3], (2, D // TILE, HD // TILE), 0, 2) < 1).astype(jnp.int32), jax.random.fold_in(splits[3], 1), 0, 1)
    lengths = draw_lengths(jax.random.fold_in(jax.random.fold_in(splits[7], part), 71), part)
    queries = draw_queries(jax.random.fold_in(jax.random.fold_in(splits[7], part), 71), part)
    cotangent = normal_values(part_splits[6], (DOCS, DEC_LEN, HD), 1.0, 6.0, ((1, 4), (2, 4)))
    return {"encoder": encoder, "key_weight": key_weight, "value_weight": value_weight, "tile_mask": tile_mask, "lengths": lengths, "queries": queries, "cotangent": cotangent}


SCALE = 0.125
FLOOR_SCORE = -1e30


def expand(tile_grid, tile_edge):
    return jnp.repeat(jnp.repeat(tile_grid, tile_edge, axis=0), tile_edge, axis=1)


def attend(keys, values, queries, cotangent, length):
    position = jnp.arange(keys.shape[0])[None, :]
    live = position < length
    scores = jnp.dot(queries, keys.T, preferred_element_type=jnp.float32) * SCALE
    scores = jnp.where(live, scores, FLOOR_SCORE)
    row_max = jnp.max(scores, axis=1, keepdims=True)
    weights = jnp.where(live, jnp.exp(scores - row_max), 0.0)
    probs = weights / jnp.sum(weights, axis=1, keepdims=True)
    probs_low = probs.astype(jnp.bfloat16)
    output = jnp.dot(probs_low, values, preferred_element_type=jnp.float32)
    delta = jnp.sum(cotangent.astype(jnp.float32) * output, axis=1, keepdims=True)
    prob_grad = jnp.dot(cotangent, values.T, preferred_element_type=jnp.float32)
    score_grad = (probs * (prob_grad - delta) * SCALE).astype(jnp.bfloat16)
    query_grad = jnp.dot(score_grad, keys, preferred_element_type=jnp.float32)
    key_grad = jnp.dot(score_grad.T, queries, preferred_element_type=jnp.float32)
    value_grad = jnp.dot(probs_low.T, cotangent, preferred_element_type=jnp.float32)
    return (output.astype(jnp.bfloat16), query_grad.astype(jnp.bfloat16),
            key_grad.astype(jnp.bfloat16), value_grad.astype(jnp.bfloat16))


def reference(encoder, key_weight, value_weight, tile_mask, lengths, queries, cotangent):
    key_masked = key_weight * expand(tile_mask[0], TILE).astype(jnp.bfloat16)
    value_masked = value_weight * expand(tile_mask[1], TILE).astype(jnp.bfloat16)
    flat = encoder.reshape(DOCS * ENC_LEN, D)
    keys = jnp.dot(flat, key_masked, preferred_element_type=jnp.float32).astype(jnp.bfloat16)
    values = jnp.dot(flat, value_masked, preferred_element_type=jnp.float32).astype(jnp.bfloat16)

    def by_pair(block, rows):
        return block.reshape(DOCS, rows, HEADS, DH).transpose(0, 2, 1, 3).reshape(DOCS * HEADS, rows, DH)

    def by_row(block, rows):
        return block.reshape(DOCS, HEADS, rows, DH).transpose(0, 2, 1, 3).reshape(DOCS * rows, HEADS * DH)

    pair_length = jnp.repeat(lengths, HEADS)

    def one_pair(items):
        return attend(items[0], items[1], items[2], items[3], items[4])

    outputs, query_grads, key_grads, value_grads = lax.map(
        one_pair, (by_pair(keys, ENC_LEN), by_pair(values, ENC_LEN),
                   by_pair(queries, DEC_LEN), by_pair(cotangent, DEC_LEN), pair_length))
    key_rows = by_row(key_grads, ENC_LEN)
    value_rows = by_row(value_grads, ENC_LEN)
    grad_total = jnp.dot(key_rows, key_masked.T, preferred_element_type=jnp.float32)
    grad_total = grad_total + jnp.dot(value_rows, value_masked.T, preferred_element_type=jnp.float32)
    encoder_grad = grad_total.astype(jnp.bfloat16).reshape(DOCS, ENC_LEN, D)
    attention = by_row(outputs, DEC_LEN).reshape(DOCS, DEC_LEN, HD)
    query_grad = by_row(query_grads, DEC_LEN).reshape(DOCS, DEC_LEN, HD)
    return attention, query_grad, encoder_grad
```

```python
import functools

import jax
import jax.numpy as jnp
from jax import lax
from jax.experimental import pallas as pl
from jax.experimental.pallas import tpu as pltpu
from jax.sharding import PartitionSpec as P

DH = 64
TILE = 64
DOCS = 4


SCALE = 0.125
FLOOR_SCORE = -1e30

BF = jnp.bfloat16
F32 = jnp.float32


def expand(tile_grid, tile_edge):
    return jnp.repeat(jnp.repeat(tile_grid, tile_edge, axis=0), tile_edge, axis=1)


def attend(keys, values, queries, cotangent, length):
    position = jnp.arange(keys.shape[0])[None, :]
    live = position < length
    scores = jnp.dot(queries, keys.T, preferred_element_type=jnp.float32) * SCALE
    scores = jnp.where(live, scores, FLOOR_SCORE)
    row_max = jnp.max(scores, axis=1, keepdims=True)
    weights = jnp.where(live, jnp.exp(scores - row_max), 0.0)
    probs = weights / jnp.sum(weights, axis=1, keepdims=True)
    probs_low = probs.astype(jnp.bfloat16)
    output = jnp.dot(probs_low, values, preferred_element_type=jnp.float32)
    delta = jnp.sum(cotangent.astype(jnp.float32) * output, axis=1, keepdims=True)
    prob_grad = jnp.dot(cotangent, values.T, preferred_element_type=jnp.float32)
    score_grad = (probs * (prob_grad - delta) * SCALE).astype(jnp.bfloat16)
    query_grad = jnp.dot(score_grad, keys, preferred_element_type=jnp.float32)
    key_grad = jnp.dot(score_grad.T, queries, preferred_element_type=jnp.float32)
    value_grad = jnp.dot(probs_low.T, cotangent, preferred_element_type=jnp.float32)
    return (
        output.astype(jnp.bfloat16),
        query_grad.astype(jnp.bfloat16),
        key_grad.astype(jnp.bfloat16),
        value_grad.astype(jnp.bfloat16),
    )


def project(encoder, key_piece, value_piece):
    count = key_piece.shape[0]
    flat = encoder.reshape(DOCS * encoder.shape[1], count)
    key_flat = jnp.dot(flat, key_piece, preferred_element_type=jnp.float32)
    value_flat = jnp.dot(flat, value_piece, preferred_element_type=jnp.float32)
    shape_out = (DOCS, encoder.shape[1], key_piece.shape[1])
    return (key_flat.reshape(shape_out), value_flat.reshape(shape_out))


def back_product(key_rows, value_rows, key_piece, value_piece):
    contract = (((1,), (1,)), ((), ()))
    total = lax.dot_general(key_rows, key_piece, contract, preferred_element_type=jnp.float32)
    return total + lax.dot_general(
        value_rows, value_piece, contract, preferred_element_type=jnp.float32
    )


def general_body(encoder, key_weight, value_weight, tile_mask, lengths, queries, cotangent):
    seq_count = lax.axis_size("seq")
    enc_rows = encoder.shape[1]
    dec_rows = queries.shape[1]
    group_heads = queries.shape[2] // DH
    pair_count = DOCS * group_heads
    local_pairs = pair_count // seq_count
    key_masked = key_weight * expand(tile_mask[0], TILE).astype(jnp.bfloat16)
    value_masked = value_weight * expand(tile_mask[1], TILE).astype(jnp.bfloat16)
    full_key, full_value = (
        lax.all_gather(key_masked, "seq", axis=0, tiled=True),
        lax.all_gather(value_masked, "seq", axis=0, tiled=True),
    )
    key_sum, value_sum = project(encoder, full_key, full_value)

    def to_pairs(first, second, rows):
        joined = jnp.concatenate(
            [
                first.reshape(DOCS, rows, group_heads, DH),
                second.reshape(DOCS, rows, group_heads, DH),
            ],
            axis=3,
        )
        return joined.transpose(0, 2, 1, 3).reshape(pair_count, rows, 2 * DH)

    def from_pairs(block, rows):
        shaped = block.reshape(DOCS, group_heads, rows, 2 * DH).transpose(0, 2, 1, 3)
        first = shaped[..., :DH].reshape(DOCS, rows, group_heads * DH)
        second = shaped[..., DH:].reshape(DOCS, rows, group_heads * DH)
        return (first, second)

    query_pairs = to_pairs(queries, cotangent, dec_rows)
    query_owned = lax.all_to_all(query_pairs, "seq", split_axis=0, concat_axis=1, tiled=True)
    kv_pairs = to_pairs(key_sum.astype(jnp.bfloat16), value_sum.astype(jnp.bfloat16), enc_rows)
    kv_owned = lax.all_to_all(kv_pairs, "seq", split_axis=0, concat_axis=1, tiled=True)
    pair_ids = lax.axis_index("seq") * local_pairs + jnp.arange(local_pairs)
    doc_of_pair = pair_ids // group_heads
    pair_length = jnp.sum(
        jnp.where(doc_of_pair[:, None] == jnp.arange(DOCS)[None, :], lengths[None, :], 0), axis=1
    )

    def owner_pair(items):
        pair_kv, pair_query, length = items
        output, query_grad, key_grad, value_grad = attend(
            pair_kv[:, :DH], pair_kv[:, DH:], pair_query[:, :DH], pair_query[:, DH:], length
        )
        return (
            jnp.concatenate([output, query_grad], axis=1),
            jnp.concatenate([key_grad, value_grad], axis=1),
        )

    front, back = lax.map(owner_pair, (kv_owned, query_owned, pair_length))
    front_rows, back_rows = (
        lax.all_to_all(front, "seq", split_axis=1, concat_axis=0, tiled=True),
        lax.all_to_all(back, "seq", split_axis=1, concat_axis=0, tiled=True),
    )
    attention, query_grad = from_pairs(front_rows, dec_rows)
    key_grads, value_grads = from_pairs(back_rows, enc_rows)
    key_rows = key_grads.reshape(DOCS * enc_rows, group_heads * DH)
    value_rows = value_grads.reshape(DOCS * enc_rows, group_heads * DH)
    grad_terms = back_product(key_rows, value_rows, full_key, full_value)
    grad_share = lax.psum_scatter(grad_terms, "head", scatter_dimension=1, tiled=True)
    encoder_grad = grad_share.astype(jnp.bfloat16).reshape(DOCS, enc_rows, grad_share.shape[1])
    return (attention, query_grad, encoder_grad)


SEQ = 4
RING = (0, 1, 3, 2)


def fits(mesh, encoder, key_weight, queries):
    return (
        mesh.shape["seq"] == SEQ
        and mesh.shape["head"] == 4
        and mesh.shape["grp"] == 2
        and encoder.shape[0] == DOCS * 2
        and key_weight.shape[1] // 4 // SEQ == 4 * DH
        and key_weight.shape[0] == encoder.shape[2] == 4096
        and encoder.shape[1] == 256
        and queries.shape[1] == 64
    )


def prune_kernel(place, key_ref, value_ref, mask_ref, own_ref, *message_refs):
    rows = key_ref.shape[0]
    half = rows // 2
    s, g = place[0], place[1]

    def write(out_ref, first_tile, tiles, column):
        at = pl.ds(pl.multiple_of(column * 256, 256), 256)
        for t in range(tiles):
            tile = first_tile + t
            row = pl.ds(pl.multiple_of(tile * TILE, TILE), TILE)
            for side, ref in ((0, key_ref), (1, value_ref)):
                keep = mask_ref[side, pl.ds(tile, 1), at]
                out_ref[t * TILE : (t + 1) * TILE, side * 256 : (side + 1) * 256] = (
                    ref[row, at].astype(F32) * keep
                ).astype(BF)

    write(own_ref, 0, rows // TILE, s)
    for j, ref in enumerate(message_refs):
        write(ref, g * (half // TILE), half // TILE, lax.rem(s + j + 1, SEQ))


def prune(place, key_weight, value_weight, mask_columns):
    rows = key_weight.shape[0]
    whole = pl.BlockSpec(memory_space=pltpu.VMEM)
    return pl.pallas_call(
        prune_kernel,
        out_shape=[jax.ShapeDtypeStruct((rows, 512), BF)]
        + [jax.ShapeDtypeStruct((rows // 2, 512), BF)] * 3,
        in_specs=[pl.BlockSpec(memory_space=pltpu.SMEM)] + [whole] * 3,
        out_specs=[whole] * 4,
        name="prune",
    )(place, key_weight, value_weight, mask_columns)


NT = (((1,), (1,)), ((), ()))
TN = (((0,), (0,)), ((), ()))
NN = (((1,), (0,)), ((), ()))


def dot(a, b, dims=NN):
    return lax.dot_general(a, b, dims, preferred_element_type=F32)


def main_kernel(place, lengths, *refs):
    (
        enc, e1, e2, e3, x1, x2, x3,
        w_own, z1, z2, z3, y1, y2, y3,
        v_own, vz1, vz2, vz3, vy1, vy2, vy3,
        qc,
        att_ref, qg_ref,
        a0, a1, a2, a3, b0, b1, b2, b3, core_ref, own_ref,
        enc_s, w_s, grad_s, part_s, sems,
    ) = refs
    s, g, h = place[0], place[1], place[2]
    c = lax.rem(h, 2)
    x = h // 2
    origin = [place[3], place[4], place[5]]
    copies = []

    def move(src, dst):
        copy = pltpu.make_async_copy(src, dst, sems.at[len(copies)])
        copy.start()
        copies.append(copy)

    def rows_of(doc, at):
        return enc_s.at[doc, pl.ds(pl.multiple_of(at * 64, 64), 64)]

    for i in range(2):
        move(enc.at[2 * i + c], rows_of(i, s))
    for k, (mine, other) in enumerate(((e1, x1), (e2, x2), (e3, x3))):
        move(mine, rows_of(x, origin[k]))
        move(other, rows_of(1 - x, origin[k]))

    def weight_rows(core, at, half, count):
        return w_s.at[core, pl.ds(pl.multiple_of(at * 1024 + half * 512, 512), count)]

    for core, own, zs, ys in (
        (c, w_own, (z1, z2, z3), (y1, y2, y3)),
        (1 - c, v_own, (vz1, vz2, vz3), (vy1, vy2, vy3)),
    ):
        move(own, weight_rows(core, s, 0, 1024))
        for j in range(3):
            at = lax.rem(s + 3 - j, SEQ)
            move(zs[j], weight_rows(core, at, g, 512))
            move(ys[j], weight_rows(core, at, 1 - g, 512))
    for copy in copies:
        copy.wait()

    row_head = lax.broadcasted_iota(jnp.int32, (256, 256), 0) // DH
    col_head = lax.broadcasted_iota(jnp.int32, (256, 256), 1) // DH
    same = row_head == col_head
    position = lax.broadcasted_iota(jnp.int32, (256, 256), 1)

    def spread(block):
        four = jnp.concatenate([block] * 4, axis=0)
        return jnp.where(same, four, jnp.zeros_like(four))

    def gather_heads(block):
        kept = jnp.where(same, block, 0.0)
        return (kept[0:64] + kept[64:128]) + (kept[128:192] + kept[192:256])

    for core in range(2):
        for doc in range(2):
            both = dot(enc_s[doc], w_s[core])
            keys = both[:, :256].astype(BF)
            values = both[:, 256:].astype(BF)
            slot = lax.rem(core + c, 2)
            query = spread(qc[slot, 0, doc].reshape(64, 256))
            cot = spread(qc[slot, 1, doc].reshape(64, 256))
            live = position < lengths[2 * doc + c]
            scores = dot(query, keys, NT) * SCALE
            scores = jnp.where(live, scores, FLOOR_SCORE)
            row_max = jnp.max(scores, axis=1, keepdims=True)
            weights = jnp.where(live, jnp.exp(scores - row_max), 0.0)
            probs = weights / jnp.sum(weights, axis=1, keepdims=True)
            low = probs.astype(BF)
            output = dot(low, values)
            delta = jnp.sum(cot.astype(F32) * output, axis=1, keepdims=True)
            prob_grad = dot(cot, values, NT)
            score_grad = (probs * (prob_grad - delta) * SCALE).astype(BF)
            query_grad = dot(score_grad, keys)
            att_ref[slot, doc] = gather_heads(output).astype(BF)
            qg_ref[slot, doc] = gather_heads(query_grad).astype(BF)
            grad_s[core, doc * 256 : (doc + 1) * 256, 0:256] = dot(score_grad, query, TN).astype(BF)
            grad_s[core, doc * 256 : (doc + 1) * 256, 256:512] = dot(low, cot, TN).astype(BF)

    for flip, outs in ((2, (a0, a1, a2, a3)), (3, (b0, b1, b2, b3)), (1, None), (0, None)):
        block = lax.bitwise_xor(h, flip)

        def column(n, carry):
            at = pl.ds(pl.multiple_of(block * 1024 + n * 256, 256), 256)
            part = dot(grad_s[0], w_s[0, at, :], NT) + dot(grad_s[1], w_s[1, at, :], NT)
            part_s[:, :, pl.ds(pl.multiple_of(n * 256, 256), 256)] = part.reshape(2, 256, 256)
            return carry

        lax.fori_loop(0, 4, column, 0)
        for j in range(4):
            at = pl.ds(pl.multiple_of(lax.rem(s + j, SEQ) * 64, 64), 64)
            for doc in range(2):
                value = part_s[doc, at, :]
                if outs is not None:
                    outs[j][doc] = value.astype(BF)
                elif flip == 1:
                    core_ref[j, doc] = value.astype(BF)
                else:
                    own_ref[j, doc] = value


def main_call(place, lengths, arrays):
    here = pl.BlockSpec(memory_space=pl.ANY)
    vmem = pl.BlockSpec(memory_space=pltpu.VMEM)
    smem = pl.BlockSpec(memory_space=pltpu.SMEM)
    piece = jax.ShapeDtypeStruct((2, 64, 1024), BF)
    front = jax.ShapeDtypeStruct((2, 2, 64, 256), BF)
    return pl.pallas_call(
        main_kernel,
        out_shape=[front, front]
        + [piece] * 8
        + [jax.ShapeDtypeStruct((4, 2, 64, 1024), BF), jax.ShapeDtypeStruct((4, 2, 64, 1024), F32)],
        in_specs=[smem, smem] + [here] * 21 + [vmem],
        out_specs=[vmem] * 12,
        scratch_shapes=[
            pltpu.VMEM((2, 256, 4096), BF),
            pltpu.VMEM((2, 4096, 512), BF),
            pltpu.VMEM((2, 512, 512), BF),
            pltpu.VMEM((2, 256, 1024), F32),
            pltpu.SemaphoreType.DMA((22,)),
        ],
        compiler_params=pltpu.CompilerParams(vmem_limit_bytes=48 * 1024 * 1024),
        name="attend",
    )(place, lengths, *arrays)


def body(encoder, key_weight, value_weight, tile_mask, lengths, queries, cotangent):
    s, g, h = lax.axis_index("seq"), lax.axis_index("grp"), lax.axis_index("head")
    c = lax.rem(h, 2)
    ring = jnp.array(RING, jnp.int32)
    spot = jnp.array([RING.index(i) for i in range(SEQ)], jnp.int32)[s]
    origins = [ring[lax.rem(spot + SEQ - k, SEQ)] for k in (1, 2, 3)]
    place = jnp.stack([s, g, h] + origins).astype(jnp.int32)

    def shift(value, j):
        return lax.ppermute(value, "seq", [(a, (a + j) % SEQ) for a in range(SEQ)])

    def flip(value, bits):
        return lax.ppermute(value, "head", [(a, a ^ bits) for a in range(4)])

    def around(value):
        return lax.ppermute(value, "seq", [(RING[i], RING[(i + 1) % SEQ]) for i in range(SEQ)])

    def across(value):
        return lax.ppermute(value, "grp", [(0, 1), (1, 0)])

    mask_columns = jnp.repeat(tile_mask, TILE, axis=2).astype(F32)
    w_own, m1, m2, m3 = prune(place, key_weight, value_weight, mask_columns)
    e0 = lax.dynamic_index_in_dim(encoder, h, 0, keepdims=False)
    e1 = around(e0)
    z2 = shift(m2, 2)
    z1 = shift(m1, 1)
    z3 = shift(m3, 3)
    e2 = around(e1)
    e3 = around(e2)

    both = jnp.stack([queries, cotangent]).reshape(2, 2, 2, 16, 1024)
    mine = lax.dynamic_index_in_dim(both, c, 2, keepdims=False)
    theirs = flip(lax.dynamic_index_in_dim(both, 1 - c, 2, keepdims=False), 1)
    qc = jnp.stack([mine, theirs]).reshape(2, 2, 2, 16, SEQ, 256).transpose(4, 0, 1, 2, 3, 5)
    qc = lax.all_to_all(qc, "seq", split_axis=0, concat_axis=0, tiled=True)
    qc = qc.transpose(1, 2, 3, 0, 4, 5).reshape(2, 2, 2, 64, 256)

    x1, x2, x3 = flip(e1, 2), flip(e2, 2), flip(e3, 2)
    y2, y1, y3 = across(z2), across(z1), across(z3)
    firsts = [w_own, z1, z2, z3, y1, y2, y3]
    seconds = [flip(value, 1) for value in firsts]
    outs = main_call(place, lengths, [encoder, e1, e2, e3, x1, x2, x3] + firsts + seconds + [qc])
    att, qgrad = outs[0], outs[1]
    to_x, to_far, to_core, own = outs[2:6], outs[6:10], outs[10], outs[11]

    from_core = flip(to_core, 1)
    terms = []
    for j in (2, 1, 3, 0):
        near = flip(to_x[j], 2).astype(F32)
        far = flip(to_far[j], 3).astype(F32)
        summed = jnp.stack([own[j] + near, from_core[j].astype(F32) + far])
        if j:
            summed = shift(summed.astype(BF), j).astype(F32)
        terms.append(summed)
    total = ((terms[0] + terms[1]) + (terms[2] + terms[3])).astype(BF)
    total = jnp.where(c == 0, total, total[::-1])
    encoder_grad = total.transpose(1, 0, 2, 3).reshape(DOCS, 64, 1024)

    front = jnp.stack([att, qgrad], axis=1)
    other = flip(front[1], 1)
    back = jnp.stack([front[0], other]).reshape(2, 2, 2, SEQ, 16, 256).transpose(3, 0, 1, 2, 4, 5)
    back = lax.all_to_all(back, "seq", split_axis=0, concat_axis=0, tiled=True)
    back = back.transpose(2, 3, 1, 4, 0, 5).reshape(2, 2, 2, 16, 1024)
    back = jnp.where(c == 0, back, back[:, :, ::-1])
    back = back.reshape(2, DOCS, 16, 1024)
    return (back[0], back[1], encoder_grad)


def solution(mesh):
    placed = (
        P("grp", "seq", None),
        P("seq", "head"),
        P("seq", "head"),
        P(None, "seq", "head"),
        P("grp"),
        P("grp", "seq", "head"),
        P("grp", "seq", "head"),
    )

    def step(*arrays):
        plan = body if fits(mesh, arrays[0], arrays[1], arrays[5]) else general_body
        return jax.shard_map(
            plan,
            mesh=mesh,
            in_specs=placed,
            out_specs=(P("grp", "seq", "head"),) * 3,
            check_vma=False,
        )(*arrays)

    return step
```

```python
import functools

import jax
import jax.numpy as jnp
from jax import lax
from jax.experimental import pallas as pl
from jax.experimental.pallas import tpu as pltpu
from jax.sharding import PartitionSpec as P

DH = 64
TILE = 64
DOCS = 4


SCALE = 0.125
FLOOR_SCORE = -1e30

BF = jnp.bfloat16
F32 = jnp.float32


def expand(tile_grid, tile_edge):
    return jnp.repeat(jnp.repeat(tile_grid, tile_edge, axis=0), tile_edge, axis=1)


def attend(keys, values, queries, cotangent, length):
    position = jnp.arange(keys.shape[0])[None, :]
    live = position < length
    scores = jnp.dot(queries, keys.T, preferred_element_type=jnp.float32) * SCALE
    scores = jnp.where(live, scores, FLOOR_SCORE)
    row_max = jnp.max(scores, axis=1, keepdims=True)
    weights = jnp.where(live, jnp.exp(scores - row_max), 0.0)
    probs = weights / jnp.sum(weights, axis=1, keepdims=True)
    probs_low = probs.astype(jnp.bfloat16)
    output = jnp.dot(probs_low, values, preferred_element_type=jnp.float32)
    delta = jnp.sum(cotangent.astype(jnp.float32) * output, axis=1, keepdims=True)
    prob_grad = jnp.dot(cotangent, values.T, preferred_element_type=jnp.float32)
    score_grad = (probs * (prob_grad - delta) * SCALE).astype(jnp.bfloat16)
    query_grad = jnp.dot(score_grad, keys, preferred_element_type=jnp.float32)
    key_grad = jnp.dot(score_grad.T, queries, preferred_element_type=jnp.float32)
    value_grad = jnp.dot(probs_low.T, cotangent, preferred_element_type=jnp.float32)
    return (
        output.astype(jnp.bfloat16),
        query_grad.astype(jnp.bfloat16),
        key_grad.astype(jnp.bfloat16),
        value_grad.astype(jnp.bfloat16),
    )


def project(encoder, key_piece, value_piece):
    count = key_piece.shape[0]
    flat = encoder.reshape(DOCS * encoder.shape[1], count)
    key_flat = jnp.dot(flat, key_piece, preferred_element_type=jnp.float32)
    value_flat = jnp.dot(flat, value_piece, preferred_element_type=jnp.float32)
    shape_out = (DOCS, encoder.shape[1], key_piece.shape[1])
    return (key_flat.reshape(shape_out), value_flat.reshape(shape_out))


def back_product(key_rows, value_rows, key_piece, value_piece):
    contract = (((1,), (1,)), ((), ()))
    total = lax.dot_general(key_rows, key_piece, contract, preferred_element_type=jnp.float32)
    return total + lax.dot_general(
        value_rows, value_piece, contract, preferred_element_type=jnp.float32
    )


def general_body(encoder, key_weight, value_weight, tile_mask, lengths, queries, cotangent):
    seq_count = lax.axis_size("seq")
    enc_rows = encoder.shape[1]
    dec_rows = queries.shape[1]
    group_heads = queries.shape[2] // DH
    pair_count = DOCS * group_heads
    local_pairs = pair_count // seq_count
    key_masked = key_weight * expand(tile_mask[0], TILE).astype(jnp.bfloat16)
    value_masked = value_weight * expand(tile_mask[1], TILE).astype(jnp.bfloat16)
    full_key, full_value = (
        lax.all_gather(key_masked, "seq", axis=0, tiled=True),
        lax.all_gather(value_masked, "seq", axis=0, tiled=True),
    )
    key_sum, value_sum = project(encoder, full_key, full_value)

    def to_pairs(first, second, rows):
        joined = jnp.concatenate(
            [
                first.reshape(DOCS, rows, group_heads, DH),
                second.reshape(DOCS, rows, group_heads, DH),
            ],
            axis=3,
        )
        return joined.transpose(0, 2, 1, 3).reshape(pair_count, rows, 2 * DH)

    def from_pairs(block, rows):
        shaped = block.reshape(DOCS, group_heads, rows, 2 * DH).transpose(0, 2, 1, 3)
        first = shaped[..., :DH].reshape(DOCS, rows, group_heads * DH)
        second = shaped[..., DH:].reshape(DOCS, rows, group_heads * DH)
        return (first, second)

    query_pairs = to_pairs(queries, cotangent, dec_rows)
    query_owned = lax.all_to_all(query_pairs, "seq", split_axis=0, concat_axis=1, tiled=True)
    kv_pairs = to_pairs(key_sum.astype(jnp.bfloat16), value_sum.astype(jnp.bfloat16), enc_rows)
    kv_owned = lax.all_to_all(kv_pairs, "seq", split_axis=0, concat_axis=1, tiled=True)
    pair_ids = lax.axis_index("seq") * local_pairs + jnp.arange(local_pairs)
    doc_of_pair = pair_ids // group_heads
    pair_length = jnp.sum(
        jnp.where(doc_of_pair[:, None] == jnp.arange(DOCS)[None, :], lengths[None, :], 0), axis=1
    )

    def owner_pair(items):
        pair_kv, pair_query, length = items
        output, query_grad, key_grad, value_grad = attend(
            pair_kv[:, :DH], pair_kv[:, DH:], pair_query[:, :DH], pair_query[:, DH:], length
        )
        return (
            jnp.concatenate([output, query_grad], axis=1),
            jnp.concatenate([key_grad, value_grad], axis=1),
        )

    front, back = lax.map(owner_pair, (kv_owned, query_owned, pair_length))
    front_rows, back_rows = (
        lax.all_to_all(front, "seq", split_axis=1, concat_axis=0, tiled=True),
        lax.all_to_all(back, "seq", split_axis=1, concat_axis=0, tiled=True),
    )
    attention, query_grad = from_pairs(front_rows, dec_rows)
    key_grads, value_grads = from_pairs(back_rows, enc_rows)
    key_rows = key_grads.reshape(DOCS * enc_rows, group_heads * DH)
    value_rows = value_grads.reshape(DOCS * enc_rows, group_heads * DH)
    grad_terms = back_product(key_rows, value_rows, full_key, full_value)
    grad_share = lax.psum_scatter(grad_terms, "head", scatter_dimension=1, tiled=True)
    encoder_grad = grad_share.astype(jnp.bfloat16).reshape(DOCS, enc_rows, grad_share.shape[1])
    return (attention, query_grad, encoder_grad)


SEQ = 4
PIECE = 512
SENT = PIECE + 64


def fits(mesh, encoder, key_weight, queries):
    return (
        mesh.shape["seq"] == SEQ
        and mesh.shape["head"] == 4
        and mesh.shape["grp"] == 2
        and encoder.shape == (DOCS * 2, 256, 4096)
        and key_weight.shape == (4096, 4096)
        and queries.shape == (DOCS * 2, 64, 4096)
    )


def gray(value):
    return lax.bitwise_xor(value, value // 2)


def ring_back(s, k):
    return gray(lax.rem(gray(s) + SEQ - k, SEQ))


def prune_kernel(mask_ref, key_ref, value_ref, query_ref, cot_ref, own_ref, *message_refs):
    s, g = lax.axis_index("seq"), lax.axis_index("grp")
    left = lax.broadcasted_iota(jnp.int32, (1, 128), 1) < TILE

    def write(out_ref, first_tile, tiles, column):
        for t in range(tiles):
            tile = first_tile + t
            row = pl.ds(pl.multiple_of(tile * TILE, TILE), TILE)
            for side, ref in ((0, key_ref), (1, value_ref)):
                for part in range(2):
                    at = pl.ds(pl.multiple_of(column * 256 + part * 128, 128), 128)
                    first = mask_ref[side, tile, column * 4 + part * 2]
                    second = mask_ref[side, tile, column * 4 + part * 2 + 1]
                    keep = jnp.where(left, first, second).astype(F32)
                    to = side * 256 + part * 128
                    out_ref[t * TILE : (t + 1) * TILE, to : to + 128] = (
                        ref[row, at].astype(F32) * keep
                    ).astype(BF)
        at = pl.ds(pl.multiple_of(column * 256, 256), 256)
        out_ref[tiles * TILE :, 0:256] = query_ref[:, at]
        out_ref[tiles * TILE :, 256:512] = cot_ref[:, at]

    for j in (2, 1, 3):
        write(message_refs[j - 1], g * 8, 8, lax.rem(s + j, SEQ))
    write(own_ref, 0, 16, s)


def prune(tile_mask, key_weight, value_weight, queries, cotangent):
    whole = pl.BlockSpec(memory_space=pltpu.VMEM)
    return pl.pallas_call(
        prune_kernel,
        out_shape=[jax.ShapeDtypeStruct((2 * PIECE + 64, 512), BF)]
        + [jax.ShapeDtypeStruct((SENT, 512), BF)] * 3,
        in_specs=[pl.BlockSpec(memory_space=pltpu.SMEM)] + [whole] * 4,
        out_specs=[whole] * 4,
        name="prune",
    )(tile_mask, key_weight, value_weight, queries, cotangent)


NT = (((1,), (1,)), ((), ()))
TN = (((0,), (0,)), ((), ()))
NN = (((1,), (0,)), ((), ()))


def dot(a, b, dims=NN):
    return lax.dot_general(a, b, dims, preferred_element_type=F32)


def partial_blocks(block, grad, weight, part):
    def column(n, carry):
        at = pl.ds(pl.multiple_of(block * 1024 + n * 256, 256), 256)
        total = dot(grad[0], weight[0, at, :], NT) + dot(grad[1], weight[1, at, :], NT)
        part[:, :, pl.ds(pl.multiple_of(n * 256, 256), 256)] = total.reshape(2, 256, 256)
        return carry

    lax.fori_loop(0, 4, column, 0)


def main_kernel(lengths, *refs):
    (
        enc, ea, eb, ec, ed, ef, xa, xb, xc, xd, xf,
        w_own, z1, z2, z3, y1, y2, y3,
        v_own, vz1, vz2, vz3, vy1, vy2, vy3,
        att_ref, qg_ref, grad_ref, weight_ref,
        a1, a2, a30, b1, b2, b3, b0, core_ref,
        enc_s, w_s, qc_s, grad_s, part_s, sems,
    ) = refs
    s, g, h = lax.axis_index("seq"), lax.axis_index("grp"), lax.axis_index("head")
    c = lax.rem(h, 2)
    x = h // 2
    middle = jnp.logical_or(s == 1, s == 2)
    copies = []

    def move(src, dst, other=None):
        sem = sems.at[len(copies)]
        copy = pltpu.make_async_copy(src, dst, sem)
        if other is None:
            copy.start()
        else:
            pl.when(middle)(lambda: copy.start())
            pl.when(jnp.logical_not(middle))(lambda: pltpu.make_async_copy(other, dst, sem).start())
        copies.append(copy)

    def rows_of(doc, at):
        return enc_s.at[doc, pl.ds(pl.multiple_of(at * 64, 64), 64)]

    low_half = s < 2
    second = jnp.where(low_half, 2, 1)
    third = jnp.where(low_half, 3, 0)
    for i in range(2):
        move(enc.at[2 * i + c], rows_of(i, s))
    for doc, first_from, second_from, third_from in (
        (x, ea, (eb, ed), (ec, ef)),
        (1 - x, xa, (xb, xd), (xc, xf)),
    ):
        move(first_from, rows_of(doc, lax.bitwise_xor(s, 1)))
        move(second_from[0], rows_of(doc, second), second_from[1])
        move(third_from[0], rows_of(doc, third), third_from[1])

    def weight_rows(core, at, half, count):
        return w_s.at[core, pl.ds(pl.multiple_of(at * 1024 + half * PIECE, PIECE), count)]

    for core, own, zs, ys in (
        (c, w_own, (z1, z2, z3), (y1, y2, y3)),
        (1 - c, v_own, (vz1, vz2, vz3), (vy1, vy2, vy3)),
    ):
        move(own.at[0 : 2 * PIECE], weight_rows(core, s, 0, 2 * PIECE))
        move(own.at[2 * PIECE : 2 * PIECE + 64], qc_s.at[core, s])
        for j in range(3):
            at = lax.rem(s + 3 - j, SEQ)
            move(zs[j].at[0:PIECE], weight_rows(core, at, g, PIECE))
            move(ys[j].at[0:PIECE], weight_rows(core, at, 1 - g, PIECE))
            move(zs[j].at[PIECE:SENT], qc_s.at[core, at])
    for copy in copies:
        copy.wait()
    save = pltpu.make_async_copy(w_s, weight_ref, sems.at[0])
    save.start()

    row_head = lax.broadcasted_iota(jnp.int32, (256, 256), 0) // DH
    col_head = lax.broadcasted_iota(jnp.int32, (256, 256), 1) // DH
    same = row_head == col_head
    position = lax.broadcasted_iota(jnp.int32, (256, 256), 1)

    def spread(block):
        four = jnp.concatenate([block] * 4, axis=0)
        return jnp.where(same, four, jnp.zeros_like(four))

    def gather_heads(block):
        kept = jnp.where(same, block, 0.0)
        return (kept[0:64] + kept[64:128]) + (kept[128:192] + kept[192:256])

    for core in range(2):
        slot = lax.rem(core + c, 2)
        for doc in range(2):
            both = dot(enc_s[doc], w_s[core])
            keys = both[:, :256].astype(BF)
            values = both[:, 256:].astype(BF)
            at = pl.ds(pl.multiple_of((2 * doc + c) * 16, 16), 16)
            query = spread(qc_s[core, :, at, 0:256].reshape(64, 256))
            cot = spread(qc_s[core, :, at, 256:512].reshape(64, 256))
            live = position < lengths[2 * doc + c]
            scores = dot(query, keys, NT) * SCALE
            scores = jnp.where(live, scores, FLOOR_SCORE)
            row_max = jnp.max(scores, axis=1, keepdims=True)
            weights = jnp.where(live, jnp.exp(scores - row_max), 0.0)
            probs = weights / jnp.sum(weights, axis=1, keepdims=True)
            low = probs.astype(BF)
            output = dot(low, values)
            delta = jnp.sum(cot.astype(F32) * output, axis=1, keepdims=True)
            prob_grad = dot(cot, values, NT)
            score_grad = (probs * (prob_grad - delta) * SCALE).astype(BF)
            query_grad = dot(score_grad, keys)
            att_ref[slot, doc] = gather_heads(output).astype(BF)
            qg_ref[slot, doc] = gather_heads(query_grad).astype(BF)
            grad_s[core, doc * 256 : (doc + 1) * 256, 0:256] = dot(score_grad, query, TN).astype(BF)
            grad_s[core, doc * 256 : (doc + 1) * 256, 256:512] = dot(low, cot, TN).astype(BF)

    cores = [core_ref.at[k] for k in range(4)]
    for flip, outs in (
        (2, (a30.at[1], a1, a2, a30.at[0])),
        (3, (b0, b1, b2, b3)),
        (1, cores),
    ):
        partial_blocks(lax.bitwise_xor(h, flip), grad_s, w_s, part_s)
        for k in range(4):
            at = pl.ds(pl.multiple_of(ring_back(s, k) * 64, 64), 64)
            for doc in range(2):
                outs[k][doc] = part_s[doc, at, :].astype(BF)
    grad_ref[...] = grad_s[...]
    save.wait()


def main_call(lengths, arrays):
    here = pl.BlockSpec(memory_space=pl.ANY)
    vmem = pl.BlockSpec(memory_space=pltpu.VMEM)
    smem = pl.BlockSpec(memory_space=pltpu.SMEM)
    piece = jax.ShapeDtypeStruct((2, 64, 1024), BF)
    front = jax.ShapeDtypeStruct((2, 2, 64, 256), BF)
    return pl.pallas_call(
        main_kernel,
        out_shape=[
            front,
            front,
            jax.ShapeDtypeStruct((2, 512, 512), BF),
            jax.ShapeDtypeStruct((2, 4096, 512), BF),
        ]
        + [piece] * 2
        + [jax.ShapeDtypeStruct((2, 2, 64, 1024), BF)]
        + [piece] * 4
        + [jax.ShapeDtypeStruct((4, 2, 64, 1024), BF)],
        in_specs=[smem] + [here] * len(arrays),
        out_specs=[vmem] * 3 + [here] + [vmem] * 8,
        scratch_shapes=[
            pltpu.VMEM((2, 256, 4096), BF),
            pltpu.VMEM((2, 4096, 512), BF),
            pltpu.VMEM((2, 4, 64, 512), BF),
            pltpu.VMEM((2, 512, 512), BF),
            pltpu.VMEM((2, 256, 1024), F32),
            pltpu.SemaphoreType.DMA((32,)),
        ],
        compiler_params=pltpu.CompilerParams(vmem_limit_bytes=48 * 1024 * 1024),
        cost_estimate=pl.CostEstimate(
            flops=8 * 10**9, bytes_accessed=30 * 2**20, transcendentals=2**18
        ),
        name="attend",
    )(lengths, *arrays)


def near_kernel(grad, weight, own_ref, part_s):
    s, h = lax.axis_index("seq"), lax.axis_index("head")
    partial_blocks(h, grad, weight, part_s)
    for k in range(4):
        at = pl.ds(pl.multiple_of(ring_back(s, k) * 64, 64), 64)
        for doc in range(2):
            own_ref[k, doc] = part_s[doc, at, :]


def near_call(grad, weight):
    vmem = pl.BlockSpec(memory_space=pltpu.VMEM)
    return pl.pallas_call(
        near_kernel,
        out_shape=jax.ShapeDtypeStruct((4, 2, 64, 1024), F32),
        in_specs=[vmem, vmem],
        out_specs=vmem,
        scratch_shapes=[pltpu.VMEM((2, 256, 1024), F32)],
        compiler_params=pltpu.CompilerParams(vmem_limit_bytes=48 * 1024 * 1024),
        cost_estimate=pl.CostEstimate(
            flops=10**9, bytes_accessed=10 * 2**20, transcendentals=0
        ),
        name="near",
    )(grad, weight)


def final_kernel(own, core, near, far, near_sum, far_sum, out_ref):
    c = lax.rem(lax.axis_index("head"), 2)
    for i in range(2):
        mine = own[0, i] + near[1, i].astype(F32) + near_sum[i].astype(F32)
        theirs = core[0, i].astype(F32) + far[i].astype(F32) + far_sum[i].astype(F32)
        out_ref[2 * i + c] = mine.astype(BF)
        out_ref[2 * i + 1 - c] = theirs.astype(BF)


def small_call(kernel, shape, name, *arrays):
    vmem = pl.BlockSpec(memory_space=pltpu.VMEM)
    return pl.pallas_call(
        kernel,
        out_shape=jax.ShapeDtypeStruct(shape, BF),
        in_specs=[vmem] * len(arrays),
        out_specs=vmem,
        name=name,
    )(*arrays)


def after(value, *first):
    return lax.optimization_barrier((value,) + first)[0]


def body(encoder, key_weight, value_weight, tile_mask, lengths, queries, cotangent):
    h = lax.axis_index("head")
    c = lax.rem(h, 2)

    def shift(value, j):
        return lax.ppermute(value, "seq", [(a, (a + j) % SEQ) for a in range(SEQ)])

    def along(value, pairs):
        return lax.ppermute(value, "seq", pairs)

    def flip(value, bits, seqs=range(SEQ)):
        pairs = [(a * 4 + b, a * 4 + (b ^ bits)) for a in seqs for b in range(4)]
        return lax.ppermute(value, ("seq", "head"), pairs)

    def across(value):
        return lax.ppermute(value, "grp", [(0, 1), (1, 0)])

    inner, ends = (1, 2), (0, 3)
    outward = [(1, 0), (2, 3)]
    swap = [(1, 2), (2, 1)]
    e0 = lax.dynamic_index_in_dim(encoder, h, 0, keepdims=False)
    ea = along(e0, [(0, 1), (1, 0), (2, 3), (3, 2)])
    eb = along(e0, swap)
    w_own, m1, m2, m3 = prune(
        tile_mask, key_weight, value_weight, queries.reshape(64, 1024), cotangent.reshape(64, 1024)
    )
    z2 = shift(m2, 2)
    v_own = flip(after(w_own, m2), 1)
    xa = flip(ea, 2)
    ec = along(ea, swap)
    z1 = shift(after(m1, ea), 1)
    xb = flip(eb, 2, inner)
    ed = along(eb, outward)
    y2 = across(z2)
    vz2 = flip(z2, 1)
    xc = flip(ec, 2, inner)
    ef = along(ec, outward)
    z3 = shift(after(m3, ec), 3)
    xd = flip(ed, 2, ends)
    y1 = across(z1)
    vz1 = flip(z1, 1)
    vy2 = flip(y2, 1)
    xf = flip(ef, 2, ends)
    y3 = across(z3)
    vz3 = flip(z3, 1)
    vy1 = flip(y1, 1)
    vy3 = flip(y3, 1)

    outs = main_call(
        lengths,
        [encoder, ea, eb, ec, ed, ef, xa, xb, xc, xd, xf]
        + [w_own, z1, z2, z3, y1, y2, y3]
        + [v_own, vz1, vz2, vz3, vy1, vy2, vy3],
    )
    att, qgrad, grad, weight = outs[:4]
    a1, a2, a30, b1, b2, b3, b0, to_core = outs[4:]

    def onward(value):
        pairs = [(0, 1), (1, 3), (3, 2), (2, 0)]
        return along(value, pairs)

    from_core = flip(to_core, 1)
    a1, b1, a2, b2 = flip(a1, 2), flip(b1, 3), flip(a2, 2), flip(b2, 3)
    a30, b3, b0 = flip(a30, 2), flip(b3, 3), flip(b0, 3)
    own = near_call(after(grad, a1), weight)

    def summed(*parts):
        total = parts[0].astype(F32)
        for part in parts[1:]:
            total = total + part.astype(F32)
        return total.astype(BF)

    near1 = onward(summed(own[1], a1))
    far1 = onward(summed(from_core[1], b1))
    near2 = onward(summed(own[2], a2, near1))
    far2 = onward(summed(from_core[2], b2, far1))
    near3 = onward(summed(own[3], a30[0], near2))
    far3 = onward(summed(from_core[3], b3, far2))
    encoder_grad = small_call(
        final_kernel, (DOCS, 64, 1024), "final", own, from_core, a30, b0, near3, far3
    )

    front = jnp.stack([att, qgrad], axis=1)
    other = flip(front[1], 1)
    back = jnp.stack([front[0], other]).reshape(2, 2, 2, SEQ, 16, 256).transpose(3, 0, 1, 2, 4, 5)
    back = lax.all_to_all(back, "seq", split_axis=0, concat_axis=0, tiled=True)
    back = back.transpose(2, 3, 1, 4, 0, 5).reshape(2, 2, 2, 16, 1024)
    back = jnp.where(c == 0, back, back[:, :, ::-1])
    back = back.reshape(2, DOCS, 16, 1024)
    return (back[0], back[1], encoder_grad)


def solution(mesh):
    placed = (
        P("grp", "seq", None),
        P("seq", "head"),
        P("seq", "head"),
        P(None, "seq", "head"),
        P("grp"),
        P("grp", "seq", "head"),
        P("grp", "seq", "head"),
    )

    def step(*arrays):
        plan = body if fits(mesh, arrays[0], arrays[1], arrays[5]) else general_body
        return jax.shard_map(
            plan,
            mesh=mesh,
            in_specs=placed,
            out_specs=(P("grp", "seq", "head"),) * 3,
            check_vma=False,
        )(*arrays)

    return step
```

```python
import functools

import jax
import jax.numpy as jnp
from jax import lax
from jax.experimental import pallas as pl
from jax.experimental.pallas import tpu as pltpu
from jax.sharding import PartitionSpec as P

DH = 64
TILE = 64
DOCS = 4


SCALE = 0.125
FLOOR_SCORE = -1e30

BF = jnp.bfloat16
F32 = jnp.float32


def expand(tile_grid, tile_edge):
    return jnp.repeat(jnp.repeat(tile_grid, tile_edge, axis=0), tile_edge, axis=1)


def attend(keys, values, queries, cotangent, length):
    position = jnp.arange(keys.shape[0])[None, :]
    live = position < length
    scores = jnp.dot(queries, keys.T, preferred_element_type=jnp.float32) * SCALE
    scores = jnp.where(live, scores, FLOOR_SCORE)
    row_max = jnp.max(scores, axis=1, keepdims=True)
    weights = jnp.where(live, jnp.exp(scores - row_max), 0.0)
    probs = weights / jnp.sum(weights, axis=1, keepdims=True)
    probs_low = probs.astype(jnp.bfloat16)
    output = jnp.dot(probs_low, values, preferred_element_type=jnp.float32)
    delta = jnp.sum(cotangent.astype(jnp.float32) * output, axis=1, keepdims=True)
    prob_grad = jnp.dot(cotangent, values.T, preferred_element_type=jnp.float32)
    score_grad = (probs * (prob_grad - delta) * SCALE).astype(jnp.bfloat16)
    query_grad = jnp.dot(score_grad, keys, preferred_element_type=jnp.float32)
    key_grad = jnp.dot(score_grad.T, queries, preferred_element_type=jnp.float32)
    value_grad = jnp.dot(probs_low.T, cotangent, preferred_element_type=jnp.float32)
    return (
        output.astype(jnp.bfloat16),
        query_grad.astype(jnp.bfloat16),
        key_grad.astype(jnp.bfloat16),
        value_grad.astype(jnp.bfloat16),
    )


def project(encoder, key_piece, value_piece):
    count = key_piece.shape[0]
    flat = encoder.reshape(DOCS * encoder.shape[1], count)
    key_flat = jnp.dot(flat, key_piece, preferred_element_type=jnp.float32)
    value_flat = jnp.dot(flat, value_piece, preferred_element_type=jnp.float32)
    shape_out = (DOCS, encoder.shape[1], key_piece.shape[1])
    return (key_flat.reshape(shape_out), value_flat.reshape(shape_out))


def back_product(key_rows, value_rows, key_piece, value_piece):
    contract = (((1,), (1,)), ((), ()))
    total = lax.dot_general(key_rows, key_piece, contract, preferred_element_type=jnp.float32)
    return total + lax.dot_general(
        value_rows, value_piece, contract, preferred_element_type=jnp.float32
    )


def general_body(encoder, key_weight, value_weight, tile_mask, lengths, queries, cotangent):
    seq_count = lax.axis_size("seq")
    enc_rows = encoder.shape[1]
    dec_rows = queries.shape[1]
    group_heads = queries.shape[2] // DH
    pair_count = DOCS * group_heads
    local_pairs = pair_count // seq_count
    key_masked = key_weight * expand(tile_mask[0], TILE).astype(jnp.bfloat16)
    value_masked = value_weight * expand(tile_mask[1], TILE).astype(jnp.bfloat16)
    full_key, full_value = (
        lax.all_gather(key_masked, "seq", axis=0, tiled=True),
        lax.all_gather(value_masked, "seq", axis=0, tiled=True),
    )
    key_sum, value_sum = project(encoder, full_key, full_value)

    def to_pairs(first, second, rows):
        joined = jnp.concatenate(
            [
                first.reshape(DOCS, rows, group_heads, DH),
                second.reshape(DOCS, rows, group_heads, DH),
            ],
            axis=3,
        )
        return joined.transpose(0, 2, 1, 3).reshape(pair_count, rows, 2 * DH)

    def from_pairs(block, rows):
        shaped = block.reshape(DOCS, group_heads, rows, 2 * DH).transpose(0, 2, 1, 3)
        first = shaped[..., :DH].reshape(DOCS, rows, group_heads * DH)
        second = shaped[..., DH:].reshape(DOCS, rows, group_heads * DH)
        return (first, second)

    query_pairs = to_pairs(queries, cotangent, dec_rows)
    query_owned = lax.all_to_all(query_pairs, "seq", split_axis=0, concat_axis=1, tiled=True)
    kv_pairs = to_pairs(key_sum.astype(jnp.bfloat16), value_sum.astype(jnp.bfloat16), enc_rows)
    kv_owned = lax.all_to_all(kv_pairs, "seq", split_axis=0, concat_axis=1, tiled=True)
    pair_ids = lax.axis_index("seq") * local_pairs + jnp.arange(local_pairs)
    doc_of_pair = pair_ids // group_heads
    pair_length = jnp.sum(
        jnp.where(doc_of_pair[:, None] == jnp.arange(DOCS)[None, :], lengths[None, :], 0), axis=1
    )

    def owner_pair(items):
        pair_kv, pair_query, length = items
        output, query_grad, key_grad, value_grad = attend(
            pair_kv[:, :DH], pair_kv[:, DH:], pair_query[:, :DH], pair_query[:, DH:], length
        )
        return (
            jnp.concatenate([output, query_grad], axis=1),
            jnp.concatenate([key_grad, value_grad], axis=1),
        )

    front, back = lax.map(owner_pair, (kv_owned, query_owned, pair_length))
    front_rows, back_rows = (
        lax.all_to_all(front, "seq", split_axis=1, concat_axis=0, tiled=True),
        lax.all_to_all(back, "seq", split_axis=1, concat_axis=0, tiled=True),
    )
    attention, query_grad = from_pairs(front_rows, dec_rows)
    key_grads, value_grads = from_pairs(back_rows, enc_rows)
    key_rows = key_grads.reshape(DOCS * enc_rows, group_heads * DH)
    value_rows = value_grads.reshape(DOCS * enc_rows, group_heads * DH)
    grad_terms = back_product(key_rows, value_rows, full_key, full_value)
    grad_share = lax.psum_scatter(grad_terms, "head", scatter_dimension=1, tiled=True)
    encoder_grad = grad_share.astype(jnp.bfloat16).reshape(DOCS, enc_rows, grad_share.shape[1])
    return (attention, query_grad, encoder_grad)


SEQ = 4
PIECE = 512
SENT = PIECE + 64


def fits(mesh, encoder, key_weight, queries):
    return (
        mesh.shape["seq"] == SEQ
        and mesh.shape["head"] == 4
        and mesh.shape["grp"] == 2
        and encoder.shape == (DOCS * 2, 256, 4096)
        and key_weight.shape == (4096, 4096)
        and queries.shape == (DOCS * 2, 64, 4096)
    )


def prune_kernel(mask_ref, key_ref, value_ref, query_ref, cot_ref, own_ref, *message_refs):
    s, g = lax.axis_index("seq"), lax.axis_index("grp")
    left = lax.broadcasted_iota(jnp.int32, (1, 128), 1) < TILE

    def write(out_ref, first_tile, tiles, column):
        for t in range(tiles):
            tile = first_tile + t
            row = pl.ds(pl.multiple_of(tile * TILE, TILE), TILE)
            for side, ref in ((0, key_ref), (1, value_ref)):
                for part in range(2):
                    at = pl.ds(pl.multiple_of(column * 256 + part * 128, 128), 128)
                    first = mask_ref[side, tile, column * 4 + part * 2]
                    second = mask_ref[side, tile, column * 4 + part * 2 + 1]
                    keep = jnp.where(left, first, second).astype(F32)
                    to = side * 256 + part * 128
                    out_ref[t * TILE : (t + 1) * TILE, to : to + 128] = (
                        ref[row, at].astype(F32) * keep
                    ).astype(BF)
        at = pl.ds(pl.multiple_of(column * 256, 256), 256)
        out_ref[tiles * TILE :, 0:256] = query_ref[:, at]
        out_ref[tiles * TILE :, 256:512] = cot_ref[:, at]

    for k in (2, 3, 1):
        write(message_refs[k - 1], g * 8, 8, lax.bitwise_xor(s, k))
    write(own_ref, 0, 16, s)


def prune(tile_mask, key_weight, value_weight, queries, cotangent):
    whole = pl.BlockSpec(memory_space=pltpu.VMEM)
    return pl.pallas_call(
        prune_kernel,
        out_shape=[jax.ShapeDtypeStruct((2 * PIECE + 64, 512), BF)]
        + [jax.ShapeDtypeStruct((SENT, 512), BF)] * 3,
        in_specs=[pl.BlockSpec(memory_space=pltpu.SMEM)] + [whole] * 4,
        out_specs=[whole] * 4,
        name="prune",
    )(tile_mask, key_weight, value_weight, queries, cotangent)


NT = (((1,), (1,)), ((), ()))
TN = (((0,), (0,)), ((), ()))
NN = (((1,), (0,)), ((), ()))


def dot(a, b, dims=NN):
    return lax.dot_general(a, b, dims, preferred_element_type=F32)


def partial_blocks(block, grad, weight, part):
    def column(n, carry):
        at = pl.ds(pl.multiple_of(block * 1024 + n * 256, 256), 256)
        total = dot(grad[0], weight[0, at, :], NT) + dot(grad[1], weight[1, at, :], NT)
        part[:, :, pl.ds(pl.multiple_of(n * 256, 256), 256)] = total.reshape(2, 256, 256)
        return carry

    lax.fori_loop(0, 4, column, 0)


def main_kernel(lengths, *refs):
    (
        enc, e1, e2, e3, x1, x2, x3,
        w_own, z1, z2, z3, y1, y2, y3,
        v_own, vz1, vz2, vz3, vy1, vy2, vy3,
        att_ref, qg_ref, grad_ref, weight_ref,
        a3, b3, a2, b2, b1, a10, b0, core_ref,
        enc_s, w_s, qc_s, grad_s, part_s, sems,
    ) = refs
    s, g, h = lax.axis_index("seq"), lax.axis_index("grp"), lax.axis_index("head")
    c = lax.rem(h, 2)
    x = h // 2
    copies = []

    def move(src, dst):
        copy = pltpu.make_async_copy(src, dst, sems.at[len(copies)])
        copy.start()
        copies.append(copy)

    def rows_of(doc, at):
        return enc_s.at[doc, pl.ds(pl.multiple_of(at * 64, 64), 64)]

    for i in range(2):
        move(enc.at[2 * i + c], rows_of(i, s))
    for k, (mine, other) in enumerate(((e1, x1), (e2, x2), (e3, x3))):
        at = lax.bitwise_xor(s, k + 1)
        move(mine, rows_of(x, at))
        move(other, rows_of(1 - x, at))

    def weight_rows(core, at, half, count):
        return w_s.at[core, pl.ds(pl.multiple_of(at * 1024 + half * PIECE, PIECE), count)]

    for core, own, zs, ys in (
        (c, w_own, (z1, z2, z3), (y1, y2, y3)),
        (1 - c, v_own, (vz1, vz2, vz3), (vy1, vy2, vy3)),
    ):
        move(own.at[0 : 2 * PIECE], weight_rows(core, s, 0, 2 * PIECE))
        move(own.at[2 * PIECE : 2 * PIECE + 64], qc_s.at[core, s])
        for j in range(3):
            at = lax.bitwise_xor(s, j + 1)
            move(zs[j].at[0:PIECE], weight_rows(core, at, g, PIECE))
            move(ys[j].at[0:PIECE], weight_rows(core, at, 1 - g, PIECE))
            move(zs[j].at[PIECE:SENT], qc_s.at[core, at])
    for copy in copies:
        copy.wait()
    save = pltpu.make_async_copy(w_s, weight_ref, sems.at[0])
    save.start()

    row_head = lax.broadcasted_iota(jnp.int32, (256, 256), 0) // DH
    col_head = lax.broadcasted_iota(jnp.int32, (256, 256), 1) // DH
    same = row_head == col_head
    position = lax.broadcasted_iota(jnp.int32, (256, 256), 1)

    def spread(block):
        four = jnp.concatenate([block] * 4, axis=0)
        return jnp.where(same, four, jnp.zeros_like(four))

    def gather_heads(block):
        kept = jnp.where(same, block, 0.0)
        return (kept[0:64] + kept[64:128]) + (kept[128:192] + kept[192:256])

    for core in range(2):
        slot = lax.rem(core + c, 2)
        for doc in range(2):
            both = dot(enc_s[doc], w_s[core])
            keys = both[:, :256].astype(BF)
            values = both[:, 256:].astype(BF)
            at = pl.ds(pl.multiple_of((2 * doc + c) * 16, 16), 16)
            query = spread(qc_s[core, :, at, 0:256].reshape(64, 256))
            cot = spread(qc_s[core, :, at, 256:512].reshape(64, 256))
            live = position < lengths[2 * doc + c]
            scores = dot(query, keys, NT) * SCALE
            scores = jnp.where(live, scores, FLOOR_SCORE)
            row_max = jnp.max(scores, axis=1, keepdims=True)
            weights = jnp.where(live, jnp.exp(scores - row_max), 0.0)
            probs = weights / jnp.sum(weights, axis=1, keepdims=True)
            low = probs.astype(BF)
            output = dot(low, values)
            delta = jnp.sum(cot.astype(F32) * output, axis=1, keepdims=True)
            prob_grad = dot(cot, values, NT)
            score_grad = (probs * (prob_grad - delta) * SCALE).astype(BF)
            query_grad = dot(score_grad, keys)
            att_ref[slot, doc] = gather_heads(output).astype(BF)
            qg_ref[slot, doc] = gather_heads(query_grad).astype(BF)
            grad_s[core, doc * 256 : (doc + 1) * 256, 0:256] = dot(score_grad, query, TN).astype(BF)
            grad_s[core, doc * 256 : (doc + 1) * 256, 256:512] = dot(low, cot, TN).astype(BF)

    cores = [core_ref.at[k] for k in range(4)]
    for flip, outs in (
        (2, (a10.at[1], a10.at[0], a2, a3)),
        (3, (b0, b1, b2, b3)),
        (1, cores),
    ):
        partial_blocks(lax.bitwise_xor(h, flip), grad_s, w_s, part_s)
        for k in range(4):
            at = pl.ds(pl.multiple_of(lax.bitwise_xor(s, k) * 64, 64), 64)
            for doc in range(2):
                outs[k][doc] = part_s[doc, at, :].astype(BF)
    grad_ref[...] = grad_s[...]
    save.wait()


def main_call(lengths, arrays):
    here = pl.BlockSpec(memory_space=pl.ANY)
    vmem = pl.BlockSpec(memory_space=pltpu.VMEM)
    smem = pl.BlockSpec(memory_space=pltpu.SMEM)
    piece = jax.ShapeDtypeStruct((2, 64, 1024), BF)
    front = jax.ShapeDtypeStruct((2, 2, 64, 256), BF)
    return pl.pallas_call(
        main_kernel,
        out_shape=[
            front,
            front,
            jax.ShapeDtypeStruct((2, 512, 512), BF),
            jax.ShapeDtypeStruct((2, 4096, 512), BF),
        ]
        + [piece] * 5
        + [jax.ShapeDtypeStruct((2, 2, 64, 1024), BF)]
        + [piece]
        + [jax.ShapeDtypeStruct((4, 2, 64, 1024), BF)],
        in_specs=[smem] + [here] * len(arrays),
        out_specs=[vmem] * 3 + [here] + [vmem] * 8,
        scratch_shapes=[
            pltpu.VMEM((2, 256, 4096), BF),
            pltpu.VMEM((2, 4096, 512), BF),
            pltpu.VMEM((2, 4, 64, 512), BF),
            pltpu.VMEM((2, 512, 512), BF),
            pltpu.VMEM((2, 256, 1024), F32),
            pltpu.SemaphoreType.DMA((32,)),
        ],
        compiler_params=pltpu.CompilerParams(vmem_limit_bytes=48 * 1024 * 1024),
        cost_estimate=pl.CostEstimate(
            flops=8 * 10**9, bytes_accessed=30 * 2**20, transcendentals=2**18
        ),
        name="attend",
    )(lengths, *arrays)


def near_kernel(grad, weight, own_ref, part_s):
    s, h = lax.axis_index("seq"), lax.axis_index("head")
    partial_blocks(h, grad, weight, part_s)
    for k in range(4):
        at = pl.ds(pl.multiple_of(lax.bitwise_xor(s, k) * 64, 64), 64)
        for doc in range(2):
            own_ref[k, doc] = part_s[doc, at, :]


def near_call(grad, weight):
    vmem = pl.BlockSpec(memory_space=pltpu.VMEM)
    return pl.pallas_call(
        near_kernel,
        out_shape=jax.ShapeDtypeStruct((4, 2, 64, 1024), F32),
        in_specs=[vmem, vmem],
        out_specs=vmem,
        scratch_shapes=[pltpu.VMEM((2, 256, 1024), F32)],
        compiler_params=pltpu.CompilerParams(vmem_limit_bytes=48 * 1024 * 1024),
        cost_estimate=pl.CostEstimate(
            flops=10**9, bytes_accessed=10 * 2**20, transcendentals=0
        ),
        name="near",
    )(grad, weight)


def final_kernel(own, core, near, far, near1, near2, far1, far2, out_ref):
    c = lax.rem(lax.axis_index("head"), 2)
    for i in range(2):
        mine = (own[0, i] + near[1, i].astype(F32)) + (near1[i].astype(F32) + near2[i].astype(F32))
        theirs = (core[0, i].astype(F32) + far[i].astype(F32)) + (
            far1[i].astype(F32) + far2[i].astype(F32)
        )
        out_ref[2 * i + c] = mine.astype(BF)
        out_ref[2 * i + 1 - c] = theirs.astype(BF)


def small_call(kernel, shape, name, *arrays):
    vmem = pl.BlockSpec(memory_space=pltpu.VMEM)
    return pl.pallas_call(
        kernel,
        out_shape=jax.ShapeDtypeStruct(shape, BF),
        in_specs=[vmem] * len(arrays),
        out_specs=vmem,
        name=name,
    )(*arrays)


def after(value, *first):
    return lax.optimization_barrier((value,) + first)[0]


def body(encoder, key_weight, value_weight, tile_mask, lengths, queries, cotangent):
    h = lax.axis_index("head")
    c = lax.rem(h, 2)

    def along(value, k):
        return lax.ppermute(value, "seq", [(a, a ^ k) for a in range(SEQ)])

    def flip(value, bits):
        return lax.ppermute(value, "head", [(a, a ^ bits) for a in range(4)])

    def across(value):
        return lax.ppermute(value, "grp", [(0, 1), (1, 0)])

    e0 = lax.dynamic_index_in_dim(encoder, h, 0, keepdims=False)
    e2 = along(e0, 2)
    e1 = along(e0, 1)
    w_own, m1, m2, m3 = prune(
        tile_mask, key_weight, value_weight, queries.reshape(64, 1024), cotangent.reshape(64, 1024)
    )
    z2 = along(m2, 2)
    e3 = along(e2, 1)
    z3 = along(after(m3, e1), 3)
    z1 = along(after(m1, e2), 1)
    x1, x2, x3 = flip(e1, 2), flip(e2, 2), flip(e3, 2)
    y1, y2, y3 = across(z1), across(z2), across(z3)
    v_own = flip(after(w_own, e1), 1)
    vz1, vz2, vz3 = flip(z1, 1), flip(z2, 1), flip(z3, 1)
    vy1, vy2, vy3 = flip(y1, 1), flip(y2, 1), flip(y3, 1)

    outs = main_call(
        lengths,
        [encoder, e1, e2, e3, x1, x2, x3]
        + [w_own, z1, z2, z3, y1, y2, y3]
        + [v_own, vz1, vz2, vz3, vy1, vy2, vy3],
    )
    att, qgrad, grad, weight = outs[:4]
    a3, b3, a2, b2, b1, a10, b0, to_core = outs[4:]
    from_core = flip(to_core, 1)
    a3, b3 = flip(a3, 2), flip(b3, 3)
    a2, b2 = flip(after(a2, a3), 2), flip(after(b2, a3), 3)
    b1, a10 = flip(after(b1, a2), 3), flip(after(a10, a2), 2)
    b0 = flip(b0, 3)
    own = near_call(after(grad, a3), weight)

    def summed(*parts):
        total = parts[0].astype(F32)
        for part in parts[1:]:
            total = total + part.astype(F32)
        return total.astype(BF)

    near3 = along(summed(own[3], a3), 1)
    far3 = along(summed(from_core[3], b3), 1)
    near2 = along(summed(own[2], a2, near3), 2)
    far2 = summed(from_core[2], b2, far3)
    far1 = along(summed(from_core[1], after(b1, far2)), 1)
    far2 = along(far2, 2)
    near1 = along(summed(own[1], a10[0]), 1)
    encoder_grad = small_call(
        final_kernel, (DOCS, 64, 1024), "final", own, from_core, a10, b0, near1, near2, far1, far2
    )

    front = jnp.stack([att, qgrad], axis=1)
    other = flip(front[1], 1)
    back = jnp.stack([front[0], other]).reshape(2, 2, 2, SEQ, 16, 256).transpose(3, 0, 1, 2, 4, 5)
    back = lax.all_to_all(back, "seq", split_axis=0, concat_axis=0, tiled=True)
    back = back.transpose(2, 3, 1, 4, 0, 5).reshape(2, 2, 2, 16, 1024)
    back = jnp.where(c == 0, back, back[:, :, ::-1])
    back = back.reshape(2, DOCS, 16, 1024)
    return (back[0], back[1], encoder_grad)


def solution(mesh):
    placed = (
        P("grp", "seq", None),
        P("seq", "head"),
        P("seq", "head"),
        P(None, "seq", "head"),
        P("grp"),
        P("grp", "seq", "head"),
        P("grp", "seq", "head"),
    )

    def step(*arrays):
        plan = body if fits(mesh, arrays[0], arrays[1], arrays[5]) else general_body
        return jax.shard_map(
            plan,
            mesh=mesh,
            in_specs=placed,
            out_specs=(P("grp", "seq", "head"),) * 3,
            check_vma=False,
        )(*arrays)

    return step
```

```python
import functools

import jax
import jax.numpy as jnp
from jax import lax
from jax.experimental import pallas as pl
from jax.experimental.pallas import tpu as pltpu
from jax.sharding import PartitionSpec as P

DH = 64
TILE = 64
DOCS = 4


SCALE = 0.125
FLOOR_SCORE = -1e30

BF = jnp.bfloat16
F32 = jnp.float32


def expand(tile_grid, tile_edge):
    return jnp.repeat(jnp.repeat(tile_grid, tile_edge, axis=0), tile_edge, axis=1)


def attend(keys, values, queries, cotangent, length):
    position = jnp.arange(keys.shape[0])[None, :]
    live = position < length
    scores = jnp.dot(queries, keys.T, preferred_element_type=jnp.float32) * SCALE
    scores = jnp.where(live, scores, FLOOR_SCORE)
    row_max = jnp.max(scores, axis=1, keepdims=True)
    weights = jnp.where(live, jnp.exp(scores - row_max), 0.0)
    probs = weights / jnp.sum(weights, axis=1, keepdims=True)
    probs_low = probs.astype(jnp.bfloat16)
    output = jnp.dot(probs_low, values, preferred_element_type=jnp.float32)
    delta = jnp.sum(cotangent.astype(jnp.float32) * output, axis=1, keepdims=True)
    prob_grad = jnp.dot(cotangent, values.T, preferred_element_type=jnp.float32)
    score_grad = (probs * (prob_grad - delta) * SCALE).astype(jnp.bfloat16)
    query_grad = jnp.dot(score_grad, keys, preferred_element_type=jnp.float32)
    key_grad = jnp.dot(score_grad.T, queries, preferred_element_type=jnp.float32)
    value_grad = jnp.dot(probs_low.T, cotangent, preferred_element_type=jnp.float32)
    return (
        output.astype(jnp.bfloat16),
        query_grad.astype(jnp.bfloat16),
        key_grad.astype(jnp.bfloat16),
        value_grad.astype(jnp.bfloat16),
    )


def project(encoder, key_piece, value_piece):
    count = key_piece.shape[0]
    flat = encoder.reshape(DOCS * encoder.shape[1], count)
    key_flat = jnp.dot(flat, key_piece, preferred_element_type=jnp.float32)
    value_flat = jnp.dot(flat, value_piece, preferred_element_type=jnp.float32)
    shape_out = (DOCS, encoder.shape[1], key_piece.shape[1])
    return (key_flat.reshape(shape_out), value_flat.reshape(shape_out))


def back_product(key_rows, value_rows, key_piece, value_piece):
    contract = (((1,), (1,)), ((), ()))
    total = lax.dot_general(key_rows, key_piece, contract, preferred_element_type=jnp.float32)
    return total + lax.dot_general(
        value_rows, value_piece, contract, preferred_element_type=jnp.float32
    )


def general_body(encoder, key_weight, value_weight, tile_mask, lengths, queries, cotangent):
    seq_count = lax.axis_size("seq")
    enc_rows = encoder.shape[1]
    dec_rows = queries.shape[1]
    group_heads = queries.shape[2] // DH
    pair_count = DOCS * group_heads
    local_pairs = pair_count // seq_count
    key_masked = key_weight * expand(tile_mask[0], TILE).astype(jnp.bfloat16)
    value_masked = value_weight * expand(tile_mask[1], TILE).astype(jnp.bfloat16)
    full_key, full_value = (
        lax.all_gather(key_masked, "seq", axis=0, tiled=True),
        lax.all_gather(value_masked, "seq", axis=0, tiled=True),
    )
    key_sum, value_sum = project(encoder, full_key, full_value)

    def to_pairs(first, second, rows):
        joined = jnp.concatenate(
            [
                first.reshape(DOCS, rows, group_heads, DH),
                second.reshape(DOCS, rows, group_heads, DH),
            ],
            axis=3,
        )
        return joined.transpose(0, 2, 1, 3).reshape(pair_count, rows, 2 * DH)

    def from_pairs(block, rows):
        shaped = block.reshape(DOCS, group_heads, rows, 2 * DH).transpose(0, 2, 1, 3)
        first = shaped[..., :DH].reshape(DOCS, rows, group_heads * DH)
        second = shaped[..., DH:].reshape(DOCS, rows, group_heads * DH)
        return (first, second)

    query_pairs = to_pairs(queries, cotangent, dec_rows)
    query_owned = lax.all_to_all(query_pairs, "seq", split_axis=0, concat_axis=1, tiled=True)
    kv_pairs = to_pairs(key_sum.astype(jnp.bfloat16), value_sum.astype(jnp.bfloat16), enc_rows)
    kv_owned = lax.all_to_all(kv_pairs, "seq", split_axis=0, concat_axis=1, tiled=True)
    pair_ids = lax.axis_index("seq") * local_pairs + jnp.arange(local_pairs)
    doc_of_pair = pair_ids // group_heads
    pair_length = jnp.sum(
        jnp.where(doc_of_pair[:, None] == jnp.arange(DOCS)[None, :], lengths[None, :], 0), axis=1
    )

    def owner_pair(items):
        pair_kv, pair_query, length = items
        output, query_grad, key_grad, value_grad = attend(
            pair_kv[:, :DH], pair_kv[:, DH:], pair_query[:, :DH], pair_query[:, DH:], length
        )
        return (
            jnp.concatenate([output, query_grad], axis=1),
            jnp.concatenate([key_grad, value_grad], axis=1),
        )

    front, back = lax.map(owner_pair, (kv_owned, query_owned, pair_length))
    front_rows, back_rows = (
        lax.all_to_all(front, "seq", split_axis=1, concat_axis=0, tiled=True),
        lax.all_to_all(back, "seq", split_axis=1, concat_axis=0, tiled=True),
    )
    attention, query_grad = from_pairs(front_rows, dec_rows)
    key_grads, value_grads = from_pairs(back_rows, enc_rows)
    key_rows = key_grads.reshape(DOCS * enc_rows, group_heads * DH)
    value_rows = value_grads.reshape(DOCS * enc_rows, group_heads * DH)
    grad_terms = back_product(key_rows, value_rows, full_key, full_value)
    grad_share = lax.psum_scatter(grad_terms, "head", scatter_dimension=1, tiled=True)
    encoder_grad = grad_share.astype(jnp.bfloat16).reshape(DOCS, enc_rows, grad_share.shape[1])
    return (attention, query_grad, encoder_grad)


SEQ = 4
PIECE = 512
SENT = PIECE + 64


def fits(mesh, encoder, key_weight, queries):
    return (
        mesh.shape["seq"] == SEQ
        and mesh.shape["head"] == 4
        and mesh.shape["grp"] == 2
        and encoder.shape == (DOCS * 2, 256, 4096)
        and key_weight.shape == (4096, 4096)
        and queries.shape == (DOCS * 2, 64, 4096)
    )


def prune_kernel(mask_ref, key_ref, value_ref, query_ref, cot_ref, own_ref, *message_refs):
    s, g = lax.axis_index("seq"), lax.axis_index("grp")
    left = lax.broadcasted_iota(jnp.int32, (1, 128), 1) < TILE

    def write(out_ref, first_tile, tiles, column):
        for t in range(tiles):
            tile = first_tile + t
            row = pl.ds(pl.multiple_of(tile * TILE, TILE), TILE)
            for side, ref in ((0, key_ref), (1, value_ref)):
                for part in range(2):
                    at = pl.ds(pl.multiple_of(column * 256 + part * 128, 128), 128)
                    first = mask_ref[side, tile, column * 4 + part * 2]
                    second = mask_ref[side, tile, column * 4 + part * 2 + 1]
                    keep = jnp.where(left, first, second).astype(F32)
                    to = side * 256 + part * 128
                    out_ref[t * TILE : (t + 1) * TILE, to : to + 128] = (
                        ref[row, at].astype(F32) * keep
                    ).astype(BF)
        at = pl.ds(pl.multiple_of(column * 256, 256), 256)
        out_ref[tiles * TILE :, 0:256] = query_ref[:, at]
        out_ref[tiles * TILE :, 256:512] = cot_ref[:, at]

    first, second, third = message_refs
    write(second, g * 8, 8, lax.bitwise_xor(s, 2))
    write(first, g * 8, 8, lax.bitwise_xor(s, 1))
    write(third, g * 8, 8, lax.bitwise_xor(s, 3))
    write(own_ref, 0, 16, s)


def prune(tile_mask, key_weight, value_weight, queries, cotangent):
    whole = pl.BlockSpec(memory_space=pltpu.VMEM)
    rows = (2 * PIECE + 64, SENT, SENT, SENT)
    return pl.pallas_call(
        prune_kernel,
        out_shape=[jax.ShapeDtypeStruct((count, 512), BF) for count in rows],
        in_specs=[pl.BlockSpec(memory_space=pltpu.SMEM)] + [whole] * 4,
        out_specs=[whole] * len(rows),
        name="prune",
    )(tile_mask, key_weight, value_weight, queries, cotangent)


NT = (((1,), (1,)), ((), ()))
TN = (((0,), (0,)), ((), ()))
NN = (((1,), (0,)), ((), ()))


def dot(a, b, dims=NN):
    return lax.dot_general(a, b, dims, preferred_element_type=F32)


def partial_blocks(block, grad, weight, part):
    def column(n, carry):
        at = pl.ds(pl.multiple_of(block * 1024 + n * 256, 256), 256)
        total = dot(grad[0], weight[0, at, :], NT) + dot(grad[1], weight[1, at, :], NT)
        part[:, :, pl.ds(pl.multiple_of(n * 256, 256), 256)] = total.reshape(2, 256, 256)
        return carry

    lax.fori_loop(0, 4, column, 0)


class Mover:
    def __init__(self, sems):
        self.sems = sems
        self.used = 0

    def start(self, pairs):
        copies = []
        for src, dst in pairs:
            copy = pltpu.make_async_copy(src, dst, self.sems.at[self.used])
            copy.start()
            self.used += 1
            copies.append(copy)
        return copies


def piece_rows(w_s, core, at, first, count):
    return w_s.at[core, pl.ds(pl.multiple_of(at * 1024 + first, 256), count)]


PACKED = 3 * 2 * PIECE


def pack_kernel(own, z1, z2, y1, y2, out_ref, sems):
    g = lax.axis_index("grp")
    pairs = [(own.at[0 : 2 * PIECE], out_ref.at[0 : 2 * PIECE])]
    pairs.append((own.at[2 * PIECE : 2 * PIECE + 64], out_ref.at[PACKED : PACKED + 64]))
    for k, z, y in ((1, z1, y1), (2, z2, y2)):
        for piece, side in ((z, g), (y, 1 - g)):
            first = pl.multiple_of(2 * PIECE * k + side * PIECE, PIECE)
            pairs.append((piece.at[0:PIECE], out_ref.at[pl.ds(first, PIECE)]))
        pairs.append((z.at[PIECE:SENT], out_ref.at[PACKED + 64 * k : PACKED + 64 * k + 64]))
    for copy in Mover(sems).start(pairs):
        copy.wait()


def pack_call(*arrays):
    here = pl.BlockSpec(memory_space=pl.ANY)
    return pl.pallas_call(
        pack_kernel,
        out_shape=jax.ShapeDtypeStruct((PACKED + 192, 512), BF),
        in_specs=[here] * len(arrays),
        out_specs=here,
        scratch_shapes=[pltpu.SemaphoreType.DMA((8,))],
        cost_estimate=pl.CostEstimate(flops=1, bytes_accessed=1, transcendentals=0),
        name="pack",
    )(*arrays)


def early_weights(w_s, c, s, mine, theirs):
    pairs = []
    for core, packed in ((c, mine), (1 - c, theirs)):
        for k in range(3):
            rows = packed.at[2 * PIECE * k : 2 * PIECE * (k + 1)]
            pairs.append((rows, piece_rows(w_s, core, lax.bitwise_xor(s, k), 0, 2 * PIECE)))
    return pairs


def early_kernel(*refs):
    enc, e1, e2, e3, x1, x2, x3 = refs[:7]
    mine, theirs = refs[7:9]
    sum_ref, last_ref, enc_s, w_s, sems = refs[9:]
    s, h = lax.axis_index("seq"), lax.axis_index("head")
    c = lax.rem(h, 2)
    x = h // 2
    mover = Mover(sems)

    def rows_of(doc, at):
        return enc_s.at[pl.ds(pl.multiple_of(doc * 256 + at * 64, 64), 64)]

    pairs = [(enc.at[2 * i + c], rows_of(i, s)) for i in range(2)]
    for k, (own, other) in enumerate(((e1, x1), (e2, x2), (e3, x3))):
        at = lax.bitwise_xor(s, k + 1)
        pairs += [(own, rows_of(x, at)), (other, rows_of(1 - x, at))]
    pairs += early_weights(w_s, c, s, mine, theirs)
    for copy in mover.start(pairs):
        copy.wait()

    def columns(k):
        at = lax.bitwise_xor(s, k)
        return pl.ds(pl.multiple_of(at * 1024, 1024), 1024)

    for core in range(2):
        for half in range(2):
            row = slice(half * 256, half * 256 + 256)
            total = dot(enc_s[row, columns(0)], w_s[core, columns(0), :])
            for k in (1, 2):
                total = total + dot(enc_s[row, columns(k)], w_s[core, columns(k), :])
            sum_ref[core, row] = total
    last_ref[...] = enc_s[:, columns(3)]


def early_call(arrays):
    here = pl.BlockSpec(memory_space=pl.ANY)
    vmem = pl.BlockSpec(memory_space=pltpu.VMEM)
    return pl.pallas_call(
        early_kernel,
        out_shape=[
            jax.ShapeDtypeStruct((2, 512, 512), F32),
            jax.ShapeDtypeStruct((512, 1024), BF),
        ],
        in_specs=[here] * len(arrays),
        out_specs=[vmem] * 2,
        scratch_shapes=[
            pltpu.VMEM((512, 4096), BF),
            pltpu.VMEM((2, 4096, 512), BF),
            pltpu.SemaphoreType.DMA((18,)),
        ],
        compiler_params=pltpu.CompilerParams(vmem_limit_bytes=28 * 1024 * 1024),
        cost_estimate=pl.CostEstimate(
            flops=1, bytes_accessed=1, transcendentals=0
        ),
        name="early",
    )(*arrays)


def main_kernel(lengths, *refs):
    early_sum, last_rows = refs[:2]
    mine, theirs = refs[2:5], refs[5:8]
    (
        att_ref, qg_ref, own_ref,
        a3, b3, a2, b2, b1, a10, b0, core_ref,
        w_s, qc_s, grad_s, part_s, sems,
    ) = refs[8:]
    s, g, h = lax.axis_index("seq"), lax.axis_index("grp"), lax.axis_index("head")
    c = lax.rem(h, 2)
    mover = Mover(sems)
    far = lax.bitwise_xor(s, 3)
    pairs = []
    for core, pieces in ((c, mine), (1 - c, theirs)):
        packed, z3, y3 = pieces
        for src, side in ((z3, g), (y3, 1 - g)):
            pairs.append((src.at[0:PIECE], piece_rows(w_s, core, far, side * PIECE, PIECE)))
        for k in range(3):
            rows = packed.at[PACKED + 64 * k : PACKED + 64 * k + 64]
            pairs.append((rows, qc_s.at[core, lax.bitwise_xor(s, k)]))
        pairs.append((z3.at[PIECE:SENT], qc_s.at[core, far]))
    now = mover.start(pairs)
    later = mover.start(early_weights(w_s, c, s, mine[0], theirs[0]))
    for copy in now:
        copy.wait()
    far_rows = pl.ds(pl.multiple_of(far * 1024, 1024), 1024)

    row_head = lax.broadcasted_iota(jnp.int32, (256, 256), 0) // DH
    col_head = lax.broadcasted_iota(jnp.int32, (256, 256), 1) // DH
    same = row_head == col_head
    position = lax.broadcasted_iota(jnp.int32, (256, 256), 1)

    def spread(block):
        four = jnp.concatenate([block] * 4, axis=0)
        return jnp.where(same, four, jnp.zeros_like(four))

    def gather_heads(block):
        kept = jnp.where(same, block, 0.0)
        return (kept[0:64] + kept[64:128]) + (kept[128:192] + kept[192:256])

    for core in range(2):
        slot = lax.rem(core + c, 2)
        for doc in range(2):
            row = slice(doc * 256, doc * 256 + 256)
            both = early_sum[core, row] + dot(last_rows[row], w_s[core, far_rows, :])
            keys = both[:, :256].astype(BF)
            values = both[:, 256:].astype(BF)
            at = pl.ds(pl.multiple_of((2 * doc + c) * 16, 16), 16)
            query = spread(qc_s[core, :, at, 0:256].reshape(64, 256))
            cot = spread(qc_s[core, :, at, 256:512].reshape(64, 256))
            live = position < lengths[2 * doc + c]
            scores = dot(query, keys, NT) * SCALE
            scores = jnp.where(live, scores, FLOOR_SCORE)
            row_max = jnp.max(scores, axis=1, keepdims=True)
            weights = jnp.where(live, jnp.exp(scores - row_max), 0.0)
            probs = weights / jnp.sum(weights, axis=1, keepdims=True)
            low = probs.astype(BF)
            output = dot(low, values)
            delta = jnp.sum(cot.astype(F32) * output, axis=1, keepdims=True)
            prob_grad = dot(cot, values, NT)
            score_grad = (probs * (prob_grad - delta) * SCALE).astype(BF)
            query_grad = dot(score_grad, keys)
            att_ref[slot, doc] = gather_heads(output).astype(BF)
            qg_ref[slot, doc] = gather_heads(query_grad).astype(BF)
            grad_s[core, doc * 256 : (doc + 1) * 256, 0:256] = dot(score_grad, query, TN).astype(BF)
            grad_s[core, doc * 256 : (doc + 1) * 256, 256:512] = dot(low, cot, TN).astype(BF)

    for copy in later:
        copy.wait()
    cores = [core_ref.at[k] for k in range(4)]
    owns = [own_ref.at[k] for k in range(4)]
    for flip, outs in (
        (2, (a10.at[1], a10.at[0], a2, a3)),
        (3, (b0, b1, b2, b3)),
        (1, cores),
        (0, owns),
    ):
        partial_blocks(lax.bitwise_xor(h, flip), grad_s, w_s, part_s)
        for k in range(4):
            at = pl.ds(pl.multiple_of(lax.bitwise_xor(s, k) * 64, 64), 64)
            for doc in range(2):
                outs[k][doc] = part_s[doc, at, :].astype(outs[k].dtype)


def main_call(lengths, arrays):
    here = pl.BlockSpec(memory_space=pl.ANY)
    vmem = pl.BlockSpec(memory_space=pltpu.VMEM)
    smem = pl.BlockSpec(memory_space=pltpu.SMEM)
    piece = jax.ShapeDtypeStruct((2, 64, 1024), BF)
    front = jax.ShapeDtypeStruct((2, 2, 64, 256), BF)
    return pl.pallas_call(
        main_kernel,
        out_shape=[
            front,
            front,
            jax.ShapeDtypeStruct((4, 2, 64, 1024), F32),
        ]
        + [piece] * 5
        + [jax.ShapeDtypeStruct((2, 2, 64, 1024), BF)]
        + [piece]
        + [jax.ShapeDtypeStruct((4, 2, 64, 1024), BF)],
        in_specs=[smem] + [vmem] * 2 + [here] * (len(arrays) - 2),
        out_specs=[vmem] * 11,
        scratch_shapes=[
            pltpu.VMEM((2, 4096, 512), BF),
            pltpu.VMEM((2, 4, 64, 512), BF),
            pltpu.VMEM((2, 512, 512), BF),
            pltpu.VMEM((2, 256, 1024), F32),
            pltpu.SemaphoreType.DMA((26,)),
        ],
        compiler_params=pltpu.CompilerParams(vmem_limit_bytes=34 * 1024 * 1024),
        cost_estimate=pl.CostEstimate(
            flops=6 * 10**9, bytes_accessed=24 * 2**20, transcendentals=2**18
        ),
        name="attend",
    )(lengths, *arrays)


def final_kernel(own, core, near, far, near1, near2, far1, far2, out_ref):
    c = lax.rem(lax.axis_index("head"), 2)
    for i in range(2):
        mine = (own[0, i] + near[1, i].astype(F32)) + (near1[i].astype(F32) + near2[i].astype(F32))
        theirs = (core[0, i].astype(F32) + far[i].astype(F32)) + (
            far1[i].astype(F32) + far2[i].astype(F32)
        )
        out_ref[2 * i + c] = mine.astype(BF)
        out_ref[2 * i + 1 - c] = theirs.astype(BF)


def small_call(kernel, shape, name, *arrays):
    vmem = pl.BlockSpec(memory_space=pltpu.VMEM)
    return pl.pallas_call(
        kernel,
        out_shape=jax.ShapeDtypeStruct(shape, BF),
        in_specs=[vmem] * len(arrays),
        out_specs=vmem,
        name=name,
    )(*arrays)


def together(*values):
    return lax.optimization_barrier(values)


def summed(*parts):
    total = parts[0].astype(F32)
    for part in parts[1:]:
        total = total + part.astype(F32)
    return total.astype(BF)


def body(encoder, key_weight, value_weight, tile_mask, lengths, queries, cotangent):
    h = lax.axis_index("head")
    c = lax.rem(h, 2)

    def along(value, k):
        return lax.ppermute(value, "seq", [(a, a ^ k) for a in range(SEQ)])

    def flip(value, bits):
        return lax.ppermute(value, "head", [(a, a ^ bits) for a in range(4)])

    def across(value):
        return lax.ppermute(value, "grp", [(0, 1), (1, 0)])

    e0 = lax.dynamic_index_in_dim(encoder, h, 0, keepdims=False)
    e2 = along(e0, 2)
    e1 = along(e0, 1)
    w_own, m1, m2, m3 = prune(
        tile_mask, key_weight, value_weight, queries.reshape(64, 1024), cotangent.reshape(64, 1024)
    )
    e1, m2, w_own = together(e1, m2, w_own)
    z2 = along(m2, 2)
    e2, m1 = together(e2, m1)
    z1 = along(m1, 1)
    e3 = along(e2, 1)
    x1, x2 = flip(e1, 2), flip(e2, 2)
    x1, e3, m3 = together(x1, e3, m3)
    z3 = along(m3, 3)
    x3 = flip(e3, 2)
    y1, y2 = across(z1), across(z2)
    x2, x3, z3, w_own = together(x2, x3, z3, w_own)
    y3 = across(z3)
    packed = pack_call(w_own, z1, z2, y1, y2)
    packed_there = flip(packed, 1)
    early = early_call([encoder, e1, e2, e3, x1, x2, x3, packed, packed_there])
    z3_there = flip(z3, 1)
    y3, *early = together(y3, *early)
    y3_there = flip(y3, 1)
    outs = main_call(lengths, early + [packed, z3, y3, packed_there, z3_there, y3_there])
    att, qgrad, own = outs[:3]
    a3, b3, a2, b2, b1, a10, b0, to_core = outs[3:]
    from_core = flip(to_core, 1)
    front = jnp.stack([att, qgrad], axis=1)
    other = flip(front[1], 1)
    b3, a3 = flip(b3, 3), flip(a3, 2)
    b3, core, other, b2, a2 = together(b3, from_core, other, b2, a2)
    b2, a2 = flip(b2, 3), flip(a2, 2)
    far3, own = together(summed(core[3], b3), own)
    far3 = along(far3, 1)
    near3, core = together(summed(own[3], a3), core)
    near3 = along(near3, 1)
    b2, b1, a10 = together(b2, b1, a10)
    b1, a10 = flip(b1, 3), flip(a10, 2)
    far2, own = together(summed(core[2], b2, far3), own)
    far2 = along(far2, 2)
    a2, b0 = together(a2, b0)
    b0 = flip(b0, 3)
    back = jnp.stack([front[0], other]).reshape(2, 2, 2, SEQ, 16, 256).transpose(3, 0, 1, 2, 4, 5)
    near2, core = together(summed(own[2], a2, near3), core)
    near2 = along(near2, 2)
    far1, own, back = together(summed(core[1], b1), own, back)
    far1 = along(far1, 1)
    near1 = along(summed(own[1], a10[0]), 1)
    from_core = core
    back = lax.all_to_all(back, "seq", split_axis=0, concat_axis=0, tiled=True)
    back = back.transpose(2, 3, 1, 4, 0, 5).reshape(2, 2, 2, 16, 1024)
    back = jnp.where(c == 0, back, back[:, :, ::-1])
    back = back.reshape(2, DOCS, 16, 1024)
    b0, back = together(b0, back)
    encoder_grad = small_call(
        final_kernel, (DOCS, 64, 1024), "final", own, from_core, a10, b0, near1, near2, far1, far2
    )
    return (back[0], back[1], encoder_grad)


def solution(mesh):
    placed = (
        P("grp", "seq", None),
        P("seq", "head"),
        P("seq", "head"),
        P(None, "seq", "head"),
        P("grp"),
        P("grp", "seq", "head"),
        P("grp", "seq", "head"),
    )

    def step(*arrays):
        plan = body if fits(mesh, arrays[0], arrays[1], arrays[5]) else general_body
        return jax.shard_map(
            plan,
            mesh=mesh,
            in_specs=placed,
            out_specs=(P("grp", "seq", "head"),) * 3,
            check_vma=False,
        )(*arrays)

    return step
```

```python
import functools

import jax
import jax.numpy as jnp
from jax import lax
from jax.experimental import pallas as pl
from jax.experimental.pallas import tpu as pltpu
from jax.sharding import PartitionSpec as P

DH = 64
TILE = 64
DOCS = 4


SCALE = 0.125
FLOOR_SCORE = -1e30

BF = jnp.bfloat16
F32 = jnp.float32


def expand(tile_grid, tile_edge):
    return jnp.repeat(jnp.repeat(tile_grid, tile_edge, axis=0), tile_edge, axis=1)


def attend(keys, values, queries, cotangent, length):
    position = jnp.arange(keys.shape[0])[None, :]
    live = position < length
    scores = jnp.dot(queries, keys.T, preferred_element_type=jnp.float32) * SCALE
    scores = jnp.where(live, scores, FLOOR_SCORE)
    row_max = jnp.max(scores, axis=1, keepdims=True)
    weights = jnp.where(live, jnp.exp(scores - row_max), 0.0)
    probs = weights / jnp.sum(weights, axis=1, keepdims=True)
    probs_low = probs.astype(jnp.bfloat16)
    output = jnp.dot(probs_low, values, preferred_element_type=jnp.float32)
    delta = jnp.sum(cotangent.astype(jnp.float32) * output, axis=1, keepdims=True)
    prob_grad = jnp.dot(cotangent, values.T, preferred_element_type=jnp.float32)
    score_grad = (probs * (prob_grad - delta) * SCALE).astype(jnp.bfloat16)
    query_grad = jnp.dot(score_grad, keys, preferred_element_type=jnp.float32)
    key_grad = jnp.dot(score_grad.T, queries, preferred_element_type=jnp.float32)
    value_grad = jnp.dot(probs_low.T, cotangent, preferred_element_type=jnp.float32)
    return (
        output.astype(jnp.bfloat16),
        query_grad.astype(jnp.bfloat16),
        key_grad.astype(jnp.bfloat16),
        value_grad.astype(jnp.bfloat16),
    )


def project(encoder, key_piece, value_piece):
    count = key_piece.shape[0]
    flat = encoder.reshape(DOCS * encoder.shape[1], count)
    key_flat = jnp.dot(flat, key_piece, preferred_element_type=jnp.float32)
    value_flat = jnp.dot(flat, value_piece, preferred_element_type=jnp.float32)
    shape_out = (DOCS, encoder.shape[1], key_piece.shape[1])
    return (key_flat.reshape(shape_out), value_flat.reshape(shape_out))


def back_product(key_rows, value_rows, key_piece, value_piece):
    contract = (((1,), (1,)), ((), ()))
    total = lax.dot_general(key_rows, key_piece, contract, preferred_element_type=jnp.float32)
    return total + lax.dot_general(
        value_rows, value_piece, contract, preferred_element_type=jnp.float32
    )


def general_body(encoder, key_weight, value_weight, tile_mask, lengths, queries, cotangent):
    seq_count = lax.axis_size("seq")
    enc_rows = encoder.shape[1]
    dec_rows = queries.shape[1]
    group_heads = queries.shape[2] // DH
    pair_count = DOCS * group_heads
    local_pairs = pair_count // seq_count
    key_masked = key_weight * expand(tile_mask[0], TILE).astype(jnp.bfloat16)
    value_masked = value_weight * expand(tile_mask[1], TILE).astype(jnp.bfloat16)
    full_key, full_value = (
        lax.all_gather(key_masked, "seq", axis=0, tiled=True),
        lax.all_gather(value_masked, "seq", axis=0, tiled=True),
    )
    key_sum, value_sum = project(encoder, full_key, full_value)

    def to_pairs(first, second, rows):
        joined = jnp.concatenate(
            [
                first.reshape(DOCS, rows, group_heads, DH),
                second.reshape(DOCS, rows, group_heads, DH),
            ],
            axis=3,
        )
        return joined.transpose(0, 2, 1, 3).reshape(pair_count, rows, 2 * DH)

    def from_pairs(block, rows):
        shaped = block.reshape(DOCS, group_heads, rows, 2 * DH).transpose(0, 2, 1, 3)
        first = shaped[..., :DH].reshape(DOCS, rows, group_heads * DH)
        second = shaped[..., DH:].reshape(DOCS, rows, group_heads * DH)
        return (first, second)

    query_pairs = to_pairs(queries, cotangent, dec_rows)
    query_owned = lax.all_to_all(query_pairs, "seq", split_axis=0, concat_axis=1, tiled=True)
    kv_pairs = to_pairs(key_sum.astype(jnp.bfloat16), value_sum.astype(jnp.bfloat16), enc_rows)
    kv_owned = lax.all_to_all(kv_pairs, "seq", split_axis=0, concat_axis=1, tiled=True)
    pair_ids = lax.axis_index("seq") * local_pairs + jnp.arange(local_pairs)
    doc_of_pair = pair_ids // group_heads
    pair_length = jnp.sum(
        jnp.where(doc_of_pair[:, None] == jnp.arange(DOCS)[None, :], lengths[None, :], 0), axis=1
    )

    def owner_pair(items):
        pair_kv, pair_query, length = items
        output, query_grad, key_grad, value_grad = attend(
            pair_kv[:, :DH], pair_kv[:, DH:], pair_query[:, :DH], pair_query[:, DH:], length
        )
        return (
            jnp.concatenate([output, query_grad], axis=1),
            jnp.concatenate([key_grad, value_grad], axis=1),
        )

    front, back = lax.map(owner_pair, (kv_owned, query_owned, pair_length))
    front_rows, back_rows = (
        lax.all_to_all(front, "seq", split_axis=1, concat_axis=0, tiled=True),
        lax.all_to_all(back, "seq", split_axis=1, concat_axis=0, tiled=True),
    )
    attention, query_grad = from_pairs(front_rows, dec_rows)
    key_grads, value_grads = from_pairs(back_rows, enc_rows)
    key_rows = key_grads.reshape(DOCS * enc_rows, group_heads * DH)
    value_rows = value_grads.reshape(DOCS * enc_rows, group_heads * DH)
    grad_terms = back_product(key_rows, value_rows, full_key, full_value)
    grad_share = lax.psum_scatter(grad_terms, "head", scatter_dimension=1, tiled=True)
    encoder_grad = grad_share.astype(jnp.bfloat16).reshape(DOCS, enc_rows, grad_share.shape[1])
    return (attention, query_grad, encoder_grad)


SEQ = 4
PIECE = 512
SENT = PIECE + 64


def fits(mesh, encoder, key_weight, queries):
    return (
        mesh.shape["seq"] == SEQ
        and mesh.shape["head"] == 4
        and mesh.shape["grp"] == 2
        and encoder.shape == (DOCS * 2, 256, 4096)
        and key_weight.shape == (4096, 4096)
        and queries.shape == (DOCS * 2, 64, 4096)
    )


def prune_kernel(mask_ref, key_ref, value_ref, query_ref, cot_ref, own_ref, *message_refs):
    s, g = lax.axis_index("seq"), lax.axis_index("grp")
    left = lax.broadcasted_iota(jnp.int32, (1, 128), 1) < TILE

    def write(out_ref, first_tile, tiles, column):
        for t in range(tiles):
            tile = first_tile + t
            row = pl.ds(pl.multiple_of(tile * TILE, TILE), TILE)
            for side, ref in ((0, key_ref), (1, value_ref)):
                for part in range(2):
                    at = pl.ds(pl.multiple_of(column * 256 + part * 128, 128), 128)
                    first = mask_ref[side, tile, column * 4 + part * 2]
                    second = mask_ref[side, tile, column * 4 + part * 2 + 1]
                    keep = jnp.where(left, first, second).astype(F32)
                    to = side * 256 + part * 128
                    out_ref[t * TILE : (t + 1) * TILE, to : to + 128] = (
                        ref[row, at].astype(F32) * keep
                    ).astype(BF)
        at = pl.ds(pl.multiple_of(column * 256, 256), 256)
        out_ref[tiles * TILE :, 0:256] = query_ref[:, at]
        out_ref[tiles * TILE :, 256:512] = cot_ref[:, at]

    first, second, third = message_refs
    write(second, g * 8, 8, lax.bitwise_xor(s, 2))
    write(first, g * 8, 8, lax.bitwise_xor(s, 1))
    write(third, g * 8, 8, lax.bitwise_xor(s, 3))
    write(own_ref, 0, 16, s)


def prune(tile_mask, key_weight, value_weight, queries, cotangent):
    whole = pl.BlockSpec(memory_space=pltpu.VMEM)
    rows = (2 * PIECE + 64, SENT, SENT, SENT)
    return pl.pallas_call(
        prune_kernel,
        out_shape=[jax.ShapeDtypeStruct((count, 512), BF) for count in rows],
        in_specs=[pl.BlockSpec(memory_space=pltpu.SMEM)] + [whole] * 4,
        out_specs=[whole] * len(rows),
        compiler_params=pltpu.CompilerParams(vmem_limit_bytes=12 * 1024 * 1024),
        name="prune",
    )(tile_mask, key_weight, value_weight, queries, cotangent)


NT = (((1,), (1,)), ((), ()))
TN = (((0,), (0,)), ((), ()))
NN = (((1,), (0,)), ((), ()))


def dot(a, b, dims=NN):
    return lax.dot_general(a, b, dims, preferred_element_type=F32)


def partial_blocks(block, grad, weight, part):
    def column(n, carry):
        at = pl.ds(pl.multiple_of(block * 1024 + n * 256, 256), 256)
        total = dot(grad[0], weight[0, at, :], NT) + dot(grad[1], weight[1, at, :], NT)
        part[:, :, pl.ds(pl.multiple_of(n * 256, 256), 256)] = total.reshape(2, 256, 256)
        return carry

    lax.fori_loop(0, 4, column, 0)


class Mover:
    def __init__(self, sems):
        self.sems = sems
        self.used = 0

    def start(self, pairs):
        copies = []
        for src, dst in pairs:
            copy = pltpu.make_async_copy(src, dst, self.sems.at[self.used])
            copy.start()
            self.used += 1
            copies.append(copy)
        return copies


def piece_rows(w_s, core, at, first, count):
    return w_s.at[core, pl.ds(pl.multiple_of(at * 1024 + first, 256), count)]


PACKED = 3 * 2 * PIECE


def pack_kernel(own, z1, z2, y1, y2, out_ref, sems):
    g = lax.axis_index("grp")
    pairs = [(own.at[0 : 2 * PIECE], out_ref.at[0 : 2 * PIECE])]
    pairs.append((own.at[2 * PIECE : 2 * PIECE + 64], out_ref.at[PACKED : PACKED + 64]))
    for k, z, y in ((1, z1, y1), (2, z2, y2)):
        for piece, side in ((z, g), (y, 1 - g)):
            first = pl.multiple_of(2 * PIECE * k + side * PIECE, PIECE)
            pairs.append((piece.at[0:PIECE], out_ref.at[pl.ds(first, PIECE)]))
        pairs.append((z.at[PIECE:SENT], out_ref.at[PACKED + 64 * k : PACKED + 64 * k + 64]))
    for copy in Mover(sems).start(pairs):
        copy.wait()


def pack_call(*arrays):
    here = pl.BlockSpec(memory_space=pl.ANY)
    return pl.pallas_call(
        pack_kernel,
        out_shape=jax.ShapeDtypeStruct((PACKED + 192, 512), BF),
        in_specs=[here] * len(arrays),
        out_specs=pl.BlockSpec(memory_space=pltpu.VMEM),
        scratch_shapes=[pltpu.SemaphoreType.DMA((8,))],
        compiler_params=pltpu.CompilerParams(vmem_limit_bytes=6 * 1024 * 1024),
        cost_estimate=pl.CostEstimate(flops=1, bytes_accessed=1, transcendentals=0),
        name="pack",
    )(*arrays)


def early_weights(w_s, c, s, mine, theirs):
    pairs = []
    for core, packed in ((c, mine), (1 - c, theirs)):
        for k in range(3):
            rows = packed.at[2 * PIECE * k : 2 * PIECE * (k + 1)]
            pairs.append((rows, piece_rows(w_s, core, lax.bitwise_xor(s, k), 0, 2 * PIECE)))
    return pairs


def early_kernel(*refs):
    enc, e1, e2, e3, x1, x2, x3 = refs[:7]
    mine, theirs = refs[7:9]
    sum_ref, last_ref, enc_s, w_s, sems = refs[9:]
    s, h = lax.axis_index("seq"), lax.axis_index("head")
    c = lax.rem(h, 2)
    x = h // 2
    mover = Mover(sems)

    def rows_of(doc, at):
        return enc_s.at[pl.ds(pl.multiple_of(doc * 256 + at * 64, 64), 64)]

    pairs = [(enc.at[2 * i + c], rows_of(i, s)) for i in range(2)]
    for k, (own, other) in enumerate(((e1, x1), (e2, x2), (e3, x3))):
        at = lax.bitwise_xor(s, k + 1)
        pairs += [(own, rows_of(x, at)), (other, rows_of(1 - x, at))]
    pairs += early_weights(w_s, c, s, mine, theirs)
    for copy in mover.start(pairs):
        copy.wait()

    def columns(k):
        at = lax.bitwise_xor(s, k)
        return pl.ds(pl.multiple_of(at * 1024, 1024), 1024)

    for core in range(2):
        for half in range(2):
            row = slice(half * 256, half * 256 + 256)
            total = dot(enc_s[row, columns(0)], w_s[core, columns(0), :])
            for k in (1, 2):
                total = total + dot(enc_s[row, columns(k)], w_s[core, columns(k), :])
            sum_ref[core, row] = total
    last_ref[...] = enc_s[:, columns(3)]


def early_call(arrays):
    here = pl.BlockSpec(memory_space=pl.ANY)
    vmem = pl.BlockSpec(memory_space=pltpu.VMEM)
    return pl.pallas_call(
        early_kernel,
        out_shape=[
            jax.ShapeDtypeStruct((2, 512, 512), F32),
            jax.ShapeDtypeStruct((512, 1024), BF),
        ],
        in_specs=[here] * len(arrays),
        out_specs=[vmem] * 2,
        scratch_shapes=[
            pltpu.VMEM((512, 4096), BF),
            pltpu.VMEM((2, 4096, 512), BF),
            pltpu.SemaphoreType.DMA((18,)),
        ],
        compiler_params=pltpu.CompilerParams(vmem_limit_bytes=28 * 1024 * 1024),
        cost_estimate=pl.CostEstimate(
            flops=1, bytes_accessed=1, transcendentals=0
        ),
        name="early",
    )(*arrays)


def main_kernel(lengths, *refs):
    early_sum, last_rows = refs[:2]
    mine, theirs = refs[2:5], refs[5:8]
    (
        att_ref, qg_ref, own_ref,
        a3, b3, a2, b2, b1, a10, b0, core_ref,
        w_s, qc_s, grad_s, part_s, sems,
    ) = refs[8:]
    s, g, h = lax.axis_index("seq"), lax.axis_index("grp"), lax.axis_index("head")
    c = lax.rem(h, 2)
    mover = Mover(sems)
    far = lax.bitwise_xor(s, 3)
    pairs = []
    for core, pieces in ((c, mine), (1 - c, theirs)):
        packed, z3, y3 = pieces
        for src, side in ((z3, g), (y3, 1 - g)):
            pairs.append((src.at[0:PIECE], piece_rows(w_s, core, far, side * PIECE, PIECE)))
        for k in range(3):
            rows = packed.at[PACKED + 64 * k : PACKED + 64 * k + 64]
            pairs.append((rows, qc_s.at[core, lax.bitwise_xor(s, k)]))
        pairs.append((z3.at[PIECE:SENT], qc_s.at[core, far]))
    now = mover.start(pairs)
    later = mover.start(early_weights(w_s, c, s, mine[0], theirs[0]))
    for copy in now:
        copy.wait()
    far_rows = pl.ds(pl.multiple_of(far * 1024, 1024), 1024)

    row_head = lax.broadcasted_iota(jnp.int32, (256, 256), 0) // DH
    col_head = lax.broadcasted_iota(jnp.int32, (256, 256), 1) // DH
    same = row_head == col_head
    position = lax.broadcasted_iota(jnp.int32, (256, 256), 1)

    def spread(block):
        four = jnp.concatenate([block] * 4, axis=0)
        return jnp.where(same, four, jnp.zeros_like(four))

    def gather_heads(block):
        kept = jnp.where(same, block, 0.0)
        return (kept[0:64] + kept[64:128]) + (kept[128:192] + kept[192:256])

    for core in range(2):
        slot = lax.rem(core + c, 2)
        for doc in range(2):
            row = slice(doc * 256, doc * 256 + 256)
            both = early_sum[core, row] + dot(last_rows[row], w_s[core, far_rows, :])
            keys = both[:, :256].astype(BF)
            values = both[:, 256:].astype(BF)
            at = pl.ds(pl.multiple_of((2 * doc + c) * 16, 16), 16)
            query = spread(qc_s[core, :, at, 0:256].reshape(64, 256))
            cot = spread(qc_s[core, :, at, 256:512].reshape(64, 256))
            live = position < lengths[2 * doc + c]
            scores = dot(query, keys, NT) * SCALE
            scores = jnp.where(live, scores, FLOOR_SCORE)
            row_max = jnp.max(scores, axis=1, keepdims=True)
            weights = jnp.where(live, jnp.exp(scores - row_max), 0.0)
            probs = weights / jnp.sum(weights, axis=1, keepdims=True)
            low = probs.astype(BF)
            output = dot(low, values)
            delta = jnp.sum(cot.astype(F32) * output, axis=1, keepdims=True)
            prob_grad = dot(cot, values, NT)
            score_grad = (probs * (prob_grad - delta) * SCALE).astype(BF)
            query_grad = dot(score_grad, keys)
            att_ref[slot, doc] = gather_heads(output).astype(BF)
            qg_ref[slot, doc] = gather_heads(query_grad).astype(BF)
            grad_s[core, doc * 256 : (doc + 1) * 256, 0:256] = dot(score_grad, query, TN).astype(BF)
            grad_s[core, doc * 256 : (doc + 1) * 256, 256:512] = dot(low, cot, TN).astype(BF)

    for copy in later:
        copy.wait()
    cores = [core_ref.at[k] for k in range(4)]
    owns = [own_ref.at[k] for k in range(4)]
    for flip, outs in (
        (2, (a10.at[1], a10.at[0], a2, a3)),
        (3, (b0, b1, b2, b3)),
        (1, cores),
        (0, owns),
    ):
        partial_blocks(lax.bitwise_xor(h, flip), grad_s, w_s, part_s)
        for k in range(4):
            at = pl.ds(pl.multiple_of(lax.bitwise_xor(s, k) * 64, 64), 64)
            for doc in range(2):
                outs[k][doc] = part_s[doc, at, :].astype(outs[k].dtype)


def main_call(lengths, arrays):
    here = pl.BlockSpec(memory_space=pl.ANY)
    vmem = pl.BlockSpec(memory_space=pltpu.VMEM)
    smem = pl.BlockSpec(memory_space=pltpu.SMEM)
    piece = jax.ShapeDtypeStruct((2, 64, 1024), BF)
    front = jax.ShapeDtypeStruct((2, 2, 64, 256), BF)
    return pl.pallas_call(
        main_kernel,
        out_shape=[
            front,
            front,
            jax.ShapeDtypeStruct((4, 2, 64, 1024), F32),
        ]
        + [piece] * 5
        + [jax.ShapeDtypeStruct((2, 2, 64, 1024), BF)]
        + [piece]
        + [jax.ShapeDtypeStruct((4, 2, 64, 1024), BF)],
        in_specs=[smem] + [vmem] * 2 + [here] * (len(arrays) - 2),
        out_specs=[vmem] * 11,
        scratch_shapes=[
            pltpu.VMEM((2, 4096, 512), BF),
            pltpu.VMEM((2, 4, 64, 512), BF),
            pltpu.VMEM((2, 512, 512), BF),
            pltpu.VMEM((2, 256, 1024), F32),
            pltpu.SemaphoreType.DMA((26,)),
        ],
        compiler_params=pltpu.CompilerParams(vmem_limit_bytes=34 * 1024 * 1024),
        cost_estimate=pl.CostEstimate(
            flops=6 * 10**9, bytes_accessed=24 * 2**20, transcendentals=2**18
        ),
        name="attend",
    )(lengths, *arrays)


def final_kernel(own, core, near, far, near1, near2, far1, far2, out_ref):
    c = lax.rem(lax.axis_index("head"), 2)
    for i in range(2):
        mine = (own[0, i] + near[1, i].astype(F32)) + (near1[i].astype(F32) + near2[i].astype(F32))
        theirs = (core[0, i].astype(F32) + far[i].astype(F32)) + (
            far1[i].astype(F32) + far2[i].astype(F32)
        )
        out_ref[2 * i + c] = mine.astype(BF)
        out_ref[2 * i + 1 - c] = theirs.astype(BF)


def small_call(kernel, shape, name, *arrays):
    vmem = pl.BlockSpec(memory_space=pltpu.VMEM)
    return pl.pallas_call(
        kernel,
        out_shape=jax.ShapeDtypeStruct(shape, BF),
        in_specs=[vmem] * len(arrays),
        out_specs=vmem,
        compiler_params=pltpu.CompilerParams(vmem_limit_bytes=12 * 1024 * 1024),
        name=name,
    )(*arrays)


def together(*values):
    return lax.optimization_barrier(values)


def summed(*parts):
    total = parts[0].astype(F32)
    for part in parts[1:]:
        total = total + part.astype(F32)
    return total.astype(BF)


def body(encoder, key_weight, value_weight, tile_mask, lengths, queries, cotangent):
    h = lax.axis_index("head")
    c = lax.rem(h, 2)

    def along(value, k):
        return lax.ppermute(value, "seq", [(a, a ^ k) for a in range(SEQ)])

    def flip(value, bits):
        return lax.ppermute(value, "head", [(a, a ^ bits) for a in range(4)])

    def across(value):
        return lax.ppermute(value, "grp", [(0, 1), (1, 0)])

    e0 = lax.dynamic_index_in_dim(encoder, h, 0, keepdims=False)
    e2 = along(e0, 2)
    e1 = along(e0, 1)
    w_own, m1, m2, m3 = prune(
        tile_mask, key_weight, value_weight, queries.reshape(64, 1024), cotangent.reshape(64, 1024)
    )
    e1, e2, m2, w_own = together(e1, e2, m2, w_own)
    z2 = along(m2, 2)
    e3 = along(e2, 1)
    x1, x2 = flip(e1, 2), flip(e2, 2)
    x1, m1 = together(x1, m1)
    z1 = along(m1, 1)
    x2, m3 = together(x2, m3)
    z3 = along(m3, 3)
    x3 = flip(e3, 2)
    y1, y2 = across(z1), across(z2)
    x2, x3, z3, w_own = together(x2, x3, z3, w_own)
    y3 = across(z3)
    packed = pack_call(w_own, z1, z2, y1, y2)
    packed_there = flip(packed, 1)
    early = early_call([encoder, e1, e2, e3, x1, x2, x3, packed, packed_there])
    z3_there = flip(z3, 1)
    y3, *early = together(y3, *early)
    y3_there = flip(y3, 1)
    outs = main_call(lengths, early + [packed, z3, y3, packed_there, z3_there, y3_there])
    att, qgrad, own = outs[:3]
    a3, b3, a2, b2, b1, a10, b0, to_core = outs[3:]
    from_core = flip(to_core, 1)
    front = jnp.stack([att, qgrad], axis=1)
    other = flip(front[1], 1)
    b3, a3 = flip(b3, 3), flip(a3, 2)
    b3, core, other, b2, a2 = together(b3, from_core, other, b2, a2)
    b2, a2 = flip(b2, 3), flip(a2, 2)
    far3, own = together(summed(core[3], b3), own)
    far3 = along(far3, 1)
    back = jnp.stack([front[0], other]).reshape(2, 2, 2, SEQ, 16, 256).transpose(3, 0, 1, 2, 4, 5)
    near3, core, back = together(summed(own[3], a3), core, back)
    near3 = along(near3, 1)
    b2, b1, a10 = together(b2, b1, a10)
    b1, a10 = flip(b1, 3), flip(a10, 2)
    far2, own = together(summed(core[2], b2, far3), own)
    far2 = along(far2, 2)
    a2, b0 = together(a2, b0)
    b0 = flip(b0, 3)
    near2, core = together(summed(own[2], a2, near3), core)
    near2 = along(near2, 2)
    far1, own = together(summed(core[1], b1), own)
    far1 = along(far1, 1)
    a10, near2, far2 = together(a10, near2, far2)
    near1 = along(summed(own[1], a10[0]), 1)
    from_core = core
    back = lax.all_to_all(back, "seq", split_axis=0, concat_axis=0, tiled=True)
    back = back.transpose(2, 3, 1, 4, 0, 5).reshape(2, 2, 2, 16, 1024)
    back = jnp.where(c == 0, back, back[:, :, ::-1])
    back = back.reshape(2, DOCS, 16, 1024)
    b0, back = together(b0, back)
    encoder_grad = small_call(
        final_kernel, (DOCS, 64, 1024), "final", own, from_core, a10, b0, near1, near2, far1, far2
    )
    return (back[0], back[1], encoder_grad)


def solution(mesh):
    placed = (
        P("grp", "seq", None),
        P("seq", "head"),
        P("seq", "head"),
        P(None, "seq", "head"),
        P("grp"),
        P("grp", "seq", "head"),
        P("grp", "seq", "head"),
    )

    def step(*arrays):
        plan = body if fits(mesh, arrays[0], arrays[1], arrays[5]) else general_body
        return jax.shard_map(
            plan,
            mesh=mesh,
            in_specs=placed,
            out_specs=(P("grp", "seq", "head"),) * 3,
            check_vma=False,
        )(*arrays)

    return step
```

```python
import functools

import jax
import jax.numpy as jnp
from jax import lax
from jax.experimental import pallas as pl
from jax.experimental.pallas import tpu as pltpu
from jax.sharding import PartitionSpec as P

DH = 64
TILE = 64
DOCS = 4


SCALE = 0.125
FLOOR_SCORE = -1e30

BF = jnp.bfloat16
F32 = jnp.float32


def expand(tile_grid, tile_edge):
    return jnp.repeat(jnp.repeat(tile_grid, tile_edge, axis=0), tile_edge, axis=1)


def attend(keys, values, queries, cotangent, length):
    position = jnp.arange(keys.shape[0])[None, :]
    live = position < length
    scores = jnp.dot(queries, keys.T, preferred_element_type=jnp.float32) * SCALE
    scores = jnp.where(live, scores, FLOOR_SCORE)
    row_max = jnp.max(scores, axis=1, keepdims=True)
    weights = jnp.where(live, jnp.exp(scores - row_max), 0.0)
    probs = weights / jnp.sum(weights, axis=1, keepdims=True)
    probs_low = probs.astype(jnp.bfloat16)
    output = jnp.dot(probs_low, values, preferred_element_type=jnp.float32)
    delta = jnp.sum(cotangent.astype(jnp.float32) * output, axis=1, keepdims=True)
    prob_grad = jnp.dot(cotangent, values.T, preferred_element_type=jnp.float32)
    score_grad = (probs * (prob_grad - delta) * SCALE).astype(jnp.bfloat16)
    query_grad = jnp.dot(score_grad, keys, preferred_element_type=jnp.float32)
    key_grad = jnp.dot(score_grad.T, queries, preferred_element_type=jnp.float32)
    value_grad = jnp.dot(probs_low.T, cotangent, preferred_element_type=jnp.float32)
    return (
        output.astype(jnp.bfloat16),
        query_grad.astype(jnp.bfloat16),
        key_grad.astype(jnp.bfloat16),
        value_grad.astype(jnp.bfloat16),
    )


def project(encoder, key_piece, value_piece):
    count = key_piece.shape[0]
    flat = encoder.reshape(DOCS * encoder.shape[1], count)
    key_flat = jnp.dot(flat, key_piece, preferred_element_type=jnp.float32)
    value_flat = jnp.dot(flat, value_piece, preferred_element_type=jnp.float32)
    shape_out = (DOCS, encoder.shape[1], key_piece.shape[1])
    return (key_flat.reshape(shape_out), value_flat.reshape(shape_out))


def back_product(key_rows, value_rows, key_piece, value_piece):
    contract = (((1,), (1,)), ((), ()))
    total = lax.dot_general(key_rows, key_piece, contract, preferred_element_type=jnp.float32)
    return total + lax.dot_general(
        value_rows, value_piece, contract, preferred_element_type=jnp.float32
    )


def general_body(encoder, key_weight, value_weight, tile_mask, lengths, queries, cotangent):
    seq_count = lax.axis_size("seq")
    enc_rows = encoder.shape[1]
    dec_rows = queries.shape[1]
    group_heads = queries.shape[2] // DH
    pair_count = DOCS * group_heads
    local_pairs = pair_count // seq_count
    key_masked = key_weight * expand(tile_mask[0], TILE).astype(jnp.bfloat16)
    value_masked = value_weight * expand(tile_mask[1], TILE).astype(jnp.bfloat16)
    full_key, full_value = (
        lax.all_gather(key_masked, "seq", axis=0, tiled=True),
        lax.all_gather(value_masked, "seq", axis=0, tiled=True),
    )
    key_sum, value_sum = project(encoder, full_key, full_value)

    def to_pairs(first, second, rows):
        joined = jnp.concatenate(
            [
                first.reshape(DOCS, rows, group_heads, DH),
                second.reshape(DOCS, rows, group_heads, DH),
            ],
            axis=3,
        )
        return joined.transpose(0, 2, 1, 3).reshape(pair_count, rows, 2 * DH)

    def from_pairs(block, rows):
        shaped = block.reshape(DOCS, group_heads, rows, 2 * DH).transpose(0, 2, 1, 3)
        first = shaped[..., :DH].reshape(DOCS, rows, group_heads * DH)
        second = shaped[..., DH:].reshape(DOCS, rows, group_heads * DH)
        return (first, second)

    query_pairs = to_pairs(queries, cotangent, dec_rows)
    query_owned = lax.all_to_all(query_pairs, "seq", split_axis=0, concat_axis=1, tiled=True)
    kv_pairs = to_pairs(key_sum.astype(jnp.bfloat16), value_sum.astype(jnp.bfloat16), enc_rows)
    kv_owned = lax.all_to_all(kv_pairs, "seq", split_axis=0, concat_axis=1, tiled=True)
    pair_ids = lax.axis_index("seq") * local_pairs + jnp.arange(local_pairs)
    doc_of_pair = pair_ids // group_heads
    pair_length = jnp.sum(
        jnp.where(doc_of_pair[:, None] == jnp.arange(DOCS)[None, :], lengths[None, :], 0), axis=1
    )

    def owner_pair(items):
        pair_kv, pair_query, length = items
        output, query_grad, key_grad, value_grad = attend(
            pair_kv[:, :DH], pair_kv[:, DH:], pair_query[:, :DH], pair_query[:, DH:], length
        )
        return (
            jnp.concatenate([output, query_grad], axis=1),
            jnp.concatenate([key_grad, value_grad], axis=1),
        )

    front, back = lax.map(owner_pair, (kv_owned, query_owned, pair_length))
    front_rows, back_rows = (
        lax.all_to_all(front, "seq", split_axis=1, concat_axis=0, tiled=True),
        lax.all_to_all(back, "seq", split_axis=1, concat_axis=0, tiled=True),
    )
    attention, query_grad = from_pairs(front_rows, dec_rows)
    key_grads, value_grads = from_pairs(back_rows, enc_rows)
    key_rows = key_grads.reshape(DOCS * enc_rows, group_heads * DH)
    value_rows = value_grads.reshape(DOCS * enc_rows, group_heads * DH)
    grad_terms = back_product(key_rows, value_rows, full_key, full_value)
    grad_share = lax.psum_scatter(grad_terms, "head", scatter_dimension=1, tiled=True)
    encoder_grad = grad_share.astype(jnp.bfloat16).reshape(DOCS, enc_rows, grad_share.shape[1])
    return (attention, query_grad, encoder_grad)


SEQ = 4
PIECE = 512
SENT = PIECE + 64


def fits(mesh, encoder, key_weight, queries):
    return (
        mesh.shape["seq"] == SEQ
        and mesh.shape["head"] == 4
        and mesh.shape["grp"] == 2
        and encoder.shape == (DOCS * 2, 256, 4096)
        and key_weight.shape == (4096, 4096)
        and queries.shape == (DOCS * 2, 64, 4096)
    )


def prune_kernel(mask_ref, key_ref, value_ref, query_ref, cot_ref, own_ref, *message_refs):
    s, g = lax.axis_index("seq"), lax.axis_index("grp")
    left = lax.broadcasted_iota(jnp.int32, (1, 128), 1) < TILE

    def write(out_ref, first_tile, tiles, column):
        for t in range(tiles):
            tile = first_tile + t
            row = pl.ds(pl.multiple_of(tile * TILE, TILE), TILE)
            for side, ref in ((0, key_ref), (1, value_ref)):
                for part in range(2):
                    at = pl.ds(pl.multiple_of(column * 256 + part * 128, 128), 128)
                    first = mask_ref[side, tile, column * 4 + part * 2]
                    second = mask_ref[side, tile, column * 4 + part * 2 + 1]
                    keep = jnp.where(left, first, second).astype(F32)
                    to = side * 256 + part * 128
                    out_ref[t * TILE : (t + 1) * TILE, to : to + 128] = (
                        ref[row, at].astype(F32) * keep
                    ).astype(BF)
        at = pl.ds(pl.multiple_of(column * 256, 256), 256)
        out_ref[tiles * TILE :, 0:256] = query_ref[:, at]
        out_ref[tiles * TILE :, 256:512] = cot_ref[:, at]

    first, second, third = message_refs
    write(second, g * 8, 8, lax.bitwise_xor(s, 2))
    write(first, g * 8, 8, lax.bitwise_xor(s, 1))
    write(third, g * 8, 8, lax.bitwise_xor(s, 3))
    write(own_ref, 0, 16, s)


def prune(tile_mask, key_weight, value_weight, queries, cotangent):
    whole = pl.BlockSpec(memory_space=pltpu.VMEM)
    rows = (2 * PIECE + 64, SENT, SENT, SENT)
    return pl.pallas_call(
        prune_kernel,
        out_shape=[jax.ShapeDtypeStruct((count, 512), BF) for count in rows],
        in_specs=[pl.BlockSpec(memory_space=pltpu.SMEM)] + [whole] * 4,
        out_specs=[whole] * len(rows),
        compiler_params=pltpu.CompilerParams(vmem_limit_bytes=12 * 1024 * 1024),
        name="prune",
    )(tile_mask, key_weight, value_weight, queries, cotangent)


NT = (((1,), (1,)), ((), ()))
TN = (((0,), (0,)), ((), ()))
NN = (((1,), (0,)), ((), ()))


def dot(a, b, dims=NN):
    return lax.dot_general(a, b, dims, preferred_element_type=F32)


class Mover:
    def __init__(self, sems):
        self.sems = sems
        self.used = 0

    def start(self, pairs):
        copies = []
        for src, dst in pairs:
            copy = pltpu.make_async_copy(src, dst, self.sems.at[self.used])
            copy.start()
            self.used += 1
            copies.append(copy)
        return copies


def piece_rows(w_s, core, at, first, count):
    return w_s.at[core, pl.ds(pl.multiple_of(at * 1024 + first, 256), count)]


PACKED = 3 * 2 * PIECE


def pack_kernel(own, z1, z2, y1, y2, out_ref, sems):
    g = lax.axis_index("grp")
    pairs = [(own.at[0 : 2 * PIECE], out_ref.at[0 : 2 * PIECE])]
    pairs.append((own.at[2 * PIECE : 2 * PIECE + 64], out_ref.at[PACKED : PACKED + 64]))
    for k, z, y in ((1, z1, y1), (2, z2, y2)):
        for piece, side in ((z, g), (y, 1 - g)):
            first = pl.multiple_of(2 * PIECE * k + side * PIECE, PIECE)
            pairs.append((piece.at[0:PIECE], out_ref.at[pl.ds(first, PIECE)]))
        pairs.append((z.at[PIECE:SENT], out_ref.at[PACKED + 64 * k : PACKED + 64 * k + 64]))
    for copy in Mover(sems).start(pairs):
        copy.wait()


def pack_call(*arrays):
    here = pl.BlockSpec(memory_space=pl.ANY)
    return pl.pallas_call(
        pack_kernel,
        out_shape=jax.ShapeDtypeStruct((PACKED + 192, 512), BF),
        in_specs=[here] * len(arrays),
        out_specs=pl.BlockSpec(memory_space=pltpu.VMEM),
        scratch_shapes=[pltpu.SemaphoreType.DMA((8,))],
        compiler_params=pltpu.CompilerParams(vmem_limit_bytes=6 * 1024 * 1024),
        cost_estimate=pl.CostEstimate(flops=1, bytes_accessed=1, transcendentals=0),
        name="pack",
    )(*arrays)


def early_weights(w_s, c, s, mine, theirs):
    pairs = []
    for core, packed in ((c, mine), (1 - c, theirs)):
        for k in range(3):
            rows = packed.at[2 * PIECE * k : 2 * PIECE * (k + 1)]
            pairs.append((rows, piece_rows(w_s, core, lax.bitwise_xor(s, k), 0, 2 * PIECE)))
    return pairs


def early_kernel(*refs):
    enc, e1, e2, e3, x1, x2, x3 = refs[:7]
    mine, theirs = refs[7:9]
    sum_ref, last_ref, enc_s, w_s, sems = refs[9:]
    s, h = lax.axis_index("seq"), lax.axis_index("head")
    c = lax.rem(h, 2)
    x = h // 2
    mover = Mover(sems)

    def rows_of(doc, at):
        return enc_s.at[pl.ds(pl.multiple_of(doc * 256 + at * 64, 64), 64)]

    pairs = [(enc.at[2 * i + c], rows_of(i, s)) for i in range(2)]
    for k, (own, other) in enumerate(((e1, x1), (e2, x2), (e3, x3))):
        at = lax.bitwise_xor(s, k + 1)
        pairs += [(own, rows_of(x, at)), (other, rows_of(1 - x, at))]
    pairs += early_weights(w_s, c, s, mine, theirs)
    for copy in mover.start(pairs):
        copy.wait()

    def columns(k):
        at = lax.bitwise_xor(s, k)
        return pl.ds(pl.multiple_of(at * 1024, 1024), 1024)

    for core in range(2):
        for half in range(2):
            row = slice(half * 256, half * 256 + 256)
            total = dot(enc_s[row, columns(0)], w_s[core, columns(0), :])
            for k in (1, 2):
                total = total + dot(enc_s[row, columns(k)], w_s[core, columns(k), :])
            sum_ref[core, row] = total
    last_ref[...] = enc_s[:, columns(3)]


def early_call(arrays):
    here = pl.BlockSpec(memory_space=pl.ANY)
    vmem = pl.BlockSpec(memory_space=pltpu.VMEM)
    return pl.pallas_call(
        early_kernel,
        out_shape=[
            jax.ShapeDtypeStruct((2, 512, 512), F32),
            jax.ShapeDtypeStruct((512, 1024), BF),
        ],
        in_specs=[here] * len(arrays),
        out_specs=[vmem] * 2,
        scratch_shapes=[
            pltpu.VMEM((512, 4096), BF),
            pltpu.VMEM((2, 4096, 512), BF),
            pltpu.SemaphoreType.DMA((18,)),
        ],
        compiler_params=pltpu.CompilerParams(vmem_limit_bytes=28 * 1024 * 1024),
        cost_estimate=pl.CostEstimate(
            flops=1, bytes_accessed=1, transcendentals=0
        ),
        name="early",
    )(*arrays)


def main_kernel(lengths, *refs):
    early_sum, last_rows = refs[:2]
    mine, theirs = refs[2:5], refs[5:8]
    (
        att_ref, qg_ref, own_ref,
        a3, b3, a2, b2, b1, a10, b0, core_ref,
        w_s, qc_s, grad_s, sems,
    ) = refs[8:]
    s, g, h = lax.axis_index("seq"), lax.axis_index("grp"), lax.axis_index("head")
    c = lax.rem(h, 2)
    mover = Mover(sems)
    far = lax.bitwise_xor(s, 3)
    pairs = []
    for core, pieces in ((c, mine), (1 - c, theirs)):
        packed, z3, y3 = pieces
        for src, side in ((z3, g), (y3, 1 - g)):
            pairs.append((src.at[0:PIECE], piece_rows(w_s, core, far, side * PIECE, PIECE)))
        for k in range(3):
            rows = packed.at[PACKED + 64 * k : PACKED + 64 * k + 64]
            pairs.append((rows, qc_s.at[core, lax.bitwise_xor(s, k)]))
        pairs.append((z3.at[PIECE:SENT], qc_s.at[core, far]))
    now = mover.start(pairs)
    later = mover.start(early_weights(w_s, c, s, mine[0], theirs[0]))
    for copy in now:
        copy.wait()
    far_rows = pl.ds(pl.multiple_of(far * 1024, 1024), 1024)

    row_head = lax.broadcasted_iota(jnp.int32, (256, 256), 0) // DH
    col_head = lax.broadcasted_iota(jnp.int32, (256, 256), 1) // DH
    same = row_head == col_head
    position = lax.broadcasted_iota(jnp.int32, (256, 256), 1)

    def spread(block):
        four = jnp.concatenate([block] * 4, axis=0)
        return jnp.where(same, four, jnp.zeros_like(four))

    def gather_heads(block):
        kept = jnp.where(same, block, 0.0)
        return (kept[0:64] + kept[64:128]) + (kept[128:192] + kept[192:256])

    for core in range(2):
        slot = lax.rem(core + c, 2)
        for doc in range(2):
            row = slice(doc * 256, doc * 256 + 256)
            both = early_sum[core, row] + dot(last_rows[row], w_s[core, far_rows, :])
            keys = both[:, :256].astype(BF)
            values = both[:, 256:].astype(BF)
            at = pl.ds(pl.multiple_of((2 * doc + c) * 16, 16), 16)
            query = spread(qc_s[core, :, at, 0:256].reshape(64, 256))
            cot = spread(qc_s[core, :, at, 256:512].reshape(64, 256))
            live = position < lengths[2 * doc + c]
            scores = dot(query, keys, NT) * SCALE
            scores = jnp.where(live, scores, FLOOR_SCORE)
            row_max = jnp.max(scores, axis=1, keepdims=True)
            weights = jnp.where(live, jnp.exp(scores - row_max), 0.0)
            probs = weights / jnp.sum(weights, axis=1, keepdims=True)
            low = probs.astype(BF)
            output = dot(low, values)
            delta = jnp.sum(cot.astype(F32) * output, axis=1, keepdims=True)
            prob_grad = dot(cot, values, NT)
            score_grad = (probs * (prob_grad - delta) * SCALE).astype(BF)
            query_grad = dot(score_grad, keys)
            att_ref[slot, doc] = gather_heads(output).astype(BF)
            qg_ref[slot, doc] = gather_heads(query_grad).astype(BF)
            key_grad = dot(score_grad, query, TN).astype(BF)
            value_grad = dot(low, cot, TN).astype(BF)
            for at in range(4):
                first = lax.bitwise_xor(s, at) * 128 + doc * 64
                to = pl.ds(pl.multiple_of(first, 64), 64)
                grad_s[core, to, 0:256] = key_grad[at * 64 : at * 64 + 64]
                grad_s[core, to, 256:512] = value_grad[at * 64 : at * 64 + 64]

    for copy in later:
        copy.wait()
    cores = [core_ref.at[k] for k in range(4)]
    owns = [own_ref.at[k] for k in range(4)]
    for flip, outs in (
        (2, (a10.at[1], a10.at[0], a2, a3)),
        (3, (b0, b1, b2, b3)),
        (1, cores),
        (0, owns),
    ):
        block = lax.bitwise_xor(h, flip)
        for n in range(4):
            at = pl.ds(pl.multiple_of(block * 1024 + n * 256, 256), 256)
            total = dot(grad_s[0], w_s[0, at, :], NT) + dot(grad_s[1], w_s[1, at, :], NT)
            for k in range(4):
                for doc in range(2):
                    first = k * 128 + doc * 64
                    outs[k][doc, :, n * 256 : n * 256 + 256] = total[first : first + 64].astype(
                        outs[k].dtype
                    )


def main_call(lengths, arrays):
    here = pl.BlockSpec(memory_space=pl.ANY)
    vmem = pl.BlockSpec(memory_space=pltpu.VMEM)
    smem = pl.BlockSpec(memory_space=pltpu.SMEM)
    piece = jax.ShapeDtypeStruct((2, 64, 1024), BF)
    front = jax.ShapeDtypeStruct((2, 2, 64, 256), BF)
    return pl.pallas_call(
        main_kernel,
        out_shape=[
            front,
            front,
            jax.ShapeDtypeStruct((4, 2, 64, 1024), F32),
        ]
        + [piece] * 5
        + [jax.ShapeDtypeStruct((2, 2, 64, 1024), BF)]
        + [piece]
        + [jax.ShapeDtypeStruct((4, 2, 64, 1024), BF)],
        in_specs=[smem] + [vmem] * 2 + [here] * (len(arrays) - 2),
        out_specs=[vmem] * 11,
        scratch_shapes=[
            pltpu.VMEM((2, 4096, 512), BF),
            pltpu.VMEM((2, 4, 64, 512), BF),
            pltpu.VMEM((2, 512, 512), BF),
            pltpu.SemaphoreType.DMA((26,)),
        ],
        compiler_params=pltpu.CompilerParams(vmem_limit_bytes=34 * 1024 * 1024),
        cost_estimate=pl.CostEstimate(
            flops=6 * 10**9, bytes_accessed=24 * 2**20, transcendentals=2**18
        ),
        name="attend",
    )(lengths, *arrays)


def final_kernel(own, core, near, far, near1, near2, far1, far2, out_ref):
    c = lax.rem(lax.axis_index("head"), 2)
    for i in range(2):
        mine = (own[0, i] + near[1, i].astype(F32)) + (near1[i].astype(F32) + near2[i].astype(F32))
        theirs = (core[0, i].astype(F32) + far[i].astype(F32)) + (
            far1[i].astype(F32) + far2[i].astype(F32)
        )
        out_ref[2 * i + c] = mine.astype(BF)
        out_ref[2 * i + 1 - c] = theirs.astype(BF)


def small_call(kernel, shape, name, *arrays):
    vmem = pl.BlockSpec(memory_space=pltpu.VMEM)
    return pl.pallas_call(
        kernel,
        out_shape=jax.ShapeDtypeStruct(shape, BF),
        in_specs=[vmem] * len(arrays),
        out_specs=vmem,
        compiler_params=pltpu.CompilerParams(vmem_limit_bytes=12 * 1024 * 1024),
        name=name,
    )(*arrays)


def together(*values):
    return lax.optimization_barrier(values)


def summed(*parts):
    total = parts[0].astype(F32)
    for part in parts[1:]:
        total = total + part.astype(F32)
    return total.astype(BF)


def body(encoder, key_weight, value_weight, tile_mask, lengths, queries, cotangent):
    h = lax.axis_index("head")
    c = lax.rem(h, 2)

    def along(value, k):
        return lax.ppermute(value, "seq", [(a, a ^ k) for a in range(SEQ)])

    def flip(value, bits):
        return lax.ppermute(value, "head", [(a, a ^ bits) for a in range(4)])

    def across(value):
        return lax.ppermute(value, "grp", [(0, 1), (1, 0)])

    e0 = lax.dynamic_index_in_dim(encoder, h, 0, keepdims=False)
    e2 = along(e0, 2)
    e1 = along(e0, 1)
    w_own, m1, m2, m3 = prune(
        tile_mask, key_weight, value_weight, queries.reshape(64, 1024), cotangent.reshape(64, 1024)
    )
    e1, e2, m2, w_own = together(e1, e2, m2, w_own)
    z2 = along(m2, 2)
    e3 = along(e2, 1)
    x1, x2 = flip(e1, 2), flip(e2, 2)
    e3, x1, x2, m1, m3 = together(e3, x1, x2, m1, m3)
    z1, z3 = along(m1, 1), along(m3, 3)
    x3 = flip(e3, 2)
    y1, y2 = across(z1), across(z2)
    x3, z3, w_own = together(x3, z3, w_own)
    y3 = across(z3)
    packed = pack_call(w_own, z1, z2, y1, y2)
    packed_there = flip(packed, 1)
    early = early_call([encoder, e1, e2, e3, x1, x2, x3, packed, packed_there])
    z3_there = flip(z3, 1)
    y3, *early = together(y3, *early)
    y3_there = flip(y3, 1)
    outs = main_call(lengths, early + [packed, z3, y3, packed_there, z3_there, y3_there])
    att, qgrad, own = outs[:3]
    a3, b3, a2, b2, b1, a10, b0, to_core = outs[3:]
    from_core = flip(to_core, 1)
    front = jnp.stack([att, qgrad], axis=1)
    other = flip(front[1], 1)
    b3, a3 = flip(b3, 3), flip(a3, 2)
    b3, core, other, b2, a2 = together(b3, from_core, other, b2, a2)
    b2, a2 = flip(b2, 3), flip(a2, 2)
    far3, own = together(summed(core[3], b3), own)
    far3 = along(far3, 1)
    near3, core = together(summed(own[3], a3), core)
    near3 = along(near3, 1)
    b2, b1, a10 = together(b2, b1, a10)
    b1, a10 = flip(b1, 3), flip(a10, 2)
    far2, own = together(summed(core[2], b2, far3), own)
    far2 = along(far2, 2)
    a2, b0 = together(a2, b0)
    b0 = flip(b0, 3)
    near2, core = together(summed(own[2], a2, near3), core)
    near2 = along(near2, 2)
    back = jnp.stack([front[0], other]).reshape(2, 2, 2, SEQ, 16, 256).transpose(3, 0, 1, 2, 4, 5)
    far1, own, back = together(summed(core[1], b1), own, back)
    far1 = along(far1, 1)
    a10, near2, far2 = together(a10, near2, far2)
    near1 = along(summed(own[1], a10[0]), 1)
    from_core = core
    back = lax.all_to_all(back, "seq", split_axis=0, concat_axis=0, tiled=True)
    back = back.transpose(2, 3, 1, 4, 0, 5).reshape(2, 2, 2, 16, 1024)
    back = jnp.where(c == 0, back, back[:, :, ::-1])
    back = back.reshape(2, DOCS, 16, 1024)
    b0, back = together(b0, back)
    encoder_grad = small_call(
        final_kernel, (DOCS, 64, 1024), "final", own, from_core, a10, b0, near1, near2, far1, far2
    )
    return (back[0], back[1], encoder_grad)


def solution(mesh):
    placed = (
        P("grp", "seq", None),
        P("seq", "head"),
        P("seq", "head"),
        P(None, "seq", "head"),
        P("grp"),
        P("grp", "seq", "head"),
        P("grp", "seq", "head"),
    )

    def step(*arrays):
        plan = body if fits(mesh, arrays[0], arrays[1], arrays[5]) else general_body
        return jax.shard_map(
            plan,
            mesh=mesh,
            in_specs=placed,
            out_specs=(P("grp", "seq", "head"),) * 3,
            check_vma=False,
        )(*arrays)

    return step
```

```python
import functools

import jax
import jax.numpy as jnp
from jax import lax
from jax.experimental import pallas as pl
from jax.experimental.pallas import tpu as pltpu
from jax.sharding import PartitionSpec as P

DH = 64
TILE = 64
DOCS = 4


SCALE = 0.125
FLOOR_SCORE = -1e30

BF = jnp.bfloat16
F32 = jnp.float32


def expand(tile_grid, tile_edge):
    return jnp.repeat(jnp.repeat(tile_grid, tile_edge, axis=0), tile_edge, axis=1)


def attend(keys, values, queries, cotangent, length):
    position = jnp.arange(keys.shape[0])[None, :]
    live = position < length
    scores = jnp.dot(queries, keys.T, preferred_element_type=jnp.float32) * SCALE
    scores = jnp.where(live, scores, FLOOR_SCORE)
    row_max = jnp.max(scores, axis=1, keepdims=True)
    weights = jnp.where(live, jnp.exp(scores - row_max), 0.0)
    probs = weights / jnp.sum(weights, axis=1, keepdims=True)
    probs_low = probs.astype(jnp.bfloat16)
    output = jnp.dot(probs_low, values, preferred_element_type=jnp.float32)
    delta = jnp.sum(cotangent.astype(jnp.float32) * output, axis=1, keepdims=True)
    prob_grad = jnp.dot(cotangent, values.T, preferred_element_type=jnp.float32)
    score_grad = (probs * (prob_grad - delta) * SCALE).astype(jnp.bfloat16)
    query_grad = jnp.dot(score_grad, keys, preferred_element_type=jnp.float32)
    key_grad = jnp.dot(score_grad.T, queries, preferred_element_type=jnp.float32)
    value_grad = jnp.dot(probs_low.T, cotangent, preferred_element_type=jnp.float32)
    return (
        output.astype(jnp.bfloat16),
        query_grad.astype(jnp.bfloat16),
        key_grad.astype(jnp.bfloat16),
        value_grad.astype(jnp.bfloat16),
    )


def project(encoder, key_piece, value_piece):
    count = key_piece.shape[0]
    flat = encoder.reshape(DOCS * encoder.shape[1], count)
    key_flat = jnp.dot(flat, key_piece, preferred_element_type=jnp.float32)
    value_flat = jnp.dot(flat, value_piece, preferred_element_type=jnp.float32)
    shape_out = (DOCS, encoder.shape[1], key_piece.shape[1])
    return (key_flat.reshape(shape_out), value_flat.reshape(shape_out))


def back_product(key_rows, value_rows, key_piece, value_piece):
    contract = (((1,), (1,)), ((), ()))
    total = lax.dot_general(key_rows, key_piece, contract, preferred_element_type=jnp.float32)
    return total + lax.dot_general(
        value_rows, value_piece, contract, preferred_element_type=jnp.float32
    )


def general_body(encoder, key_weight, value_weight, tile_mask, lengths, queries, cotangent):
    seq_count = lax.axis_size("seq")
    enc_rows = encoder.shape[1]
    dec_rows = queries.shape[1]
    group_heads = queries.shape[2] // DH
    pair_count = DOCS * group_heads
    local_pairs = pair_count // seq_count
    key_masked = key_weight * expand(tile_mask[0], TILE).astype(jnp.bfloat16)
    value_masked = value_weight * expand(tile_mask[1], TILE).astype(jnp.bfloat16)
    full_key, full_value = (
        lax.all_gather(key_masked, "seq", axis=0, tiled=True),
        lax.all_gather(value_masked, "seq", axis=0, tiled=True),
    )
    key_sum, value_sum = project(encoder, full_key, full_value)

    def to_pairs(first, second, rows):
        joined = jnp.concatenate(
            [
                first.reshape(DOCS, rows, group_heads, DH),
                second.reshape(DOCS, rows, group_heads, DH),
            ],
            axis=3,
        )
        return joined.transpose(0, 2, 1, 3).reshape(pair_count, rows, 2 * DH)

    def from_pairs(block, rows):
        shaped = block.reshape(DOCS, group_heads, rows, 2 * DH).transpose(0, 2, 1, 3)
        first = shaped[..., :DH].reshape(DOCS, rows, group_heads * DH)
        second = shaped[..., DH:].reshape(DOCS, rows, group_heads * DH)
        return (first, second)

    query_pairs = to_pairs(queries, cotangent, dec_rows)
    query_owned = lax.all_to_all(query_pairs, "seq", split_axis=0, concat_axis=1, tiled=True)
    kv_pairs = to_pairs(key_sum.astype(jnp.bfloat16), value_sum.astype(jnp.bfloat16), enc_rows)
    kv_owned = lax.all_to_all(kv_pairs, "seq", split_axis=0, concat_axis=1, tiled=True)
    pair_ids = lax.axis_index("seq") * local_pairs + jnp.arange(local_pairs)
    doc_of_pair = pair_ids // group_heads
    pair_length = jnp.sum(
        jnp.where(doc_of_pair[:, None] == jnp.arange(DOCS)[None, :], lengths[None, :], 0), axis=1
    )

    def owner_pair(items):
        pair_kv, pair_query, length = items
        output, query_grad, key_grad, value_grad = attend(
            pair_kv[:, :DH], pair_kv[:, DH:], pair_query[:, :DH], pair_query[:, DH:], length
        )
        return (
            jnp.concatenate([output, query_grad], axis=1),
            jnp.concatenate([key_grad, value_grad], axis=1),
        )

    front, back = lax.map(owner_pair, (kv_owned, query_owned, pair_length))
    front_rows, back_rows = (
        lax.all_to_all(front, "seq", split_axis=1, concat_axis=0, tiled=True),
        lax.all_to_all(back, "seq", split_axis=1, concat_axis=0, tiled=True),
    )
    attention, query_grad = from_pairs(front_rows, dec_rows)
    key_grads, value_grads = from_pairs(back_rows, enc_rows)
    key_rows = key_grads.reshape(DOCS * enc_rows, group_heads * DH)
    value_rows = value_grads.reshape(DOCS * enc_rows, group_heads * DH)
    grad_terms = back_product(key_rows, value_rows, full_key, full_value)
    grad_share = lax.psum_scatter(grad_terms, "head", scatter_dimension=1, tiled=True)
    encoder_grad = grad_share.astype(jnp.bfloat16).reshape(DOCS, enc_rows, grad_share.shape[1])
    return (attention, query_grad, encoder_grad)


SEQ = 4
PIECE = 512


def fits(mesh, encoder, key_weight, queries):
    return (
        mesh.shape["seq"] == SEQ
        and mesh.shape["head"] == 4
        and mesh.shape["grp"] == 2
        and encoder.shape == (DOCS * 2, 256, 4096)
        and key_weight.shape == (4096, 4096)
        and queries.shape == (DOCS * 2, 64, 4096)
    )


def prune_kernel(mask_ref, key_ref, value_ref, query_ref, cot_ref, own_ref, *message_refs):
    s, g = lax.axis_index("seq"), lax.axis_index("grp")
    left = lax.broadcasted_iota(jnp.int32, (1, 128), 1) < TILE

    def write(out_ref, first_tile, tiles, column):
        for t in range(tiles):
            tile = first_tile + t
            row = pl.ds(pl.multiple_of(tile * TILE, TILE), TILE)
            for side, ref in ((0, key_ref), (1, value_ref)):
                for part in range(2):
                    at = pl.ds(pl.multiple_of(column * 256 + part * 128, 128), 128)
                    first = mask_ref[side, tile, column * 4 + part * 2]
                    second = mask_ref[side, tile, column * 4 + part * 2 + 1]
                    keep = jnp.where(left, first, second).astype(F32)
                    to = side * 256 + part * 128
                    out_ref[t * TILE : (t + 1) * TILE, to : to + 128] = (
                        ref[row, at].astype(F32) * keep
                    ).astype(BF)

    first, second, third = message_refs[:3]
    for k, ref in enumerate(message_refs[3:]):
        at = pl.ds(pl.multiple_of(lax.bitwise_xor(s, k) * 256, 256), 256)
        ref[:, 0:256] = query_ref[:, at]
        ref[:, 256:512] = cot_ref[:, at]
    write(second, g * 8, 8, lax.bitwise_xor(s, 2))
    write(first, g * 8, 8, lax.bitwise_xor(s, 1))
    write(third, g * 8, 8, lax.bitwise_xor(s, 3))
    write(own_ref, 0, 16, s)


def prune(tile_mask, key_weight, value_weight, queries, cotangent):
    whole = pl.BlockSpec(memory_space=pltpu.VMEM)
    shapes = [(2 * PIECE, 512)] + [(PIECE, 512)] * 3 + [(64, 512)] * 4
    return pl.pallas_call(
        prune_kernel,
        out_shape=[jax.ShapeDtypeStruct(shape, BF) for shape in shapes],
        in_specs=[pl.BlockSpec(memory_space=pltpu.SMEM)] + [whole] * 4,
        out_specs=[whole] * len(shapes),
        compiler_params=pltpu.CompilerParams(vmem_limit_bytes=12 * 1024 * 1024),
        name="prune",
    )(tile_mask, key_weight, value_weight, queries, cotangent)


NT = (((1,), (1,)), ((), ()))
TN = (((0,), (0,)), ((), ()))
NN = (((1,), (0,)), ((), ()))


def dot(a, b, dims=NN):
    return lax.dot_general(a, b, dims, preferred_element_type=F32)


class Mover:
    def __init__(self, sems):
        self.sems = sems
        self.used = 0

    def start(self, pairs):
        copies = []
        for src, dst in pairs:
            copy = pltpu.make_async_copy(src, dst, self.sems.at[self.used])
            copy.start()
            self.used += 1
            copies.append(copy)
        return copies


def piece_rows(w_s, core, at, first, count):
    return w_s.at[core, pl.ds(pl.multiple_of(at * 1024 + first, 256), count)]


PACKED = 3 * 2 * PIECE


def pack_kernel(own, z1, z2, y1, y2, q0, q1, q2, q3, out_ref, sems):
    g = lax.axis_index("grp")
    pairs = [(own, out_ref.at[0 : 2 * PIECE])]
    for k, z, y in ((1, z1, y1), (2, z2, y2)):
        for piece, side in ((z, g), (y, 1 - g)):
            first = pl.multiple_of(2 * PIECE * k + side * PIECE, PIECE)
            pairs.append((piece, out_ref.at[pl.ds(first, PIECE)]))
    for k, piece in enumerate((q0, q1, q2, q3)):
        first = PACKED + 64 * lax.bitwise_xor(lax.axis_index("seq"), k)
        pairs.append((piece, out_ref.at[pl.ds(pl.multiple_of(first, 64), 64)]))
    for copy in Mover(sems).start(pairs):
        copy.wait()


def pack_call(*arrays):
    here = pl.BlockSpec(memory_space=pl.ANY)
    return pl.pallas_call(
        pack_kernel,
        out_shape=jax.ShapeDtypeStruct((PACKED + 256, 512), BF),
        in_specs=[here] * len(arrays),
        out_specs=pl.BlockSpec(memory_space=pltpu.VMEM),
        scratch_shapes=[pltpu.SemaphoreType.DMA((9,))],
        compiler_params=pltpu.CompilerParams(vmem_limit_bytes=6 * 1024 * 1024),
        cost_estimate=pl.CostEstimate(flops=1, bytes_accessed=1, transcendentals=0),
        name="pack",
    )(*arrays)


def early_weights(w_s, c, s, mine, theirs):
    pairs = []
    for core, packed in ((c, mine), (1 - c, theirs)):
        for k in range(3):
            rows = packed.at[2 * PIECE * k : 2 * PIECE * (k + 1)]
            pairs.append((rows, piece_rows(w_s, core, lax.bitwise_xor(s, k), 0, 2 * PIECE)))
    return pairs


def early_kernel(*refs):
    enc, e1, e2, e3, x1, x2, x3 = refs[:7]
    mine, theirs = refs[7:9]
    sum_ref, last_ref, enc_s, w_s, sems = refs[9:]
    s, h = lax.axis_index("seq"), lax.axis_index("head")
    c = lax.rem(h, 2)
    x = h // 2
    mover = Mover(sems)

    def rows_of(doc, at):
        return enc_s.at[pl.ds(pl.multiple_of(doc * 256 + at * 64, 64), 64)]

    pairs = [(enc.at[2 * i + c], rows_of(i, s)) for i in range(2)]
    for k, (own, other) in enumerate(((e1, x1), (e2, x2), (e3, x3))):
        at = lax.bitwise_xor(s, k + 1)
        pairs += [(own, rows_of(x, at)), (other, rows_of(1 - x, at))]
    pairs += early_weights(w_s, c, s, mine, theirs)
    for copy in mover.start(pairs):
        copy.wait()

    def columns(k):
        at = lax.bitwise_xor(s, k)
        return pl.ds(pl.multiple_of(at * 1024, 1024), 1024)

    for core in range(2):
        for half in range(2):
            row = slice(half * 256, half * 256 + 256)
            total = dot(enc_s[row, columns(0)], w_s[core, columns(0), :])
            for k in (1, 2):
                total = total + dot(enc_s[row, columns(k)], w_s[core, columns(k), :])
            sum_ref[core, row] = total
    last_ref[...] = enc_s[:, columns(3)]


def early_call(arrays):
    here = pl.BlockSpec(memory_space=pl.ANY)
    vmem = pl.BlockSpec(memory_space=pltpu.VMEM)
    return pl.pallas_call(
        early_kernel,
        out_shape=[
            jax.ShapeDtypeStruct((2, 512, 512), F32),
            jax.ShapeDtypeStruct((512, 1024), BF),
        ],
        in_specs=[here] * len(arrays),
        out_specs=[vmem] * 2,
        scratch_shapes=[
            pltpu.VMEM((512, 4096), BF),
            pltpu.VMEM((2, 4096, 512), BF),
            pltpu.SemaphoreType.DMA((18,)),
        ],
        compiler_params=pltpu.CompilerParams(vmem_limit_bytes=28 * 1024 * 1024),
        cost_estimate=pl.CostEstimate(
            flops=1, bytes_accessed=1, transcendentals=0
        ),
        name="early",
    )(*arrays)


def main_kernel(lengths, *refs):
    early_sum, last_rows = refs[:2]
    mine, theirs = refs[2:5], refs[5:8]
    (
        att_ref, qg_ref, own_ref,
        a3, b3, a2, b2, b1, a10, b0, core_ref,
        w_s, qc_s, grad_s, sems,
    ) = refs[8:]
    s, g, h = lax.axis_index("seq"), lax.axis_index("grp"), lax.axis_index("head")
    c = lax.rem(h, 2)
    mover = Mover(sems)
    far = lax.bitwise_xor(s, 3)
    pairs = []
    for core, pieces in ((c, mine), (1 - c, theirs)):
        packed, z3, y3 = pieces
        for src, side in ((z3, g), (y3, 1 - g)):
            pairs.append((src, piece_rows(w_s, core, far, side * PIECE, PIECE)))
        for d in range(SEQ):
            pairs.append((packed.at[PACKED + 64 * d : PACKED + 64 * d + 64], qc_s.at[core, d]))
    now = mover.start(pairs)
    later = mover.start(early_weights(w_s, c, s, mine[0], theirs[0]))
    for copy in now:
        copy.wait()
    far_rows = pl.ds(pl.multiple_of(far * 1024, 1024), 1024)

    row_head = lax.broadcasted_iota(jnp.int32, (256, 256), 0) // DH
    col_head = lax.broadcasted_iota(jnp.int32, (256, 256), 1) // DH
    same = row_head == col_head
    position = lax.broadcasted_iota(jnp.int32, (256, 256), 1)

    def spread(block):
        four = jnp.concatenate([block] * 4, axis=0)
        return jnp.where(same, four, jnp.zeros_like(four))

    def gather_heads(block):
        kept = jnp.where(same, block, 0.0)
        return (kept[0:64] + kept[64:128]) + (kept[128:192] + kept[192:256])

    for core in range(2):
        slot = lax.rem(core + c, 2)
        for doc in range(2):
            row = slice(doc * 256, doc * 256 + 256)
            both = early_sum[core, row] + dot(last_rows[row], w_s[core, far_rows, :])
            keys = both[:, :256].astype(BF)
            values = both[:, 256:].astype(BF)
            at = pl.ds(pl.multiple_of((2 * doc + c) * 16, 16), 16)
            query = spread(qc_s[core, :, at, 0:256].reshape(64, 256))
            cot = spread(qc_s[core, :, at, 256:512].reshape(64, 256))
            live = position < lengths[2 * doc + c]
            scores = dot(query, keys, NT) * SCALE
            scores = jnp.where(live, scores, FLOOR_SCORE)
            row_max = jnp.max(scores, axis=1, keepdims=True)
            weights = jnp.where(live, jnp.exp(scores - row_max), 0.0)
            probs = weights / jnp.sum(weights, axis=1, keepdims=True)
            low = probs.astype(BF)
            output = dot(low, values)
            delta = jnp.sum(cot.astype(F32) * output, axis=1, keepdims=True)
            prob_grad = dot(cot, values, NT)
            score_grad = (probs * (prob_grad - delta) * SCALE).astype(BF)
            query_grad = dot(score_grad, keys)
            att_ref[slot, doc] = gather_heads(output).astype(BF)
            qg_ref[slot, doc] = gather_heads(query_grad).astype(BF)
            key_grad = dot(score_grad, query, TN).astype(BF)
            value_grad = dot(low, cot, TN).astype(BF)
            for at in range(4):
                first = lax.bitwise_xor(s, at) * 128 + doc * 64
                to = pl.ds(pl.multiple_of(first, 64), 64)
                grad_s[core, to, 0:256] = key_grad[at * 64 : at * 64 + 64]
                grad_s[core, to, 256:512] = value_grad[at * 64 : at * 64 + 64]

    for copy in later:
        copy.wait()
    cores = [core_ref.at[k] for k in range(4)]
    owns = [own_ref.at[k] for k in range(4)]
    for flip, outs in (
        (2, (a10.at[1], a10.at[0], a2, a3)),
        (3, (b0, b1, b2, b3)),
        (1, cores),
        (0, owns),
    ):
        block = lax.bitwise_xor(h, flip)
        for n in range(4):
            at = pl.ds(pl.multiple_of(block * 1024 + n * 256, 256), 256)
            total = dot(grad_s[0], w_s[0, at, :], NT) + dot(grad_s[1], w_s[1, at, :], NT)
            for k in range(4):
                for doc in range(2):
                    first = k * 128 + doc * 64
                    outs[k][doc, :, n * 256 : n * 256 + 256] = total[first : first + 64].astype(
                        outs[k].dtype
                    )


def main_call(lengths, arrays):
    here = pl.BlockSpec(memory_space=pl.ANY)
    vmem = pl.BlockSpec(memory_space=pltpu.VMEM)
    smem = pl.BlockSpec(memory_space=pltpu.SMEM)
    piece = jax.ShapeDtypeStruct((2, 64, 1024), BF)
    front = jax.ShapeDtypeStruct((2, 2, 64, 256), BF)
    return pl.pallas_call(
        main_kernel,
        out_shape=[
            front,
            front,
            jax.ShapeDtypeStruct((4, 2, 64, 1024), F32),
        ]
        + [piece] * 5
        + [jax.ShapeDtypeStruct((2, 2, 64, 1024), BF)]
        + [piece]
        + [jax.ShapeDtypeStruct((4, 2, 64, 1024), BF)],
        in_specs=[smem] + [vmem] * 2 + [here] * (len(arrays) - 2),
        out_specs=[vmem] * 11,
        scratch_shapes=[
            pltpu.VMEM((2, 4096, 512), BF),
            pltpu.VMEM((2, 4, 64, 512), BF),
            pltpu.VMEM((2, 512, 512), BF),
            pltpu.SemaphoreType.DMA((26,)),
        ],
        compiler_params=pltpu.CompilerParams(vmem_limit_bytes=34 * 1024 * 1024),
        cost_estimate=pl.CostEstimate(
            flops=6 * 10**9, bytes_accessed=24 * 2**20, transcendentals=2**18
        ),
        name="attend",
    )(lengths, *arrays)


def final_kernel(own, core, near, far, near1, near2, far1, far2, out_ref):
    c = lax.rem(lax.axis_index("head"), 2)
    for i in range(2):
        mine = (own[0, i] + near[1, i].astype(F32)) + (near1[i].astype(F32) + near2[i].astype(F32))
        theirs = (core[0, i].astype(F32) + far[i].astype(F32)) + (
            far1[i].astype(F32) + far2[i].astype(F32)
        )
        out_ref[2 * i + c] = mine.astype(BF)
        out_ref[2 * i + 1 - c] = theirs.astype(BF)


def small_call(kernel, shape, name, *arrays):
    vmem = pl.BlockSpec(memory_space=pltpu.VMEM)
    return pl.pallas_call(
        kernel,
        out_shape=jax.ShapeDtypeStruct(shape, BF),
        in_specs=[vmem] * len(arrays),
        out_specs=vmem,
        compiler_params=pltpu.CompilerParams(vmem_limit_bytes=12 * 1024 * 1024),
        name=name,
    )(*arrays)


def together(*values):
    return lax.optimization_barrier(values)


def summed(*parts):
    total = parts[0].astype(F32)
    for part in parts[1:]:
        total = total + part.astype(F32)
    return total.astype(BF)


def body(encoder, key_weight, value_weight, tile_mask, lengths, queries, cotangent):
    h = lax.axis_index("head")
    c = lax.rem(h, 2)

    def along(value, k):
        return lax.ppermute(value, "seq", [(a, a ^ k) for a in range(SEQ)])

    def flip(value, bits):
        return lax.ppermute(value, "head", [(a, a ^ bits) for a in range(4)])

    def across(value):
        return lax.ppermute(value, "grp", [(0, 1), (1, 0)])

    e0 = lax.dynamic_index_in_dim(encoder, h, 0, keepdims=False)
    e2 = along(e0, 2)
    e1 = along(e0, 1)
    w_own, m1, m2, m3, q0, q1, q2, q3 = prune(
        tile_mask, key_weight, value_weight, queries.reshape(64, 1024), cotangent.reshape(64, 1024)
    )
    q1, q2, q3 = along(q1, 1), along(q2, 2), along(q3, 3)
    e1, e2, m1, m2, q1, q2, q3 = together(e1, e2, m1, m2, q1, q2, q3)
    z2, z1 = along(m2, 2), along(m1, 1)
    e3 = along(e2, 1)
    x1, x2 = flip(e1, 2), flip(e2, 2)
    x1, x2, m3 = together(x1, x2, m3)
    z3 = along(m3, 3)
    x1, z2 = together(x1, z2)
    x2, e3 = together(x2, e3)
    y2 = across(z2)
    x3 = flip(e3, 2)
    y1 = across(z1)
    z3, x3, w_own = together(z3, x3, w_own)
    y3 = across(z3)
    packed = pack_call(w_own, z1, z2, y1, y2, q0, q1, q2, q3)
    packed_there = flip(packed, 1)
    early = early_call([encoder, e1, e2, e3, x1, x2, x3, packed, packed_there])
    z3_there = flip(z3, 1)
    y3, *early = together(y3, *early)
    y3_there = flip(y3, 1)
    outs = main_call(lengths, early + [packed, z3, y3, packed_there, z3_there, y3_there])
    att, qgrad, own = outs[:3]
    a3, b3, a2, b2, b1, a10, b0, to_core = outs[3:]
    from_core = flip(to_core, 1)
    front = jnp.stack([att, qgrad], axis=1)
    other = flip(front[1], 1)
    b3, a3 = flip(b3, 3), flip(a3, 2)
    b3, core, other, b2, a2 = together(b3, from_core, other, b2, a2)
    b2, a2 = flip(b2, 3), flip(a2, 2)
    far3, own = together(summed(core[3], b3), own)
    far3 = along(far3, 1)
    near3, core = together(summed(own[3], a3), core)
    near3 = along(near3, 1)
    b2, b1, a10 = together(b2, b1, a10)
    b1, a10 = flip(b1, 3), flip(a10, 2)
    far2, own = together(summed(core[2], b2, far3), own)
    far2 = along(far2, 2)
    a2, b0 = together(a2, b0)
    b0 = flip(b0, 3)
    near2, core = together(summed(own[2], a2, near3), core)
    near2 = along(near2, 2)
    back = jnp.stack([front[0], other]).reshape(2, 2, 2, SEQ, 16, 256).transpose(3, 0, 1, 2, 4, 5)
    far1, own, back = together(summed(core[1], b1), own, back)
    far1 = along(far1, 1)
    a10, near2, far2 = together(a10, near2, far2)
    near1 = along(summed(own[1], a10[0]), 1)
    from_core = core
    back = lax.all_to_all(back, "seq", split_axis=0, concat_axis=0, tiled=True)
    back = back.transpose(2, 3, 1, 4, 0, 5).reshape(2, 2, 2, 16, 1024)
    back = jnp.where(c == 0, back, back[:, :, ::-1])
    back = back.reshape(2, DOCS, 16, 1024)
    b0, back = together(b0, back)
    encoder_grad = small_call(
        final_kernel, (DOCS, 64, 1024), "final", own, from_core, a10, b0, near1, near2, far1, far2
    )
    return (back[0], back[1], encoder_grad)


def solution(mesh):
    placed = (
        P("grp", "seq", None),
        P("seq", "head"),
        P("seq", "head"),
        P(None, "seq", "head"),
        P("grp"),
        P("grp", "seq", "head"),
        P("grp", "seq", "head"),
    )

    def step(*arrays):
        plan = body if fits(mesh, arrays[0], arrays[1], arrays[5]) else general_body
        return jax.shard_map(
            plan,
            mesh=mesh,
            in_specs=placed,
            out_specs=(P("grp", "seq", "head"),) * 3,
            check_vma=False,
        )(*arrays)

    return step
```

```python
import functools

import jax
import jax.numpy as jnp
from jax import lax
from jax.experimental import pallas as pl
from jax.experimental.pallas import tpu as pltpu
from jax.sharding import PartitionSpec as P

DH = 64
TILE = 64
DOCS = 4


SCALE = 0.125
FLOOR_SCORE = -1e30

BF = jnp.bfloat16
F32 = jnp.float32


def expand(tile_grid, tile_edge):
    return jnp.repeat(jnp.repeat(tile_grid, tile_edge, axis=0), tile_edge, axis=1)


def attend(keys, values, queries, cotangent, length):
    position = jnp.arange(keys.shape[0])[None, :]
    live = position < length
    scores = jnp.dot(queries, keys.T, preferred_element_type=jnp.float32) * SCALE
    scores = jnp.where(live, scores, FLOOR_SCORE)
    row_max = jnp.max(scores, axis=1, keepdims=True)
    weights = jnp.where(live, jnp.exp(scores - row_max), 0.0)
    probs = weights / jnp.sum(weights, axis=1, keepdims=True)
    probs_low = probs.astype(jnp.bfloat16)
    output = jnp.dot(probs_low, values, preferred_element_type=jnp.float32)
    delta = jnp.sum(cotangent.astype(jnp.float32) * output, axis=1, keepdims=True)
    prob_grad = jnp.dot(cotangent, values.T, preferred_element_type=jnp.float32)
    score_grad = (probs * (prob_grad - delta) * SCALE).astype(jnp.bfloat16)
    query_grad = jnp.dot(score_grad, keys, preferred_element_type=jnp.float32)
    key_grad = jnp.dot(score_grad.T, queries, preferred_element_type=jnp.float32)
    value_grad = jnp.dot(probs_low.T, cotangent, preferred_element_type=jnp.float32)
    return (
        output.astype(jnp.bfloat16),
        query_grad.astype(jnp.bfloat16),
        key_grad.astype(jnp.bfloat16),
        value_grad.astype(jnp.bfloat16),
    )


def project(encoder, key_piece, value_piece):
    count = key_piece.shape[0]
    flat = encoder.reshape(DOCS * encoder.shape[1], count)
    key_flat = jnp.dot(flat, key_piece, preferred_element_type=jnp.float32)
    value_flat = jnp.dot(flat, value_piece, preferred_element_type=jnp.float32)
    shape_out = (DOCS, encoder.shape[1], key_piece.shape[1])
    return (key_flat.reshape(shape_out), value_flat.reshape(shape_out))


def back_product(key_rows, value_rows, key_piece, value_piece):
    contract = (((1,), (1,)), ((), ()))
    total = lax.dot_general(key_rows, key_piece, contract, preferred_element_type=jnp.float32)
    return total + lax.dot_general(
        value_rows, value_piece, contract, preferred_element_type=jnp.float32
    )


def general_body(encoder, key_weight, value_weight, tile_mask, lengths, queries, cotangent):
    seq_count = lax.axis_size("seq")
    enc_rows = encoder.shape[1]
    dec_rows = queries.shape[1]
    group_heads = queries.shape[2] // DH
    pair_count = DOCS * group_heads
    local_pairs = pair_count // seq_count
    key_masked = key_weight * expand(tile_mask[0], TILE).astype(jnp.bfloat16)
    value_masked = value_weight * expand(tile_mask[1], TILE).astype(jnp.bfloat16)
    full_key, full_value = (
        lax.all_gather(key_masked, "seq", axis=0, tiled=True),
        lax.all_gather(value_masked, "seq", axis=0, tiled=True),
    )
    key_sum, value_sum = project(encoder, full_key, full_value)

    def to_pairs(first, second, rows):
        joined = jnp.concatenate(
            [
                first.reshape(DOCS, rows, group_heads, DH),
                second.reshape(DOCS, rows, group_heads, DH),
            ],
            axis=3,
        )
        return joined.transpose(0, 2, 1, 3).reshape(pair_count, rows, 2 * DH)

    def from_pairs(block, rows):
        shaped = block.reshape(DOCS, group_heads, rows, 2 * DH).transpose(0, 2, 1, 3)
        first = shaped[..., :DH].reshape(DOCS, rows, group_heads * DH)
        second = shaped[..., DH:].reshape(DOCS, rows, group_heads * DH)
        return (first, second)

    query_pairs = to_pairs(queries, cotangent, dec_rows)
    query_owned = lax.all_to_all(query_pairs, "seq", split_axis=0, concat_axis=1, tiled=True)
    kv_pairs = to_pairs(key_sum.astype(jnp.bfloat16), value_sum.astype(jnp.bfloat16), enc_rows)
    kv_owned = lax.all_to_all(kv_pairs, "seq", split_axis=0, concat_axis=1, tiled=True)
    pair_ids = lax.axis_index("seq") * local_pairs + jnp.arange(local_pairs)
    doc_of_pair = pair_ids // group_heads
    pair_length = jnp.sum(
        jnp.where(doc_of_pair[:, None] == jnp.arange(DOCS)[None, :], lengths[None, :], 0), axis=1
    )

    def owner_pair(items):
        pair_kv, pair_query, length = items
        output, query_grad, key_grad, value_grad = attend(
            pair_kv[:, :DH], pair_kv[:, DH:], pair_query[:, :DH], pair_query[:, DH:], length
        )
        return (
            jnp.concatenate([output, query_grad], axis=1),
            jnp.concatenate([key_grad, value_grad], axis=1),
        )

    front, back = lax.map(owner_pair, (kv_owned, query_owned, pair_length))
    front_rows, back_rows = (
        lax.all_to_all(front, "seq", split_axis=1, concat_axis=0, tiled=True),
        lax.all_to_all(back, "seq", split_axis=1, concat_axis=0, tiled=True),
    )
    attention, query_grad = from_pairs(front_rows, dec_rows)
    key_grads, value_grads = from_pairs(back_rows, enc_rows)
    key_rows = key_grads.reshape(DOCS * enc_rows, group_heads * DH)
    value_rows = value_grads.reshape(DOCS * enc_rows, group_heads * DH)
    grad_terms = back_product(key_rows, value_rows, full_key, full_value)
    grad_share = lax.psum_scatter(grad_terms, "head", scatter_dimension=1, tiled=True)
    encoder_grad = grad_share.astype(jnp.bfloat16).reshape(DOCS, enc_rows, grad_share.shape[1])
    return (attention, query_grad, encoder_grad)


SEQ = 4
PIECE = 512


def fits(mesh, encoder, key_weight, queries):
    return (
        mesh.shape["seq"] == SEQ
        and mesh.shape["head"] == 4
        and mesh.shape["grp"] == 2
        and encoder.shape == (DOCS * 2, 256, 4096)
        and key_weight.shape == (4096, 4096)
        and queries.shape == (DOCS * 2, 64, 4096)
    )


def prune_kernel(mask_ref, key_ref, value_ref, query_ref, cot_ref, own_ref, *message_refs):
    s, g = lax.axis_index("seq"), lax.axis_index("grp")
    left = lax.broadcasted_iota(jnp.int32, (1, 128), 1) < TILE

    def write(out_ref, first_tile, tiles, column):
        for t in range(tiles):
            tile = first_tile + t
            row = pl.ds(pl.multiple_of(tile * TILE, TILE), TILE)
            for side, ref in ((0, key_ref), (1, value_ref)):
                for part in range(2):
                    at = pl.ds(pl.multiple_of(column * 256 + part * 128, 128), 128)
                    first = mask_ref[side, tile, column * 4 + part * 2]
                    second = mask_ref[side, tile, column * 4 + part * 2 + 1]
                    keep = jnp.where(left, first, second).astype(F32)
                    to = side * 256 + part * 128
                    out_ref[t * TILE : (t + 1) * TILE, to : to + 128] = (
                        ref[row, at].astype(F32) * keep
                    ).astype(BF)

    first, second, third = message_refs[:3]
    for k, ref in enumerate(message_refs[3:]):
        at = pl.ds(pl.multiple_of(lax.bitwise_xor(s, k) * 256, 256), 256)
        ref[:, 0:256] = query_ref[:, at]
        ref[:, 256:512] = cot_ref[:, at]
    write(second, g * 8, 8, lax.bitwise_xor(s, 2))
    write(first, g * 8, 8, lax.bitwise_xor(s, 1))
    write(third, g * 8, 8, lax.bitwise_xor(s, 3))
    write(own_ref, 0, 16, s)


def prune(tile_mask, key_weight, value_weight, queries, cotangent):
    whole = pl.BlockSpec(memory_space=pltpu.VMEM)
    shapes = [(2 * PIECE, 512)] + [(PIECE, 512)] * 3 + [(64, 512)] * 4
    return pl.pallas_call(
        prune_kernel,
        out_shape=[jax.ShapeDtypeStruct(shape, BF) for shape in shapes],
        in_specs=[pl.BlockSpec(memory_space=pltpu.SMEM)] + [whole] * 4,
        out_specs=[whole] * len(shapes),
        compiler_params=pltpu.CompilerParams(vmem_limit_bytes=12 * 1024 * 1024),
        name="prune",
    )(tile_mask, key_weight, value_weight, queries, cotangent)


NT = (((1,), (1,)), ((), ()))
TN = (((0,), (0,)), ((), ()))
NN = (((1,), (0,)), ((), ()))


def dot(a, b, dims=NN):
    return lax.dot_general(a, b, dims, preferred_element_type=F32)


class Mover:
    def __init__(self, sems):
        self.sems = sems
        self.used = 0

    def start(self, pairs):
        copies = []
        for src, dst in pairs:
            copy = pltpu.make_async_copy(src, dst, self.sems.at[self.used])
            copy.start()
            self.used += 1
            copies.append(copy)
        return copies


def piece_rows(w_s, core, at, first, count):
    return w_s.at[core, pl.ds(pl.multiple_of(at * 1024 + first, 256), count)]


PACKED = 3 * 2 * PIECE


def pack_kernel(own, z1, z2, y1, y2, q0, q1, q2, q3, out_ref, sems):
    g = lax.axis_index("grp")
    pairs = [(own, out_ref.at[0 : 2 * PIECE])]
    for k, z, y in ((1, z1, y1), (2, z2, y2)):
        for piece, side in ((z, g), (y, 1 - g)):
            first = pl.multiple_of(2 * PIECE * k + side * PIECE, PIECE)
            pairs.append((piece, out_ref.at[pl.ds(first, PIECE)]))
    for k, piece in enumerate((q0, q1, q2, q3)):
        first = PACKED + 64 * lax.bitwise_xor(lax.axis_index("seq"), k)
        pairs.append((piece, out_ref.at[pl.ds(pl.multiple_of(first, 64), 64)]))
    for copy in Mover(sems).start(pairs):
        copy.wait()


def pack_call(*arrays):
    here = pl.BlockSpec(memory_space=pl.ANY)
    return pl.pallas_call(
        pack_kernel,
        out_shape=jax.ShapeDtypeStruct((PACKED + 256, 512), BF),
        in_specs=[here] * len(arrays),
        out_specs=pl.BlockSpec(memory_space=pltpu.VMEM),
        scratch_shapes=[pltpu.SemaphoreType.DMA((9,))],
        compiler_params=pltpu.CompilerParams(vmem_limit_bytes=6 * 1024 * 1024),
        cost_estimate=pl.CostEstimate(flops=1, bytes_accessed=1, transcendentals=0),
        name="pack",
    )(*arrays)


def early_weights(w_s, c, s, mine, theirs):
    pairs = []
    for core, packed in ((c, mine), (1 - c, theirs)):
        for k in range(3):
            rows = packed.at[2 * PIECE * k : 2 * PIECE * (k + 1)]
            pairs.append((rows, piece_rows(w_s, core, lax.bitwise_xor(s, k), 0, 2 * PIECE)))
    return pairs


def early_kernel(*refs):
    enc, e1, e2, e3, x1, x2, x3 = refs[:7]
    mine, theirs = refs[7:9]
    sum_ref, last_ref, enc_s, w_s, sems = refs[9:]
    s, h = lax.axis_index("seq"), lax.axis_index("head")
    c = lax.rem(h, 2)
    x = h // 2
    mover = Mover(sems)

    def rows_of(doc, at):
        return enc_s.at[pl.ds(pl.multiple_of(doc * 256 + at * 64, 64), 64)]

    pairs = [(enc.at[2 * i + c], rows_of(i, s)) for i in range(2)]
    for k, (own, other) in enumerate(((e1, x1), (e2, x2), (e3, x3))):
        at = lax.bitwise_xor(s, k + 1)
        pairs += [(own, rows_of(x, at)), (other, rows_of(1 - x, at))]
    pairs += early_weights(w_s, c, s, mine, theirs)
    for copy in mover.start(pairs):
        copy.wait()

    def columns(k):
        at = lax.bitwise_xor(s, k)
        return pl.ds(pl.multiple_of(at * 1024, 1024), 1024)

    for core in range(2):
        for half in range(2):
            row = slice(half * 256, half * 256 + 256)
            total = dot(enc_s[row, columns(0)], w_s[core, columns(0), :])
            for k in (1, 2):
                total = total + dot(enc_s[row, columns(k)], w_s[core, columns(k), :])
            sum_ref[core, row] = total
    last_ref[...] = enc_s[:, columns(3)]


def early_call(arrays):
    here = pl.BlockSpec(memory_space=pl.ANY)
    vmem = pl.BlockSpec(memory_space=pltpu.VMEM)
    return pl.pallas_call(
        early_kernel,
        out_shape=[
            jax.ShapeDtypeStruct((2, 512, 512), F32),
            jax.ShapeDtypeStruct((512, 1024), BF),
        ],
        in_specs=[here] * len(arrays),
        out_specs=[vmem] * 2,
        scratch_shapes=[
            pltpu.VMEM((512, 4096), BF),
            pltpu.VMEM((2, 4096, 512), BF),
            pltpu.SemaphoreType.DMA((18,)),
        ],
        compiler_params=pltpu.CompilerParams(vmem_limit_bytes=28 * 1024 * 1024),
        cost_estimate=pl.CostEstimate(
            flops=1, bytes_accessed=1, transcendentals=0
        ),
        name="early",
    )(*arrays)


def main_kernel(lengths, *refs):
    early_sum, last_rows = refs[:2]
    mine, theirs = refs[2:5], refs[5:8]
    (
        att_ref, qg_ref, own_ref,
        a3, b3, a2, b2, b10, a10, core_ref,
        w_s, qc_s, grad_s, sems,
    ) = refs[8:]
    s, g, h = lax.axis_index("seq"), lax.axis_index("grp"), lax.axis_index("head")
    c = lax.rem(h, 2)
    mover = Mover(sems)
    far = lax.bitwise_xor(s, 3)
    pairs = []
    for core, pieces in ((c, mine), (1 - c, theirs)):
        packed, z3, y3 = pieces
        for src, side in ((z3, g), (y3, 1 - g)):
            pairs.append((src, piece_rows(w_s, core, far, side * PIECE, PIECE)))
        for d in range(SEQ):
            pairs.append((packed.at[PACKED + 64 * d : PACKED + 64 * d + 64], qc_s.at[core, d]))
    now = mover.start(pairs)
    later = mover.start(early_weights(w_s, c, s, mine[0], theirs[0]))
    for copy in now:
        copy.wait()
    far_rows = pl.ds(pl.multiple_of(far * 1024, 1024), 1024)

    row_head = lax.broadcasted_iota(jnp.int32, (256, 256), 0) // DH
    col_head = lax.broadcasted_iota(jnp.int32, (256, 256), 1) // DH
    same = row_head == col_head
    position = lax.broadcasted_iota(jnp.int32, (256, 256), 1)

    def spread(block):
        four = jnp.concatenate([block] * 4, axis=0)
        return jnp.where(same, four, jnp.zeros_like(four))

    def gather_heads(block):
        kept = jnp.where(same, block, 0.0)
        return (kept[0:64] + kept[64:128]) + (kept[128:192] + kept[192:256])

    for core in range(2):
        slot = lax.rem(core + c, 2)
        for doc in range(2):
            row = slice(doc * 256, doc * 256 + 256)
            both = early_sum[core, row] + dot(last_rows[row], w_s[core, far_rows, :])
            keys = both[:, :256].astype(BF)
            values = both[:, 256:].astype(BF)
            at = pl.ds(pl.multiple_of((2 * doc + c) * 16, 16), 16)
            query = spread(qc_s[core, :, at, 0:256].reshape(64, 256))
            cot = spread(qc_s[core, :, at, 256:512].reshape(64, 256))
            live = position < lengths[2 * doc + c]
            scores = dot(query, keys, NT) * SCALE
            scores = jnp.where(live, scores, FLOOR_SCORE)
            row_max = jnp.max(scores, axis=1, keepdims=True)
            weights = jnp.where(live, jnp.exp(scores - row_max), 0.0)
            probs = weights / jnp.sum(weights, axis=1, keepdims=True)
            low = probs.astype(BF)
            output = dot(low, values)
            delta = jnp.sum(cot.astype(F32) * output, axis=1, keepdims=True)
            prob_grad = dot(cot, values, NT)
            score_grad = (probs * (prob_grad - delta) * SCALE).astype(BF)
            query_grad = dot(score_grad, keys)
            att_ref[slot, doc] = gather_heads(output).astype(BF)
            qg_ref[slot, doc] = gather_heads(query_grad).astype(BF)
            key_grad = dot(score_grad, query, TN).astype(BF)
            value_grad = dot(low, cot, TN).astype(BF)
            for at in range(4):
                first = lax.bitwise_xor(s, at) * 128 + doc * 64
                to = pl.ds(pl.multiple_of(first, 64), 64)
                grad_s[core, to, 0:256] = key_grad[at * 64 : at * 64 + 64]
                grad_s[core, to, 256:512] = value_grad[at * 64 : at * 64 + 64]

    for copy in later:
        copy.wait()
    cores = [core_ref.at[k] for k in range(4)]
    owns = [own_ref.at[k] for k in range(4)]
    for flip, outs in (
        (2, (a10.at[1], a10.at[0], a2, a3)),
        (3, (b10.at[1], b10.at[0], b2, b3)),
        (1, cores),
        (0, owns),
    ):
        block = lax.bitwise_xor(h, flip)
        for n in range(4):
            at = pl.ds(pl.multiple_of(block * 1024 + n * 256, 256), 256)
            total = dot(grad_s[0], w_s[0, at, :], NT) + dot(grad_s[1], w_s[1, at, :], NT)
            for k in range(4):
                for doc in range(2):
                    first = k * 128 + doc * 64
                    outs[k][doc, :, n * 256 : n * 256 + 256] = total[first : first + 64].astype(
                        outs[k].dtype
                    )


def main_call(lengths, arrays):
    here = pl.BlockSpec(memory_space=pl.ANY)
    vmem = pl.BlockSpec(memory_space=pltpu.VMEM)
    smem = pl.BlockSpec(memory_space=pltpu.SMEM)
    piece = jax.ShapeDtypeStruct((2, 64, 1024), BF)
    front = jax.ShapeDtypeStruct((2, 2, 64, 256), BF)
    return pl.pallas_call(
        main_kernel,
        out_shape=[
            front,
            front,
            jax.ShapeDtypeStruct((4, 2, 64, 1024), F32),
        ]
        + [piece] * 4
        + [jax.ShapeDtypeStruct((2, 2, 64, 1024), BF)] * 2
        + [jax.ShapeDtypeStruct((4, 2, 64, 1024), BF)],
        in_specs=[smem] + [vmem] * 2 + [here] * (len(arrays) - 2),
        out_specs=[vmem] * 10,
        scratch_shapes=[
            pltpu.VMEM((2, 4096, 512), BF),
            pltpu.VMEM((2, 4, 64, 512), BF),
            pltpu.VMEM((2, 512, 512), BF),
            pltpu.SemaphoreType.DMA((26,)),
        ],
        compiler_params=pltpu.CompilerParams(vmem_limit_bytes=34 * 1024 * 1024),
        cost_estimate=pl.CostEstimate(
            flops=6 * 10**9, bytes_accessed=24 * 2**20, transcendentals=2**18
        ),
        name="attend",
    )(lengths, *arrays)


def final_kernel(own, core, near, far, near1, near2, far1, far2, out_ref):
    c = lax.rem(lax.axis_index("head"), 2)
    for i in range(2):
        mine = (own[0, i] + near[1, i].astype(F32)) + (near1[i].astype(F32) + near2[i].astype(F32))
        theirs = (core[0, i].astype(F32) + far[1, i].astype(F32)) + (
            far1[i].astype(F32) + far2[i].astype(F32)
        )
        out_ref[2 * i + c] = mine.astype(BF)
        out_ref[2 * i + 1 - c] = theirs.astype(BF)


def small_call(kernel, shape, name, *arrays):
    vmem = pl.BlockSpec(memory_space=pltpu.VMEM)
    return pl.pallas_call(
        kernel,
        out_shape=jax.ShapeDtypeStruct(shape, BF),
        in_specs=[vmem] * len(arrays),
        out_specs=vmem,
        compiler_params=pltpu.CompilerParams(vmem_limit_bytes=12 * 1024 * 1024),
        name=name,
    )(*arrays)


def together(*values):
    return lax.optimization_barrier(values)


def summed(*parts):
    total = parts[0].astype(F32)
    for part in parts[1:]:
        total = total + part.astype(F32)
    return total.astype(BF)


def body(encoder, key_weight, value_weight, tile_mask, lengths, queries, cotangent):
    h = lax.axis_index("head")
    c = lax.rem(h, 2)

    def along(value, k):
        return lax.ppermute(value, "seq", [(a, a ^ k) for a in range(SEQ)])

    def flip(value, bits):
        return lax.ppermute(value, "head", [(a, a ^ bits) for a in range(4)])

    def across(value):
        return lax.ppermute(value, "grp", [(0, 1), (1, 0)])

    e0 = lax.dynamic_index_in_dim(encoder, h, 0, keepdims=False)
    e2 = along(e0, 2)
    e1 = along(e0, 1)
    w_own, m1, m2, m3, q0, q1, q2, q3 = prune(
        tile_mask, key_weight, value_weight, queries.reshape(64, 1024), cotangent.reshape(64, 1024)
    )
    q1, q2, q3 = along(q1, 1), along(q2, 2), along(q3, 3)
    e1, e2, m1, m2, q1, q2, q3 = together(e1, e2, m1, m2, q1, q2, q3)
    z2, z1 = along(m2, 2), along(m1, 1)
    e3 = along(e2, 1)
    x1, x2 = flip(e1, 2), flip(e2, 2)
    x1, x2, m3 = together(x1, x2, m3)
    z3 = along(m3, 3)
    x1, z2 = together(x1, z2)
    x2, e3 = together(x2, e3)
    y2 = across(z2)
    x3 = flip(e3, 2)
    y2, z1 = together(y2, z1)
    y1 = across(z1)
    z3, x3, w_own = together(z3, x3, w_own)
    y3 = across(z3)
    packed = pack_call(w_own, z1, z2, y1, y2, q0, q1, q2, q3)
    packed_there = flip(packed, 1)
    early = early_call([encoder, e1, e2, e3, x1, x2, x3, packed, packed_there])
    z3_there = flip(z3, 1)
    y3, *early = together(y3, *early)
    y3_there = flip(y3, 1)
    outs = main_call(lengths, early + [packed, z3, y3, packed_there, z3_there, y3_there])
    att, qgrad, own = outs[:3]
    a3, b3, a2, b2, b10, a10, to_core = outs[3:]
    from_core = flip(to_core, 1)
    front = jnp.stack([att, qgrad], axis=1)
    other = flip(front[1], 1)
    b3, a3 = flip(b3, 3), flip(a3, 2)
    b3, core, other, b2, a2 = together(b3, from_core, other, b2, a2)
    b2, a2 = flip(b2, 3), flip(a2, 2)
    far3, own = together(summed(core[3], b3), own)
    far3 = along(far3, 1)
    near3, core = together(summed(own[3], a3), core)
    near3 = along(near3, 1)
    b2, b10, a10 = together(b2, b10, a10)
    b10, a10 = flip(b10, 3), flip(a10, 2)
    far2, own = together(summed(core[2], b2, far3), own)
    far2 = along(far2, 2)
    near2, core = together(summed(own[2], a2, near3), core)
    near2 = along(near2, 2)
    back = jnp.stack([front[0], other]).reshape(2, 2, 2, SEQ, 16, 256).transpose(3, 0, 1, 2, 4, 5)
    near1, core, back = together(summed(own[1], a10[0]), core, back)
    near1 = along(near1, 1)
    b10, near2, far2 = together(b10, near2, far2)
    far1 = along(summed(core[1], b10[0]), 1)
    from_core = core
    back = lax.all_to_all(back, "seq", split_axis=0, concat_axis=0, tiled=True)
    back = back.transpose(2, 3, 1, 4, 0, 5).reshape(2, 2, 2, 16, 1024)
    back = jnp.where(c == 0, back, back[:, :, ::-1])
    back = back.reshape(2, DOCS, 16, 1024)
    a10, back = together(a10, back)
    encoder_grad = small_call(
        final_kernel, (DOCS, 64, 1024), "final", own, from_core, a10, b10, near1, near2, far1, far2
    )
    return (back[0], back[1], encoder_grad)


def solution(mesh):
    placed = (
        P("grp", "seq", None),
        P("seq", "head"),
        P("seq", "head"),
        P(None, "seq", "head"),
        P("grp"),
        P("grp", "seq", "head"),
        P("grp", "seq", "head"),
    )

    def step(*arrays):
        plan = body if fits(mesh, arrays[0], arrays[1], arrays[5]) else general_body
        return jax.shard_map(
            plan,
            mesh=mesh,
            in_specs=placed,
            out_specs=(P("grp", "seq", "head"),) * 3,
            check_vma=False,
        )(*arrays)

    return step
```

```python
import functools

import jax
import jax.numpy as jnp
from jax import lax
from jax.experimental import pallas as pl
from jax.experimental.pallas import tpu as pltpu
from jax.sharding import PartitionSpec as P

DH = 64
TILE = 64
DOCS = 4


SCALE = 0.125
FLOOR_SCORE = -1e30

BF = jnp.bfloat16
F32 = jnp.float32


def expand(tile_grid, tile_edge):
    return jnp.repeat(jnp.repeat(tile_grid, tile_edge, axis=0), tile_edge, axis=1)


def attend(keys, values, queries, cotangent, length):
    position = jnp.arange(keys.shape[0])[None, :]
    live = position < length
    scores = jnp.dot(queries, keys.T, preferred_element_type=jnp.float32) * SCALE
    scores = jnp.where(live, scores, FLOOR_SCORE)
    row_max = jnp.max(scores, axis=1, keepdims=True)
    weights = jnp.where(live, jnp.exp(scores - row_max), 0.0)
    probs = weights / jnp.sum(weights, axis=1, keepdims=True)
    probs_low = probs.astype(jnp.bfloat16)
    output = jnp.dot(probs_low, values, preferred_element_type=jnp.float32)
    delta = jnp.sum(cotangent.astype(jnp.float32) * output, axis=1, keepdims=True)
    prob_grad = jnp.dot(cotangent, values.T, preferred_element_type=jnp.float32)
    score_grad = (probs * (prob_grad - delta) * SCALE).astype(jnp.bfloat16)
    query_grad = jnp.dot(score_grad, keys, preferred_element_type=jnp.float32)
    key_grad = jnp.dot(score_grad.T, queries, preferred_element_type=jnp.float32)
    value_grad = jnp.dot(probs_low.T, cotangent, preferred_element_type=jnp.float32)
    return (
        output.astype(jnp.bfloat16),
        query_grad.astype(jnp.bfloat16),
        key_grad.astype(jnp.bfloat16),
        value_grad.astype(jnp.bfloat16),
    )


def project(encoder, key_piece, value_piece):
    count = key_piece.shape[0]
    flat = encoder.reshape(DOCS * encoder.shape[1], count)
    key_flat = jnp.dot(flat, key_piece, preferred_element_type=jnp.float32)
    value_flat = jnp.dot(flat, value_piece, preferred_element_type=jnp.float32)
    shape_out = (DOCS, encoder.shape[1], key_piece.shape[1])
    return (key_flat.reshape(shape_out), value_flat.reshape(shape_out))


def back_product(key_rows, value_rows, key_piece, value_piece):
    contract = (((1,), (1,)), ((), ()))
    total = lax.dot_general(key_rows, key_piece, contract, preferred_element_type=jnp.float32)
    return total + lax.dot_general(
        value_rows, value_piece, contract, preferred_element_type=jnp.float32
    )


def general_body(encoder, key_weight, value_weight, tile_mask, lengths, queries, cotangent):
    seq_count = lax.axis_size("seq")
    enc_rows = encoder.shape[1]
    dec_rows = queries.shape[1]
    group_heads = queries.shape[2] // DH
    pair_count = DOCS * group_heads
    local_pairs = pair_count // seq_count
    key_masked = key_weight * expand(tile_mask[0], TILE).astype(jnp.bfloat16)
    value_masked = value_weight * expand(tile_mask[1], TILE).astype(jnp.bfloat16)
    full_key, full_value = (
        lax.all_gather(key_masked, "seq", axis=0, tiled=True),
        lax.all_gather(value_masked, "seq", axis=0, tiled=True),
    )
    key_sum, value_sum = project(encoder, full_key, full_value)

    def to_pairs(first, second, rows):
        joined = jnp.concatenate(
            [
                first.reshape(DOCS, rows, group_heads, DH),
                second.reshape(DOCS, rows, group_heads, DH),
            ],
            axis=3,
        )
        return joined.transpose(0, 2, 1, 3).reshape(pair_count, rows, 2 * DH)

    def from_pairs(block, rows):
        shaped = block.reshape(DOCS, group_heads, rows, 2 * DH).transpose(0, 2, 1, 3)
        first = shaped[..., :DH].reshape(DOCS, rows, group_heads * DH)
        second = shaped[..., DH:].reshape(DOCS, rows, group_heads * DH)
        return (first, second)

    query_pairs = to_pairs(queries, cotangent, dec_rows)
    query_owned = lax.all_to_all(query_pairs, "seq", split_axis=0, concat_axis=1, tiled=True)
    kv_pairs = to_pairs(key_sum.astype(jnp.bfloat16), value_sum.astype(jnp.bfloat16), enc_rows)
    kv_owned = lax.all_to_all(kv_pairs, "seq", split_axis=0, concat_axis=1, tiled=True)
    pair_ids = lax.axis_index("seq") * local_pairs + jnp.arange(local_pairs)
    doc_of_pair = pair_ids // group_heads
    pair_length = jnp.sum(
        jnp.where(doc_of_pair[:, None] == jnp.arange(DOCS)[None, :], lengths[None, :], 0), axis=1
    )

    def owner_pair(items):
        pair_kv, pair_query, length = items
        output, query_grad, key_grad, value_grad = attend(
            pair_kv[:, :DH], pair_kv[:, DH:], pair_query[:, :DH], pair_query[:, DH:], length
        )
        return (
            jnp.concatenate([output, query_grad], axis=1),
            jnp.concatenate([key_grad, value_grad], axis=1),
        )

    front, back = lax.map(owner_pair, (kv_owned, query_owned, pair_length))
    front_rows, back_rows = (
        lax.all_to_all(front, "seq", split_axis=1, concat_axis=0, tiled=True),
        lax.all_to_all(back, "seq", split_axis=1, concat_axis=0, tiled=True),
    )
    attention, query_grad = from_pairs(front_rows, dec_rows)
    key_grads, value_grads = from_pairs(back_rows, enc_rows)
    key_rows = key_grads.reshape(DOCS * enc_rows, group_heads * DH)
    value_rows = value_grads.reshape(DOCS * enc_rows, group_heads * DH)
    grad_terms = back_product(key_rows, value_rows, full_key, full_value)
    grad_share = lax.psum_scatter(grad_terms, "head", scatter_dimension=1, tiled=True)
    encoder_grad = grad_share.astype(jnp.bfloat16).reshape(DOCS, enc_rows, grad_share.shape[1])
    return (attention, query_grad, encoder_grad)


SEQ = 4
PIECE = 512


def fits(mesh, encoder, key_weight, queries):
    return (
        mesh.shape["seq"] == SEQ
        and mesh.shape["head"] == 4
        and mesh.shape["grp"] == 2
        and encoder.shape == (DOCS * 2, 256, 4096)
        and key_weight.shape == (4096, 4096)
        and queries.shape == (DOCS * 2, 64, 4096)
    )


def prune_kernel(mask_ref, key_ref, value_ref, query_ref, cot_ref, own_ref, *message_refs):
    s, g = lax.axis_index("seq"), lax.axis_index("grp")
    left = lax.broadcasted_iota(jnp.int32, (1, 128), 1) < TILE

    def write(out_ref, first_tile, tiles, column):
        for t in range(tiles):
            tile = first_tile + t
            row = pl.ds(pl.multiple_of(tile * TILE, TILE), TILE)
            for side, ref in ((0, key_ref), (1, value_ref)):
                for part in range(2):
                    at = pl.ds(pl.multiple_of(column * 256 + part * 128, 128), 128)
                    first = mask_ref[side, tile, column * 4 + part * 2]
                    second = mask_ref[side, tile, column * 4 + part * 2 + 1]
                    keep = jnp.where(left, first, second).astype(F32)
                    to = side * 256 + part * 128
                    out_ref[t * TILE : (t + 1) * TILE, to : to + 128] = (
                        ref[row, at].astype(F32) * keep
                    ).astype(BF)

    first, second, third = message_refs[:3]
    for k, ref in enumerate(message_refs[3:]):
        at = pl.ds(pl.multiple_of(lax.bitwise_xor(s, k) * 256, 256), 256)
        ref[:, 0:256] = query_ref[:, at]
        ref[:, 256:512] = cot_ref[:, at]
    write(second, g * 8, 8, lax.bitwise_xor(s, 2))
    write(first, g * 8, 8, lax.bitwise_xor(s, 1))
    write(third, g * 8, 8, lax.bitwise_xor(s, 3))
    write(own_ref, 0, 16, s)


def prune(tile_mask, key_weight, value_weight, queries, cotangent):
    whole = pl.BlockSpec(memory_space=pltpu.VMEM)
    shapes = [(2 * PIECE, 512)] + [(PIECE, 512)] * 3 + [(64, 512)] * 4
    return pl.pallas_call(
        prune_kernel,
        out_shape=[jax.ShapeDtypeStruct(shape, BF) for shape in shapes],
        in_specs=[pl.BlockSpec(memory_space=pltpu.SMEM)] + [whole] * 4,
        out_specs=[whole] * len(shapes),
        compiler_params=pltpu.CompilerParams(vmem_limit_bytes=12 * 1024 * 1024),
        name="prune",
    )(tile_mask, key_weight, value_weight, queries, cotangent)


NT = (((1,), (1,)), ((), ()))
TN = (((0,), (0,)), ((), ()))
NN = (((1,), (0,)), ((), ()))


def dot(a, b, dims=NN):
    return lax.dot_general(a, b, dims, preferred_element_type=F32)


class Mover:
    def __init__(self, sems):
        self.sems = sems
        self.used = 0

    def start(self, pairs):
        copies = []
        for src, dst in pairs:
            copy = pltpu.make_async_copy(src, dst, self.sems.at[self.used])
            copy.start()
            self.used += 1
            copies.append(copy)
        return copies


def piece_rows(w_s, core, at, first, count):
    return w_s.at[core, pl.ds(pl.multiple_of(at * 1024 + first, 256), count)]


PACKED = 3 * 2 * PIECE


def pack_kernel(own, z1, z2, y1, y2, q0, q1, q2, q3, out_ref, sems):
    g = lax.axis_index("grp")
    pairs = [(own, out_ref.at[0 : 2 * PIECE])]
    for k, z, y in ((1, z1, y1), (2, z2, y2)):
        for piece, side in ((z, g), (y, 1 - g)):
            first = pl.multiple_of(2 * PIECE * k + side * PIECE, PIECE)
            pairs.append((piece, out_ref.at[pl.ds(first, PIECE)]))
    for k, piece in enumerate((q0, q1, q2, q3)):
        first = PACKED + 64 * lax.bitwise_xor(lax.axis_index("seq"), k)
        pairs.append((piece, out_ref.at[pl.ds(pl.multiple_of(first, 64), 64)]))
    for copy in Mover(sems).start(pairs):
        copy.wait()


def pack_call(*arrays):
    here = pl.BlockSpec(memory_space=pl.ANY)
    return pl.pallas_call(
        pack_kernel,
        out_shape=jax.ShapeDtypeStruct((PACKED + 256, 512), BF),
        in_specs=[here] * len(arrays),
        out_specs=pl.BlockSpec(memory_space=pltpu.VMEM),
        scratch_shapes=[pltpu.SemaphoreType.DMA((9,))],
        compiler_params=pltpu.CompilerParams(vmem_limit_bytes=6 * 1024 * 1024),
        cost_estimate=pl.CostEstimate(flops=1, bytes_accessed=1, transcendentals=0),
        name="pack",
    )(*arrays)


def early_weights(w_s, c, s, mine, theirs):
    pairs = []
    for core, packed in ((c, mine), (1 - c, theirs)):
        for k in range(3):
            rows = packed.at[2 * PIECE * k : 2 * PIECE * (k + 1)]
            pairs.append((rows, piece_rows(w_s, core, lax.bitwise_xor(s, k), 0, 2 * PIECE)))
    return pairs


def early_kernel(*refs):
    enc, e1, e2, e3, x1, x2, x3 = refs[:7]
    mine, theirs = refs[7:9]
    sum_ref, last_ref, enc_s, w_s, sems = refs[9:]
    s, h = lax.axis_index("seq"), lax.axis_index("head")
    c = lax.rem(h, 2)
    x = h // 2
    mover = Mover(sems)

    def rows_of(doc, at):
        return enc_s.at[pl.ds(pl.multiple_of(doc * 256 + at * 64, 64), 64)]

    pairs = [(enc.at[2 * i + c], rows_of(i, s)) for i in range(2)]
    for k, (own, other) in enumerate(((e1, x1), (e2, x2), (e3, x3))):
        at = lax.bitwise_xor(s, k + 1)
        pairs += [(own, rows_of(x, at)), (other, rows_of(1 - x, at))]
    pairs += early_weights(w_s, c, s, mine, theirs)
    for copy in mover.start(pairs):
        copy.wait()

    def columns(k):
        at = lax.bitwise_xor(s, k)
        return pl.ds(pl.multiple_of(at * 1024, 1024), 1024)

    for core in range(2):
        for half in range(2):
            row = slice(half * 256, half * 256 + 256)
            total = dot(enc_s[row, columns(0)], w_s[core, columns(0), :])
            for k in (1, 2):
                total = total + dot(enc_s[row, columns(k)], w_s[core, columns(k), :])
            sum_ref[core, row] = total
    last_ref[...] = enc_s[:, columns(3)]


def early_call(arrays):
    here = pl.BlockSpec(memory_space=pl.ANY)
    vmem = pl.BlockSpec(memory_space=pltpu.VMEM)
    return pl.pallas_call(
        early_kernel,
        out_shape=[
            jax.ShapeDtypeStruct((2, 512, 512), F32),
            jax.ShapeDtypeStruct((512, 1024), BF),
        ],
        in_specs=[here] * len(arrays),
        out_specs=[vmem] * 2,
        scratch_shapes=[
            pltpu.VMEM((512, 4096), BF),
            pltpu.VMEM((2, 4096, 512), BF),
            pltpu.SemaphoreType.DMA((18,)),
        ],
        compiler_params=pltpu.CompilerParams(vmem_limit_bytes=28 * 1024 * 1024),
        cost_estimate=pl.CostEstimate(
            flops=1, bytes_accessed=1, transcendentals=0
        ),
        name="early",
    )(*arrays)


def main_kernel(lengths, *refs):
    early_sum, last_rows = refs[:2]
    mine, theirs = refs[2:5], refs[5:8]
    (
        att_ref, qg_ref, own_ref,
        a3, b3, a2, b2, b10, a10, core_ref,
        w_s, qc_s, grad_s, sems,
    ) = refs[8:]
    s, g, h = lax.axis_index("seq"), lax.axis_index("grp"), lax.axis_index("head")
    c = lax.rem(h, 2)
    mover = Mover(sems)
    far = lax.bitwise_xor(s, 3)
    pairs = []
    for core, pieces in ((c, mine), (1 - c, theirs)):
        packed, z3, y3 = pieces
        for src, side in ((z3, g), (y3, 1 - g)):
            pairs.append((src, piece_rows(w_s, core, far, side * PIECE, PIECE)))
        for d in range(SEQ):
            pairs.append((packed.at[PACKED + 64 * d : PACKED + 64 * d + 64], qc_s.at[core, d]))
    now = mover.start(pairs)
    later = mover.start(early_weights(w_s, c, s, mine[0], theirs[0]))
    for copy in now:
        copy.wait()
    far_rows = pl.ds(pl.multiple_of(far * 1024, 1024), 1024)

    row_head = lax.broadcasted_iota(jnp.int32, (256, 256), 0) // DH
    col_head = lax.broadcasted_iota(jnp.int32, (256, 256), 1) // DH
    same = row_head == col_head
    position = lax.broadcasted_iota(jnp.int32, (256, 256), 1)

    def spread(block):
        four = jnp.concatenate([block] * 4, axis=0)
        return jnp.where(same, four, jnp.zeros_like(four))

    def gather_heads(block):
        kept = jnp.where(same, block, 0.0)
        return (kept[0:64] + kept[64:128]) + (kept[128:192] + kept[192:256])

    for core in range(2):
        slot = lax.rem(core + c, 2)
        for doc in range(2):
            row = slice(doc * 256, doc * 256 + 256)
            both = early_sum[core, row] + dot(last_rows[row], w_s[core, far_rows, :])
            keys = both[:, :256].astype(BF)
            values = both[:, 256:].astype(BF)
            at = pl.ds(pl.multiple_of((2 * doc + c) * 16, 16), 16)
            query = spread(qc_s[core, :, at, 0:256].reshape(64, 256))
            cot = spread(qc_s[core, :, at, 256:512].reshape(64, 256))
            live = position < lengths[2 * doc + c]
            scores = dot(query, keys, NT) * SCALE
            scores = jnp.where(live, scores, FLOOR_SCORE)
            row_max = jnp.max(scores, axis=1, keepdims=True)
            weights = jnp.where(live, jnp.exp(scores - row_max), 0.0)
            probs = weights / jnp.sum(weights, axis=1, keepdims=True)
            low = probs.astype(BF)
            output = dot(low, values)
            delta = jnp.sum(cot.astype(F32) * output, axis=1, keepdims=True)
            prob_grad = dot(cot, values, NT)
            score_grad = (probs * (prob_grad - delta) * SCALE).astype(BF)
            query_grad = dot(score_grad, keys)
            att_ref[slot, doc] = gather_heads(output).astype(BF)
            qg_ref[slot, doc] = gather_heads(query_grad).astype(BF)
            key_grad = dot(score_grad, query, TN).astype(BF)
            value_grad = dot(low, cot, TN).astype(BF)
            for at in range(4):
                first = lax.bitwise_xor(s, at) * 128 + doc * 64
                to = pl.ds(pl.multiple_of(first, 64), 64)
                grad_s[core, to, 0:256] = key_grad[at * 64 : at * 64 + 64]
                grad_s[core, to, 256:512] = value_grad[at * 64 : at * 64 + 64]

    for copy in later:
        copy.wait()
    cores = [core_ref.at[k] for k in range(4)]
    owns = [own_ref.at[k] for k in range(4)]
    for flip, outs in (
        (2, (a10.at[1], a10.at[0], a2, a3)),
        (3, (b10.at[1], b10.at[0], b2, b3)),
        (1, cores),
        (0, owns),
    ):
        block = lax.bitwise_xor(h, flip)
        for n in range(4):
            at = pl.ds(pl.multiple_of(block * 1024 + n * 256, 256), 256)
            total = dot(grad_s[0], w_s[0, at, :], NT) + dot(grad_s[1], w_s[1, at, :], NT)
            for k in range(4):
                for doc in range(2):
                    first = k * 128 + doc * 64
                    outs[k][doc, :, n * 256 : n * 256 + 256] = total[first : first + 64].astype(
                        outs[k].dtype
                    )


def main_call(lengths, arrays):
    here = pl.BlockSpec(memory_space=pl.ANY)
    vmem = pl.BlockSpec(memory_space=pltpu.VMEM)
    smem = pl.BlockSpec(memory_space=pltpu.SMEM)
    piece = jax.ShapeDtypeStruct((2, 64, 1024), BF)
    front = jax.ShapeDtypeStruct((2, 2, 64, 256), BF)
    return pl.pallas_call(
        main_kernel,
        out_shape=[
            front,
            front,
            jax.ShapeDtypeStruct((4, 2, 64, 1024), F32),
        ]
        + [piece] * 4
        + [jax.ShapeDtypeStruct((2, 2, 64, 1024), BF)] * 2
        + [jax.ShapeDtypeStruct((4, 2, 64, 1024), BF)],
        in_specs=[smem] + [vmem] * 2 + [here] * (len(arrays) - 2),
        out_specs=[vmem] * 10,
        scratch_shapes=[
            pltpu.VMEM((2, 4096, 512), BF),
            pltpu.VMEM((2, 4, 64, 512), BF),
            pltpu.VMEM((2, 512, 512), BF),
            pltpu.SemaphoreType.DMA((26,)),
        ],
        compiler_params=pltpu.CompilerParams(vmem_limit_bytes=34 * 1024 * 1024),
        cost_estimate=pl.CostEstimate(
            flops=6 * 10**9, bytes_accessed=24 * 2**20, transcendentals=2**18
        ),
        name="attend",
    )(lengths, *arrays)


def final_kernel(own, core, near, far, near1, near2, far1, far2, out_ref):
    c = lax.rem(lax.axis_index("head"), 2)
    for i in range(2):
        mine = (own[0, i] + near[1, i].astype(F32)) + (near1[i].astype(F32) + near2[i].astype(F32))
        theirs = (core[0, i].astype(F32) + far[1, i].astype(F32)) + (
            far1[i].astype(F32) + far2[i].astype(F32)
        )
        out_ref[2 * i + c] = mine.astype(BF)
        out_ref[2 * i + 1 - c] = theirs.astype(BF)


def small_call(kernel, shape, name, *arrays):
    vmem = pl.BlockSpec(memory_space=pltpu.VMEM)
    return pl.pallas_call(
        kernel,
        out_shape=jax.ShapeDtypeStruct(shape, BF),
        in_specs=[vmem] * len(arrays),
        out_specs=vmem,
        compiler_params=pltpu.CompilerParams(vmem_limit_bytes=12 * 1024 * 1024),
        name=name,
    )(*arrays)


def together(*values):
    return lax.optimization_barrier(values)


def summed(*parts):
    total = parts[0].astype(F32)
    for part in parts[1:]:
        total = total + part.astype(F32)
    return total.astype(BF)


def body(encoder, key_weight, value_weight, tile_mask, lengths, queries, cotangent):
    h = lax.axis_index("head")
    c = lax.rem(h, 2)

    def along(value, k):
        return lax.ppermute(value, "seq", [(a, a ^ k) for a in range(SEQ)])

    def flip(value, bits):
        return lax.ppermute(value, "head", [(a, a ^ bits) for a in range(4)])

    def across(value):
        return lax.ppermute(value, "grp", [(0, 1), (1, 0)])

    e0 = lax.dynamic_index_in_dim(encoder, h, 0, keepdims=False)
    e2 = along(e0, 2)
    w_own, m1, m2, m3, q0, q1, q2, q3 = prune(
        tile_mask, key_weight, value_weight, queries.reshape(64, 1024), cotangent.reshape(64, 1024)
    )
    z1 = along(m1, 1)
    q1, q2, q3 = along(q1, 1), along(q2, 2), along(q3, 3)
    e2, z1, q1, q2, q3, m2, e0 = together(e2, z1, q1, q2, q3, m2, e0)
    e3, z2, x2, y1 = along(e2, 1), along(m2, 2), flip(e2, 2), across(z1)
    e3, z2, x2, y1, m3, e0 = together(e3, z2, x2, y1, m3, e0)
    z3, e1, y2, x3 = along(m3, 3), along(e0, 1), across(z2), flip(e3, 2)
    x1 = flip(e1, 2)
    z3, x3, e1, w_own = together(z3, x3, e1, w_own)
    y3 = across(z3)
    packed = pack_call(w_own, z1, z2, y1, y2, q0, q1, q2, q3)
    packed_there = flip(packed, 1)
    early = early_call([encoder, e1, e2, e3, x1, x2, x3, packed, packed_there])
    z3_there = flip(z3, 1)
    y3, *early = together(y3, *early)
    y3_there = flip(y3, 1)
    outs = main_call(lengths, early + [packed, z3, y3, packed_there, z3_there, y3_there])
    att, qgrad, own = outs[:3]
    a3, b3, a2, b2, b10, a10, to_core = outs[3:]
    from_core = flip(to_core, 1)
    front = jnp.stack([att, qgrad], axis=1)
    other = flip(front[1], 1)
    b3, a3 = flip(b3, 3), flip(a3, 2)
    b3, core, other, b2, a2 = together(b3, from_core, other, b2, a2)
    b2, a2 = flip(b2, 3), flip(a2, 2)
    far3, own = together(summed(core[3], b3), own)
    far3 = along(far3, 1)
    near3, core = together(summed(own[3], a3), core)
    near3 = along(near3, 1)
    b2, b10, a10 = together(b2, b10, a10)
    b10, a10 = flip(b10, 3), flip(a10, 2)
    far2, own = together(summed(core[2], b2, far3), own)
    far2 = along(far2, 2)
    near2, core = together(summed(own[2], a2, near3), core)
    near2 = along(near2, 2)
    back = jnp.stack([front[0], other]).reshape(2, 2, 2, SEQ, 16, 256).transpose(3, 0, 1, 2, 4, 5)
    near1, core, back = together(summed(own[1], a10[0]), core, back)
    near1 = along(near1, 1)
    b10, near2, far2 = together(b10, near2, far2)
    far1 = along(summed(core[1], b10[0]), 1)
    from_core = core
    back = lax.all_to_all(back, "seq", split_axis=0, concat_axis=0, tiled=True)
    back = back.transpose(2, 3, 1, 4, 0, 5).reshape(2, 2, 2, 16, 1024)
    back = jnp.where(c == 0, back, back[:, :, ::-1])
    back = back.reshape(2, DOCS, 16, 1024)
    a10, back = together(a10, back)
    encoder_grad = small_call(
        final_kernel, (DOCS, 64, 1024), "final", own, from_core, a10, b10, near1, near2, far1, far2
    )
    return (back[0], back[1], encoder_grad)


def solution(mesh):
    placed = (
        P("grp", "seq", None),
        P("seq", "head"),
        P("seq", "head"),
        P(None, "seq", "head"),
        P("grp"),
        P("grp", "seq", "head"),
        P("grp", "seq", "head"),
    )

    def step(*arrays):
        plan = body if fits(mesh, arrays[0], arrays[1], arrays[5]) else general_body
        return jax.shard_map(
            plan,
            mesh=mesh,
            in_specs=placed,
            out_specs=(P("grp", "seq", "head"),) * 3,
            check_vma=False,
        )(*arrays)

    return step
```

```python
import functools

import jax
import jax.numpy as jnp
from jax import lax
from jax.experimental import pallas as pl
from jax.experimental.pallas import tpu as pltpu
from jax.sharding import PartitionSpec as P

DH = 64
TILE = 64
DOCS = 4


SCALE = 0.125
FLOOR_SCORE = -1e30

BF = jnp.bfloat16
F32 = jnp.float32


def expand(tile_grid, tile_edge):
    return jnp.repeat(jnp.repeat(tile_grid, tile_edge, axis=0), tile_edge, axis=1)


def attend(keys, values, queries, cotangent, length):
    position = jnp.arange(keys.shape[0])[None, :]
    live = position < length
    scores = jnp.dot(queries, keys.T, preferred_element_type=jnp.float32) * SCALE
    scores = jnp.where(live, scores, FLOOR_SCORE)
    row_max = jnp.max(scores, axis=1, keepdims=True)
    weights = jnp.where(live, jnp.exp(scores - row_max), 0.0)
    probs = weights / jnp.sum(weights, axis=1, keepdims=True)
    probs_low = probs.astype(jnp.bfloat16)
    output = jnp.dot(probs_low, values, preferred_element_type=jnp.float32)
    delta = jnp.sum(cotangent.astype(jnp.float32) * output, axis=1, keepdims=True)
    prob_grad = jnp.dot(cotangent, values.T, preferred_element_type=jnp.float32)
    score_grad = (probs * (prob_grad - delta) * SCALE).astype(jnp.bfloat16)
    query_grad = jnp.dot(score_grad, keys, preferred_element_type=jnp.float32)
    key_grad = jnp.dot(score_grad.T, queries, preferred_element_type=jnp.float32)
    value_grad = jnp.dot(probs_low.T, cotangent, preferred_element_type=jnp.float32)
    return (
        output.astype(jnp.bfloat16),
        query_grad.astype(jnp.bfloat16),
        key_grad.astype(jnp.bfloat16),
        value_grad.astype(jnp.bfloat16),
    )


def project(encoder, key_piece, value_piece):
    count = key_piece.shape[0]
    flat = encoder.reshape(DOCS * encoder.shape[1], count)
    key_flat = jnp.dot(flat, key_piece, preferred_element_type=jnp.float32)
    value_flat = jnp.dot(flat, value_piece, preferred_element_type=jnp.float32)
    shape_out = (DOCS, encoder.shape[1], key_piece.shape[1])
    return (key_flat.reshape(shape_out), value_flat.reshape(shape_out))


def back_product(key_rows, value_rows, key_piece, value_piece):
    contract = (((1,), (1,)), ((), ()))
    total = lax.dot_general(key_rows, key_piece, contract, preferred_element_type=jnp.float32)
    return total + lax.dot_general(
        value_rows, value_piece, contract, preferred_element_type=jnp.float32
    )


def general_body(encoder, key_weight, value_weight, tile_mask, lengths, queries, cotangent):
    seq_count = lax.axis_size("seq")
    enc_rows = encoder.shape[1]
    dec_rows = queries.shape[1]
    group_heads = queries.shape[2] // DH
    pair_count = DOCS * group_heads
    local_pairs = pair_count // seq_count
    key_masked = key_weight * expand(tile_mask[0], TILE).astype(jnp.bfloat16)
    value_masked = value_weight * expand(tile_mask[1], TILE).astype(jnp.bfloat16)
    full_key, full_value = (
        lax.all_gather(key_masked, "seq", axis=0, tiled=True),
        lax.all_gather(value_masked, "seq", axis=0, tiled=True),
    )
    key_sum, value_sum = project(encoder, full_key, full_value)

    def to_pairs(first, second, rows):
        joined = jnp.concatenate(
            [
                first.reshape(DOCS, rows, group_heads, DH),
                second.reshape(DOCS, rows, group_heads, DH),
            ],
            axis=3,
        )
        return joined.transpose(0, 2, 1, 3).reshape(pair_count, rows, 2 * DH)

    def from_pairs(block, rows):
        shaped = block.reshape(DOCS, group_heads, rows, 2 * DH).transpose(0, 2, 1, 3)
        first = shaped[..., :DH].reshape(DOCS, rows, group_heads * DH)
        second = shaped[..., DH:].reshape(DOCS, rows, group_heads * DH)
        return (first, second)

    query_pairs = to_pairs(queries, cotangent, dec_rows)
    query_owned = lax.all_to_all(query_pairs, "seq", split_axis=0, concat_axis=1, tiled=True)
    kv_pairs = to_pairs(key_sum.astype(jnp.bfloat16), value_sum.astype(jnp.bfloat16), enc_rows)
    kv_owned = lax.all_to_all(kv_pairs, "seq", split_axis=0, concat_axis=1, tiled=True)
    pair_ids = lax.axis_index("seq") * local_pairs + jnp.arange(local_pairs)
    doc_of_pair = pair_ids // group_heads
    pair_length = jnp.sum(
        jnp.where(doc_of_pair[:, None] == jnp.arange(DOCS)[None, :], lengths[None, :], 0), axis=1
    )

    def owner_pair(items):
        pair_kv, pair_query, length = items
        output, query_grad, key_grad, value_grad = attend(
            pair_kv[:, :DH], pair_kv[:, DH:], pair_query[:, :DH], pair_query[:, DH:], length
        )
        return (
            jnp.concatenate([output, query_grad], axis=1),
            jnp.concatenate([key_grad, value_grad], axis=1),
        )

    front, back = lax.map(owner_pair, (kv_owned, query_owned, pair_length))
    front_rows, back_rows = (
        lax.all_to_all(front, "seq", split_axis=1, concat_axis=0, tiled=True),
        lax.all_to_all(back, "seq", split_axis=1, concat_axis=0, tiled=True),
    )
    attention, query_grad = from_pairs(front_rows, dec_rows)
    key_grads, value_grads = from_pairs(back_rows, enc_rows)
    key_rows = key_grads.reshape(DOCS * enc_rows, group_heads * DH)
    value_rows = value_grads.reshape(DOCS * enc_rows, group_heads * DH)
    grad_terms = back_product(key_rows, value_rows, full_key, full_value)
    grad_share = lax.psum_scatter(grad_terms, "head", scatter_dimension=1, tiled=True)
    encoder_grad = grad_share.astype(jnp.bfloat16).reshape(DOCS, enc_rows, grad_share.shape[1])
    return (attention, query_grad, encoder_grad)


SEQ = 4
PIECE = 512


def fits(mesh, encoder, key_weight, queries):
    return (
        mesh.shape["seq"] == SEQ
        and mesh.shape["head"] == 4
        and mesh.shape["grp"] == 2
        and encoder.shape == (DOCS * 2, 256, 4096)
        and key_weight.shape == (4096, 4096)
        and queries.shape == (DOCS * 2, 64, 4096)
    )


def prune_kernel(mask_ref, key_ref, value_ref, query_ref, cot_ref, own_ref, *message_refs):
    s, g = lax.axis_index("seq"), lax.axis_index("grp")
    left = lax.broadcasted_iota(jnp.int32, (1, 128), 1) < TILE

    def write(out_ref, first_tile, tiles, column):
        for t in range(tiles):
            tile = first_tile + t
            row = pl.ds(pl.multiple_of(tile * TILE, TILE), TILE)
            for side, ref in ((0, key_ref), (1, value_ref)):
                for part in range(2):
                    at = pl.ds(pl.multiple_of(column * 256 + part * 128, 128), 128)
                    first = mask_ref[side, tile, column * 4 + part * 2]
                    second = mask_ref[side, tile, column * 4 + part * 2 + 1]
                    keep = jnp.where(left, first, second).astype(F32)
                    to = side * 256 + part * 128
                    out_ref[t * TILE : (t + 1) * TILE, to : to + 128] = (
                        ref[row, at].astype(F32) * keep
                    ).astype(BF)

    first, second, third = message_refs[:3]
    for k, ref in enumerate(message_refs[3:]):
        at = pl.ds(pl.multiple_of(lax.bitwise_xor(s, k) * 256, 256), 256)
        ref[:, 0:256] = query_ref[:, at]
        ref[:, 256:512] = cot_ref[:, at]
    write(second, g * 8, 8, lax.bitwise_xor(s, 2))
    write(first, g * 8, 8, lax.bitwise_xor(s, 1))
    write(third, g * 8, 8, lax.bitwise_xor(s, 3))
    write(own_ref, 0, 16, s)


def prune(tile_mask, key_weight, value_weight, queries, cotangent):
    whole = pl.BlockSpec(memory_space=pltpu.VMEM)
    shapes = [(2 * PIECE, 512)] + [(PIECE, 512)] * 3 + [(64, 512)] * 4
    return pl.pallas_call(
        prune_kernel,
        out_shape=[jax.ShapeDtypeStruct(shape, BF) for shape in shapes],
        in_specs=[pl.BlockSpec(memory_space=pltpu.SMEM)] + [whole] * 4,
        out_specs=[whole] * len(shapes),
        compiler_params=pltpu.CompilerParams(vmem_limit_bytes=12 * 1024 * 1024),
        name="prune",
    )(tile_mask, key_weight, value_weight, queries, cotangent)


NT = (((1,), (1,)), ((), ()))
TN = (((0,), (0,)), ((), ()))
NN = (((1,), (0,)), ((), ()))


def dot(a, b, dims=NN):
    return lax.dot_general(a, b, dims, preferred_element_type=F32)


class Mover:
    def __init__(self, sems):
        self.sems = sems
        self.used = 0

    def start(self, pairs):
        copies = []
        for src, dst in pairs:
            copy = pltpu.make_async_copy(src, dst, self.sems.at[self.used])
            copy.start()
            self.used += 1
            copies.append(copy)
        return copies


def piece_rows(w_s, core, at, first, count):
    return w_s.at[core, pl.ds(pl.multiple_of(at * 1024 + first, 256), count)]


PACKED = 3 * 2 * PIECE


def pack_kernel(own, z1, z2, y1, y2, q0, q1, q2, q3, out_ref, sems):
    g = lax.axis_index("grp")
    pairs = [(own, out_ref.at[0 : 2 * PIECE])]
    for k, z, y in ((1, z1, y1), (2, z2, y2)):
        for piece, side in ((z, g), (y, 1 - g)):
            first = pl.multiple_of(2 * PIECE * k + side * PIECE, PIECE)
            pairs.append((piece, out_ref.at[pl.ds(first, PIECE)]))
    for k, piece in enumerate((q0, q1, q2, q3)):
        first = PACKED + 64 * lax.bitwise_xor(lax.axis_index("seq"), k)
        pairs.append((piece, out_ref.at[pl.ds(pl.multiple_of(first, 64), 64)]))
    for copy in Mover(sems).start(pairs):
        copy.wait()


def pack_call(*arrays):
    here = pl.BlockSpec(memory_space=pl.ANY)
    return pl.pallas_call(
        pack_kernel,
        out_shape=jax.ShapeDtypeStruct((PACKED + 256, 512), BF),
        in_specs=[here] * len(arrays),
        out_specs=pl.BlockSpec(memory_space=pltpu.VMEM),
        scratch_shapes=[pltpu.SemaphoreType.DMA((9,))],
        compiler_params=pltpu.CompilerParams(vmem_limit_bytes=6 * 1024 * 1024),
        cost_estimate=pl.CostEstimate(flops=1, bytes_accessed=1, transcendentals=0),
        name="pack",
    )(*arrays)


def early_weights(w_s, c, s, mine, theirs):
    pairs = []
    for core, packed in ((c, mine), (1 - c, theirs)):
        for k in range(3):
            rows = packed.at[2 * PIECE * k : 2 * PIECE * (k + 1)]
            pairs.append((rows, piece_rows(w_s, core, lax.bitwise_xor(s, k), 0, 2 * PIECE)))
    return pairs


def early_kernel(*refs):
    enc, e1, e2, e3, x1, x2, x3 = refs[:7]
    mine, theirs = refs[7:9]
    sum_ref, last_ref, enc_s, w_s, sems = refs[9:]
    s, h = lax.axis_index("seq"), lax.axis_index("head")
    c = lax.rem(h, 2)
    x = h // 2
    mover = Mover(sems)

    def rows_of(doc, at):
        return enc_s.at[pl.ds(pl.multiple_of(doc * 256 + at * 64, 64), 64)]

    pairs = [(enc.at[2 * i + c], rows_of(i, s)) for i in range(2)]
    for k, (own, other) in enumerate(((e1, x1), (e2, x2), (e3, x3))):
        at = lax.bitwise_xor(s, k + 1)
        pairs += [(own, rows_of(x, at)), (other, rows_of(1 - x, at))]
    pairs += early_weights(w_s, c, s, mine, theirs)
    for copy in mover.start(pairs):
        copy.wait()

    def columns(k):
        at = lax.bitwise_xor(s, k)
        return pl.ds(pl.multiple_of(at * 1024, 1024), 1024)

    for core in range(2):
        for half in range(2):
            row = slice(half * 256, half * 256 + 256)
            total = dot(enc_s[row, columns(0)], w_s[core, columns(0), :])
            for k in (1, 2):
                total = total + dot(enc_s[row, columns(k)], w_s[core, columns(k), :])
            sum_ref[core, row] = total
    last_ref[...] = enc_s[:, columns(3)]


def early_call(arrays):
    here = pl.BlockSpec(memory_space=pl.ANY)
    vmem = pl.BlockSpec(memory_space=pltpu.VMEM)
    return pl.pallas_call(
        early_kernel,
        out_shape=[
            jax.ShapeDtypeStruct((2, 512, 512), F32),
            jax.ShapeDtypeStruct((512, 1024), BF),
        ],
        in_specs=[here] * len(arrays),
        out_specs=[vmem] * 2,
        scratch_shapes=[
            pltpu.VMEM((512, 4096), BF),
            pltpu.VMEM((2, 4096, 512), BF),
            pltpu.SemaphoreType.DMA((18,)),
        ],
        compiler_params=pltpu.CompilerParams(vmem_limit_bytes=28 * 1024 * 1024),
        cost_estimate=pl.CostEstimate(
            flops=1, bytes_accessed=1, transcendentals=0
        ),
        name="early",
    )(*arrays)


def main_kernel(lengths, *refs):
    early_sum, last_rows = refs[:2]
    mine, theirs = refs[2:5], refs[5:8]
    (
        att_ref, qg_ref, own_ref,
        a3, b3, a2, b2, b10, a10, core_ref,
        w_s, qc_s, grad_s, sems,
    ) = refs[8:]
    s, g, h = lax.axis_index("seq"), lax.axis_index("grp"), lax.axis_index("head")
    c = lax.rem(h, 2)
    mover = Mover(sems)
    far = lax.bitwise_xor(s, 3)
    pairs = []
    for core, pieces in ((c, mine), (1 - c, theirs)):
        packed, z3, y3 = pieces
        for src, side in ((z3, g), (y3, 1 - g)):
            pairs.append((src, piece_rows(w_s, core, far, side * PIECE, PIECE)))
        for d in range(SEQ):
            pairs.append((packed.at[PACKED + 64 * d : PACKED + 64 * d + 64], qc_s.at[core, d]))
    now = mover.start(pairs)
    later = mover.start(early_weights(w_s, c, s, mine[0], theirs[0]))
    for copy in now:
        copy.wait()
    far_rows = pl.ds(pl.multiple_of(far * 1024, 1024), 1024)

    row_head = lax.broadcasted_iota(jnp.int32, (256, 256), 0) // DH
    col_head = lax.broadcasted_iota(jnp.int32, (256, 256), 1) // DH
    same = row_head == col_head
    position = lax.broadcasted_iota(jnp.int32, (256, 256), 1)

    def spread(block):
        four = jnp.concatenate([block] * 4, axis=0)
        return jnp.where(same, four, jnp.zeros_like(four))

    def gather_heads(block):
        kept = jnp.where(same, block, 0.0)
        return (kept[0:64] + kept[64:128]) + (kept[128:192] + kept[192:256])

    for core in range(2):
        slot = lax.rem(core + c, 2)
        for doc in range(2):
            row = slice(doc * 256, doc * 256 + 256)
            both = early_sum[core, row] + dot(last_rows[row], w_s[core, far_rows, :])
            keys = both[:, :256].astype(BF)
            values = both[:, 256:].astype(BF)
            at = pl.ds(pl.multiple_of((2 * doc + c) * 16, 16), 16)
            query = spread(qc_s[core, :, at, 0:256].reshape(64, 256))
            cot = spread(qc_s[core, :, at, 256:512].reshape(64, 256))
            live = position < lengths[2 * doc + c]
            scores = dot(query, keys, NT) * SCALE
            scores = jnp.where(live, scores, FLOOR_SCORE)
            row_max = jnp.max(scores, axis=1, keepdims=True)
            weights = jnp.where(live, jnp.exp(scores - row_max), 0.0)
            probs = weights / jnp.sum(weights, axis=1, keepdims=True)
            low = probs.astype(BF)
            output = dot(low, values)
            delta = jnp.sum(cot.astype(F32) * output, axis=1, keepdims=True)
            prob_grad = dot(cot, values, NT)
            score_grad = (probs * (prob_grad - delta) * SCALE).astype(BF)
            query_grad = dot(score_grad, keys)
            att_ref[slot, doc] = gather_heads(output).astype(BF)
            qg_ref[slot, doc] = gather_heads(query_grad).astype(BF)
            key_grad = dot(score_grad, query, TN).astype(BF)
            value_grad = dot(low, cot, TN).astype(BF)
            for at in range(4):
                first = lax.bitwise_xor(s, at) * 128 + doc * 64
                to = pl.ds(pl.multiple_of(first, 64), 64)
                grad_s[core, to, 0:256] = key_grad[at * 64 : at * 64 + 64]
                grad_s[core, to, 256:512] = value_grad[at * 64 : at * 64 + 64]

    for copy in later:
        copy.wait()
    cores = [core_ref.at[k] for k in range(4)]
    owns = [own_ref.at[k] for k in range(4)]
    for flip, outs in (
        (2, (a10.at[1], a10.at[0], a2, a3)),
        (3, (b10.at[1], b10.at[0], b2, b3)),
        (1, cores),
        (0, owns),
    ):
        block = lax.bitwise_xor(h, flip)
        for n in range(4):
            at = pl.ds(pl.multiple_of(block * 1024 + n * 256, 256), 256)
            total = dot(grad_s[0], w_s[0, at, :], NT) + dot(grad_s[1], w_s[1, at, :], NT)
            for k in range(4):
                for doc in range(2):
                    first = k * 128 + doc * 64
                    outs[k][doc, :, n * 256 : n * 256 + 256] = total[first : first + 64].astype(
                        outs[k].dtype
                    )


def main_call(lengths, arrays):
    here = pl.BlockSpec(memory_space=pl.ANY)
    vmem = pl.BlockSpec(memory_space=pltpu.VMEM)
    smem = pl.BlockSpec(memory_space=pltpu.SMEM)
    piece = jax.ShapeDtypeStruct((2, 64, 1024), BF)
    front = jax.ShapeDtypeStruct((2, 2, 64, 256), BF)
    return pl.pallas_call(
        main_kernel,
        out_shape=[
            front,
            front,
            jax.ShapeDtypeStruct((4, 2, 64, 1024), F32),
        ]
        + [piece] * 4
        + [jax.ShapeDtypeStruct((2, 2, 64, 1024), BF)] * 2
        + [jax.ShapeDtypeStruct((4, 2, 64, 1024), BF)],
        in_specs=[smem] + [vmem] * 2 + [here] * (len(arrays) - 2),
        out_specs=[vmem] * 10,
        scratch_shapes=[
            pltpu.VMEM((2, 4096, 512), BF),
            pltpu.VMEM((2, 4, 64, 512), BF),
            pltpu.VMEM((2, 512, 512), BF),
            pltpu.SemaphoreType.DMA((26,)),
        ],
        compiler_params=pltpu.CompilerParams(vmem_limit_bytes=34 * 1024 * 1024),
        cost_estimate=pl.CostEstimate(
            flops=6 * 10**9, bytes_accessed=24 * 2**20, transcendentals=2**18
        ),
        name="attend",
    )(lengths, *arrays)


def final_kernel(own, core, near, far, near1, near2, far1, far2, out_ref):
    c = lax.rem(lax.axis_index("head"), 2)
    for i in range(2):
        mine = (own[0, i] + near[1, i].astype(F32)) + (near1[i].astype(F32) + near2[i].astype(F32))
        theirs = (core[0, i].astype(F32) + far[1, i].astype(F32)) + (
            far1[i].astype(F32) + far2[i].astype(F32)
        )
        out_ref[2 * i + c] = mine.astype(BF)
        out_ref[2 * i + 1 - c] = theirs.astype(BF)


def small_call(kernel, shape, name, *arrays):
    vmem = pl.BlockSpec(memory_space=pltpu.VMEM)
    return pl.pallas_call(
        kernel,
        out_shape=jax.ShapeDtypeStruct(shape, BF),
        in_specs=[vmem] * len(arrays),
        out_specs=vmem,
        compiler_params=pltpu.CompilerParams(vmem_limit_bytes=12 * 1024 * 1024),
        name=name,
    )(*arrays)


def together(*values):
    return lax.optimization_barrier(values)


def summed(*parts):
    total = parts[0].astype(F32)
    for part in parts[1:]:
        total = total + part.astype(F32)
    return total.astype(BF)


def body(encoder, key_weight, value_weight, tile_mask, lengths, queries, cotangent):
    h = lax.axis_index("head")
    c = lax.rem(h, 2)

    def along(value, k):
        return lax.ppermute(value, "seq", [(a, a ^ k) for a in range(SEQ)])

    def flip(value, bits):
        return lax.ppermute(value, "head", [(a, a ^ bits) for a in range(4)])

    def across(value):
        return lax.ppermute(value, "grp", [(0, 1), (1, 0)])

    e0 = lax.dynamic_index_in_dim(encoder, h, 0, keepdims=False)
    e2 = along(e0, 2)
    e1 = along(e0, 1)
    w_own, m1, m2, m3, q0, q1, q2, q3 = prune(
        tile_mask, key_weight, value_weight, queries.reshape(64, 1024), cotangent.reshape(64, 1024)
    )
    q1, q2, q3 = along(q1, 1), along(q2, 2), along(q3, 3)
    e1, e2, m1, m2, q1, q2, q3 = together(e1, e2, m1, m2, q1, q2, q3)
    z2, z1 = along(m2, 2), along(m1, 1)
    e3 = along(e2, 1)
    x1, x2 = flip(e1, 2), flip(e2, 2)
    x1, x2, m3 = together(x1, x2, m3)
    z3 = along(m3, 3)
    x1, z2 = together(x1, z2)
    x2, e3 = together(x2, e3)
    y2 = across(z2)
    x3 = flip(e3, 2)
    y2, z1 = together(y2, z1)
    y1 = across(z1)
    z3, x3, w_own = together(z3, x3, w_own)
    y3 = across(z3)
    packed = pack_call(w_own, z1, z2, y1, y2, q0, q1, q2, q3)
    packed_there = flip(packed, 1)
    early = early_call([encoder, e1, e2, e3, x1, x2, x3, packed, packed_there])
    z3_there = flip(z3, 1)
    y3, *early = together(y3, *early)
    y3_there = flip(y3, 1)
    outs = main_call(lengths, early + [packed, z3, y3, packed_there, z3_there, y3_there])
    att, qgrad, own = outs[:3]
    a3, b3, a2, b2, b10, a10, to_core = outs[3:]
    from_core = flip(to_core, 1)
    front = jnp.stack([att, qgrad], axis=1)
    other = flip(front[1], 1)
    back = jnp.stack([front[0], other]).reshape(2, 2, 2, SEQ, 16, 256).transpose(3, 0, 1, 2, 4, 5)
    b3, a3 = flip(b3, 3), flip(a3, 2)
    b3, core, b2, a2, back = together(b3, from_core, b2, a2, back)
    back = lax.all_to_all(back, "seq", split_axis=0, concat_axis=0, tiled=True)
    b2, a2 = flip(b2, 3), flip(a2, 2)
    far3, own = together(summed(core[3], b3), own)
    far3 = along(far3, 1)
    near3, core = together(summed(own[3], a3), core)
    near3 = along(near3, 1)
    b2, b10, a10 = together(b2, b10, a10)
    b10, a10 = flip(b10, 3), flip(a10, 2)
    core, back = together(core, back)
    far2, own = together(summed(core[2], b2, far3), own)
    far2 = along(far2, 2)
    near2, core = together(summed(own[2], a2, near3), core)
    near2 = along(near2, 2)
    near1, core = together(summed(own[1], a10[0]), core)
    near1 = along(near1, 1)
    b10, near2, far2 = together(b10, near2, far2)
    far1 = along(summed(core[1], b10[0]), 1)
    from_core = core
    back = back.transpose(2, 3, 1, 4, 0, 5).reshape(2, 2, 2, 16, 1024)
    back = jnp.where(c == 0, back, back[:, :, ::-1])
    back = back.reshape(2, DOCS, 16, 1024)
    a10, back = together(a10, back)
    encoder_grad = small_call(
        final_kernel, (DOCS, 64, 1024), "final", own, from_core, a10, b10, near1, near2, far1, far2
    )
    return (back[0], back[1], encoder_grad)


def solution(mesh):
    placed = (
        P("grp", "seq", None),
        P("seq", "head"),
        P("seq", "head"),
        P(None, "seq", "head"),
        P("grp"),
        P("grp", "seq", "head"),
        P("grp", "seq", "head"),
    )

    def step(*arrays):
        plan = body if fits(mesh, arrays[0], arrays[1], arrays[5]) else general_body
        return jax.shard_map(
            plan,
            mesh=mesh,
            in_specs=placed,
            out_specs=(P("grp", "seq", "head"),) * 3,
            check_vma=False,
        )(*arrays)

    return step
```

```python
import functools

import jax
import jax.numpy as jnp
from jax import lax
from jax.experimental import pallas as pl
from jax.experimental.pallas import tpu as pltpu
from jax.sharding import PartitionSpec as P

DH = 64
TILE = 64
DOCS = 4


SCALE = 0.125
FLOOR_SCORE = -1e30

BF = jnp.bfloat16
F32 = jnp.float32


def expand(tile_grid, tile_edge):
    return jnp.repeat(jnp.repeat(tile_grid, tile_edge, axis=0), tile_edge, axis=1)


def attend(keys, values, queries, cotangent, length):
    position = jnp.arange(keys.shape[0])[None, :]
    live = position < length
    scores = jnp.dot(queries, keys.T, preferred_element_type=jnp.float32) * SCALE
    scores = jnp.where(live, scores, FLOOR_SCORE)
    row_max = jnp.max(scores, axis=1, keepdims=True)
    weights = jnp.where(live, jnp.exp(scores - row_max), 0.0)
    probs = weights / jnp.sum(weights, axis=1, keepdims=True)
    probs_low = probs.astype(jnp.bfloat16)
    output = jnp.dot(probs_low, values, preferred_element_type=jnp.float32)
    delta = jnp.sum(cotangent.astype(jnp.float32) * output, axis=1, keepdims=True)
    prob_grad = jnp.dot(cotangent, values.T, preferred_element_type=jnp.float32)
    score_grad = (probs * (prob_grad - delta) * SCALE).astype(jnp.bfloat16)
    query_grad = jnp.dot(score_grad, keys, preferred_element_type=jnp.float32)
    key_grad = jnp.dot(score_grad.T, queries, preferred_element_type=jnp.float32)
    value_grad = jnp.dot(probs_low.T, cotangent, preferred_element_type=jnp.float32)
    return (
        output.astype(jnp.bfloat16),
        query_grad.astype(jnp.bfloat16),
        key_grad.astype(jnp.bfloat16),
        value_grad.astype(jnp.bfloat16),
    )


def project(encoder, key_piece, value_piece):
    count = key_piece.shape[0]
    flat = encoder.reshape(DOCS * encoder.shape[1], count)
    key_flat = jnp.dot(flat, key_piece, preferred_element_type=jnp.float32)
    value_flat = jnp.dot(flat, value_piece, preferred_element_type=jnp.float32)
    shape_out = (DOCS, encoder.shape[1], key_piece.shape[1])
    return (key_flat.reshape(shape_out), value_flat.reshape(shape_out))


def back_product(key_rows, value_rows, key_piece, value_piece):
    contract = (((1,), (1,)), ((), ()))
    total = lax.dot_general(key_rows, key_piece, contract, preferred_element_type=jnp.float32)
    return total + lax.dot_general(
        value_rows, value_piece, contract, preferred_element_type=jnp.float32
    )


def general_body(encoder, key_weight, value_weight, tile_mask, lengths, queries, cotangent):
    seq_count = lax.axis_size("seq")
    enc_rows = encoder.shape[1]
    dec_rows = queries.shape[1]
    group_heads = queries.shape[2] // DH
    pair_count = DOCS * group_heads
    local_pairs = pair_count // seq_count
    key_masked = key_weight * expand(tile_mask[0], TILE).astype(jnp.bfloat16)
    value_masked = value_weight * expand(tile_mask[1], TILE).astype(jnp.bfloat16)
    full_key, full_value = (
        lax.all_gather(key_masked, "seq", axis=0, tiled=True),
        lax.all_gather(value_masked, "seq", axis=0, tiled=True),
    )
    key_sum, value_sum = project(encoder, full_key, full_value)

    def to_pairs(first, second, rows):
        joined = jnp.concatenate(
            [
                first.reshape(DOCS, rows, group_heads, DH),
                second.reshape(DOCS, rows, group_heads, DH),
            ],
            axis=3,
        )
        return joined.transpose(0, 2, 1, 3).reshape(pair_count, rows, 2 * DH)

    def from_pairs(block, rows):
        shaped = block.reshape(DOCS, group_heads, rows, 2 * DH).transpose(0, 2, 1, 3)
        first = shaped[..., :DH].reshape(DOCS, rows, group_heads * DH)
        second = shaped[..., DH:].reshape(DOCS, rows, group_heads * DH)
        return (first, second)

    query_pairs = to_pairs(queries, cotangent, dec_rows)
    query_owned = lax.all_to_all(query_pairs, "seq", split_axis=0, concat_axis=1, tiled=True)
    kv_pairs = to_pairs(key_sum.astype(jnp.bfloat16), value_sum.astype(jnp.bfloat16), enc_rows)
    kv_owned = lax.all_to_all(kv_pairs, "seq", split_axis=0, concat_axis=1, tiled=True)
    pair_ids = lax.axis_index("seq") * local_pairs + jnp.arange(local_pairs)
    doc_of_pair = pair_ids // group_heads
    pair_length = jnp.sum(
        jnp.where(doc_of_pair[:, None] == jnp.arange(DOCS)[None, :], lengths[None, :], 0), axis=1
    )

    def owner_pair(items):
        pair_kv, pair_query, length = items
        output, query_grad, key_grad, value_grad = attend(
            pair_kv[:, :DH], pair_kv[:, DH:], pair_query[:, :DH], pair_query[:, DH:], length
        )
        return (
            jnp.concatenate([output, query_grad], axis=1),
            jnp.concatenate([key_grad, value_grad], axis=1),
        )

    front, back = lax.map(owner_pair, (kv_owned, query_owned, pair_length))
    front_rows, back_rows = (
        lax.all_to_all(front, "seq", split_axis=1, concat_axis=0, tiled=True),
        lax.all_to_all(back, "seq", split_axis=1, concat_axis=0, tiled=True),
    )
    attention, query_grad = from_pairs(front_rows, dec_rows)
    key_grads, value_grads = from_pairs(back_rows, enc_rows)
    key_rows = key_grads.reshape(DOCS * enc_rows, group_heads * DH)
    value_rows = value_grads.reshape(DOCS * enc_rows, group_heads * DH)
    grad_terms = back_product(key_rows, value_rows, full_key, full_value)
    grad_share = lax.psum_scatter(grad_terms, "head", scatter_dimension=1, tiled=True)
    encoder_grad = grad_share.astype(jnp.bfloat16).reshape(DOCS, enc_rows, grad_share.shape[1])
    return (attention, query_grad, encoder_grad)


SEQ = 4
PIECE = 512


def fits(mesh, encoder, key_weight, queries):
    return (
        mesh.shape["seq"] == SEQ
        and mesh.shape["head"] == 4
        and mesh.shape["grp"] == 2
        and encoder.shape == (DOCS * 2, 256, 4096)
        and key_weight.shape == (4096, 4096)
        and queries.shape == (DOCS * 2, 64, 4096)
    )


def prune_kernel(mask_ref, key_ref, value_ref, query_ref, cot_ref, own_ref, *message_refs):
    s, g = lax.axis_index("seq"), lax.axis_index("grp")
    left = lax.broadcasted_iota(jnp.int32, (1, 128), 1) < TILE

    def write(out_ref, first_tile, tiles, column):
        for t in range(tiles):
            tile = first_tile + t
            row = pl.ds(pl.multiple_of(tile * TILE, TILE), TILE)
            for side, ref in ((0, key_ref), (1, value_ref)):
                for part in range(2):
                    at = pl.ds(pl.multiple_of(column * 256 + part * 128, 128), 128)
                    first = mask_ref[side, tile, column * 4 + part * 2]
                    second = mask_ref[side, tile, column * 4 + part * 2 + 1]
                    keep = jnp.where(left, first, second).astype(F32)
                    to = side * 256 + part * 128
                    out_ref[t * TILE : (t + 1) * TILE, to : to + 128] = (
                        ref[row, at].astype(F32) * keep
                    ).astype(BF)

    first, second, third = message_refs[:3]
    for k, ref in enumerate(message_refs[3:]):
        at = pl.ds(pl.multiple_of(lax.bitwise_xor(s, k) * 256, 256), 256)
        ref[:, 0:256] = query_ref[:, at]
        ref[:, 256:512] = cot_ref[:, at]
    write(second, g * 8, 8, lax.bitwise_xor(s, 2))
    write(first, g * 8, 8, lax.bitwise_xor(s, 1))
    write(third, g * 8, 8, lax.bitwise_xor(s, 3))
    write(own_ref, 0, 16, s)


def prune(tile_mask, key_weight, value_weight, queries, cotangent):
    whole = pl.BlockSpec(memory_space=pltpu.VMEM)
    shapes = [(2 * PIECE, 512)] + [(PIECE, 512)] * 3 + [(64, 512)] * 4
    return pl.pallas_call(
        prune_kernel,
        out_shape=[jax.ShapeDtypeStruct(shape, BF) for shape in shapes],
        in_specs=[pl.BlockSpec(memory_space=pltpu.SMEM)] + [whole] * 4,
        out_specs=[whole] * len(shapes),
        compiler_params=pltpu.CompilerParams(vmem_limit_bytes=12 * 1024 * 1024),
        name="prune",
    )(tile_mask, key_weight, value_weight, queries, cotangent)


NT = (((1,), (1,)), ((), ()))
TN = (((0,), (0,)), ((), ()))
NN = (((1,), (0,)), ((), ()))


def dot(a, b, dims=NN):
    return lax.dot_general(a, b, dims, preferred_element_type=F32)


class Mover:
    def __init__(self, sems):
        self.sems = sems
        self.used = 0

    def start(self, pairs):
        copies = []
        for src, dst in pairs:
            copy = pltpu.make_async_copy(src, dst, self.sems.at[self.used])
            copy.start()
            self.used += 1
            copies.append(copy)
        return copies


def piece_rows(w_s, core, at, first, count):
    return w_s.at[core, pl.ds(pl.multiple_of(at * 1024 + first, 256), count)]


PACKED = 3 * 2 * PIECE


def pack_kernel(own, z1, z2, y1, y2, q0, q1, q2, q3, out_ref, sems):
    g = lax.axis_index("grp")
    pairs = [(own, out_ref.at[0 : 2 * PIECE])]
    for k, z, y in ((1, z1, y1), (2, z2, y2)):
        for piece, side in ((z, g), (y, 1 - g)):
            first = pl.multiple_of(2 * PIECE * k + side * PIECE, PIECE)
            pairs.append((piece, out_ref.at[pl.ds(first, PIECE)]))
    for k, piece in enumerate((q0, q1, q2, q3)):
        first = PACKED + 64 * lax.bitwise_xor(lax.axis_index("seq"), k)
        pairs.append((piece, out_ref.at[pl.ds(pl.multiple_of(first, 64), 64)]))
    for copy in Mover(sems).start(pairs):
        copy.wait()


def pack_call(*arrays):
    here = pl.BlockSpec(memory_space=pl.ANY)
    return pl.pallas_call(
        pack_kernel,
        out_shape=jax.ShapeDtypeStruct((PACKED + 256, 512), BF),
        in_specs=[here] * len(arrays),
        out_specs=pl.BlockSpec(memory_space=pltpu.VMEM),
        scratch_shapes=[pltpu.SemaphoreType.DMA((9,))],
        compiler_params=pltpu.CompilerParams(vmem_limit_bytes=6 * 1024 * 1024),
        cost_estimate=pl.CostEstimate(flops=1, bytes_accessed=1, transcendentals=0),
        name="pack",
    )(*arrays)


def early_weights(w_s, c, s, mine, theirs):
    pairs = []
    for core, packed in ((c, mine), (1 - c, theirs)):
        for k in range(3):
            rows = packed.at[2 * PIECE * k : 2 * PIECE * (k + 1)]
            pairs.append((rows, piece_rows(w_s, core, lax.bitwise_xor(s, k), 0, 2 * PIECE)))
    return pairs


def early_kernel(*refs):
    enc, e1, e2, e3, x1, x2, x3 = refs[:7]
    mine, theirs = refs[7:9]
    sum_ref, last_ref, enc_s, w_s, sems = refs[9:]
    s, h = lax.axis_index("seq"), lax.axis_index("head")
    c = lax.rem(h, 2)
    x = h // 2
    mover = Mover(sems)

    def rows_of(doc, at):
        return enc_s.at[pl.ds(pl.multiple_of(doc * 256 + at * 64, 64), 64)]

    pairs = [(enc.at[2 * i + c], rows_of(i, s)) for i in range(2)]
    for k, (own, other) in enumerate(((e1, x1), (e2, x2), (e3, x3))):
        at = lax.bitwise_xor(s, k + 1)
        pairs += [(own, rows_of(x, at)), (other, rows_of(1 - x, at))]
    pairs += early_weights(w_s, c, s, mine, theirs)
    for copy in mover.start(pairs):
        copy.wait()

    def columns(k):
        at = lax.bitwise_xor(s, k)
        return pl.ds(pl.multiple_of(at * 1024, 1024), 1024)

    for core in range(2):
        for half in range(2):
            row = slice(half * 256, half * 256 + 256)
            total = dot(enc_s[row, columns(0)], w_s[core, columns(0), :])
            for k in (1, 2):
                total = total + dot(enc_s[row, columns(k)], w_s[core, columns(k), :])
            sum_ref[core, row] = total
    last_ref[...] = enc_s[:, columns(3)]


def early_call(arrays):
    here = pl.BlockSpec(memory_space=pl.ANY)
    vmem = pl.BlockSpec(memory_space=pltpu.VMEM)
    return pl.pallas_call(
        early_kernel,
        out_shape=[
            jax.ShapeDtypeStruct((2, 512, 512), F32),
            jax.ShapeDtypeStruct((512, 1024), BF),
        ],
        in_specs=[here] * len(arrays),
        out_specs=[vmem] * 2,
        scratch_shapes=[
            pltpu.VMEM((512, 4096), BF),
            pltpu.VMEM((2, 4096, 512), BF),
            pltpu.SemaphoreType.DMA((18,)),
        ],
        compiler_params=pltpu.CompilerParams(vmem_limit_bytes=28 * 1024 * 1024),
        cost_estimate=pl.CostEstimate(
            flops=1, bytes_accessed=1, transcendentals=0
        ),
        name="early",
    )(*arrays)


def main_kernel(lengths, *refs):
    early_sum, last_rows = refs[:2]
    mine, theirs = refs[2:5], refs[5:8]
    (
        att_ref, qg_ref, own_ref,
        a3, b3, a2, b2, b10, a10, core_ref,
        w_s, qc_s, grad_s, sems,
    ) = refs[8:]
    s, g, h = lax.axis_index("seq"), lax.axis_index("grp"), lax.axis_index("head")
    c = lax.rem(h, 2)
    mover = Mover(sems)
    far = lax.bitwise_xor(s, 3)
    pairs = []
    for core, pieces in ((c, mine), (1 - c, theirs)):
        packed, z3, y3 = pieces
        for src, side in ((z3, g), (y3, 1 - g)):
            pairs.append((src, piece_rows(w_s, core, far, side * PIECE, PIECE)))
        for d in range(SEQ):
            pairs.append((packed.at[PACKED + 64 * d : PACKED + 64 * d + 64], qc_s.at[core, d]))
    now = mover.start(pairs)
    later = mover.start(early_weights(w_s, c, s, mine[0], theirs[0]))
    for copy in now:
        copy.wait()
    far_rows = pl.ds(pl.multiple_of(far * 1024, 1024), 1024)

    row_head = lax.broadcasted_iota(jnp.int32, (256, 256), 0) // DH
    col_head = lax.broadcasted_iota(jnp.int32, (256, 256), 1) // DH
    same = row_head == col_head
    position = lax.broadcasted_iota(jnp.int32, (256, 256), 1)

    def spread(block):
        four = jnp.concatenate([block] * 4, axis=0)
        return jnp.where(same, four, jnp.zeros_like(four))

    def gather_heads(block):
        kept = jnp.where(same, block, 0.0)
        return (kept[0:64] + kept[64:128]) + (kept[128:192] + kept[192:256])

    for core in range(2):
        slot = lax.rem(core + c, 2)
        for doc in range(2):
            row = slice(doc * 256, doc * 256 + 256)
            both = early_sum[core, row] + dot(last_rows[row], w_s[core, far_rows, :])
            keys = both[:, :256].astype(BF)
            values = both[:, 256:].astype(BF)
            at = pl.ds(pl.multiple_of((2 * doc + c) * 16, 16), 16)
            query = spread(qc_s[core, :, at, 0:256].reshape(64, 256))
            cot = spread(qc_s[core, :, at, 256:512].reshape(64, 256))
            live = position < lengths[2 * doc + c]
            scores = dot(query, keys, NT) * SCALE
            scores = jnp.where(live, scores, FLOOR_SCORE)
            row_max = jnp.max(scores, axis=1, keepdims=True)
            weights = jnp.where(live, jnp.exp(scores - row_max), 0.0)
            probs = weights / jnp.sum(weights, axis=1, keepdims=True)
            low = probs.astype(BF)
            output = dot(low, values)
            delta = jnp.sum(cot.astype(F32) * output, axis=1, keepdims=True)
            prob_grad = dot(cot, values, NT)
            score_grad = (probs * (prob_grad - delta) * SCALE).astype(BF)
            query_grad = dot(score_grad, keys)
            att_ref[slot, doc] = gather_heads(output).astype(BF)
            qg_ref[slot, doc] = gather_heads(query_grad).astype(BF)
            key_grad = dot(score_grad, query, TN).astype(BF)
            value_grad = dot(low, cot, TN).astype(BF)
            for at in range(4):
                first = lax.bitwise_xor(s, at) * 128 + doc * 64
                to = pl.ds(pl.multiple_of(first, 64), 64)
                grad_s[core, to, 0:256] = key_grad[at * 64 : at * 64 + 64]
                grad_s[core, to, 256:512] = value_grad[at * 64 : at * 64 + 64]

    for copy in later:
        copy.wait()
    cores = [core_ref.at[k] for k in range(4)]
    owns = [own_ref.at[k] for k in range(4)]
    for flip, outs in (
        (2, (a10.at[1], a10.at[0], a2, a3)),
        (3, (b10.at[1], b10.at[0], b2, b3)),
        (1, cores),
        (0, owns),
    ):
        block = lax.bitwise_xor(h, flip)
        for n in range(4):
            at = pl.ds(pl.multiple_of(block * 1024 + n * 256, 256), 256)
            total = dot(grad_s[0], w_s[0, at, :], NT) + dot(grad_s[1], w_s[1, at, :], NT)
            for k in range(4):
                for doc in range(2):
                    first = k * 128 + doc * 64
                    outs[k][doc, :, n * 256 : n * 256 + 256] = total[first : first + 64].astype(
                        outs[k].dtype
                    )


def main_call(lengths, arrays):
    here = pl.BlockSpec(memory_space=pl.ANY)
    vmem = pl.BlockSpec(memory_space=pltpu.VMEM)
    smem = pl.BlockSpec(memory_space=pltpu.SMEM)
    piece = jax.ShapeDtypeStruct((2, 64, 1024), BF)
    front = jax.ShapeDtypeStruct((2, 2, 64, 256), BF)
    return pl.pallas_call(
        main_kernel,
        out_shape=[
            front,
            front,
            jax.ShapeDtypeStruct((4, 2, 64, 1024), F32),
        ]
        + [piece] * 4
        + [jax.ShapeDtypeStruct((2, 2, 64, 1024), BF)] * 2
        + [jax.ShapeDtypeStruct((4, 2, 64, 1024), BF)],
        in_specs=[smem] + [vmem] * 2 + [here] * (len(arrays) - 2),
        out_specs=[vmem] * 10,
        scratch_shapes=[
            pltpu.VMEM((2, 4096, 512), BF),
            pltpu.VMEM((2, 4, 64, 512), BF),
            pltpu.VMEM((2, 512, 512), BF),
            pltpu.SemaphoreType.DMA((26,)),
        ],
        compiler_params=pltpu.CompilerParams(vmem_limit_bytes=34 * 1024 * 1024),
        cost_estimate=pl.CostEstimate(
            flops=6 * 10**9, bytes_accessed=24 * 2**20, transcendentals=2**18
        ),
        name="attend",
    )(lengths, *arrays)


def final_kernel(own, core, near, far, near1, near2, far1, far2, out_ref):
    c = lax.rem(lax.axis_index("head"), 2)
    for i in range(2):
        mine = (own[0, i] + near[1, i].astype(F32)) + (near1[i].astype(F32) + near2[i].astype(F32))
        theirs = (core[0, i].astype(F32) + far[1, i].astype(F32)) + (
            far1[i].astype(F32) + far2[i].astype(F32)
        )
        out_ref[2 * i + c] = mine.astype(BF)
        out_ref[2 * i + 1 - c] = theirs.astype(BF)


def small_call(kernel, shape, name, *arrays):
    vmem = pl.BlockSpec(memory_space=pltpu.VMEM)
    return pl.pallas_call(
        kernel,
        out_shape=jax.ShapeDtypeStruct(shape, BF),
        in_specs=[vmem] * len(arrays),
        out_specs=vmem,
        compiler_params=pltpu.CompilerParams(vmem_limit_bytes=12 * 1024 * 1024),
        name=name,
    )(*arrays)


def together(*values):
    return lax.optimization_barrier(values)


def summed(*parts):
    total = parts[0].astype(F32)
    for part in parts[1:]:
        total = total + part.astype(F32)
    return total.astype(BF)


def body(encoder, key_weight, value_weight, tile_mask, lengths, queries, cotangent):
    h = lax.axis_index("head")
    c = lax.rem(h, 2)

    def along(value, k):
        return lax.ppermute(value, "seq", [(a, a ^ k) for a in range(SEQ)])

    def flip(value, bits):
        return lax.ppermute(value, "head", [(a, a ^ bits) for a in range(4)])

    def across(value):
        return lax.ppermute(value, "grp", [(0, 1), (1, 0)])

    e0 = lax.dynamic_index_in_dim(encoder, h, 0, keepdims=False)
    e2 = along(e0, 2)
    e1 = along(e0, 1)
    w_own, m1, m2, m3, q0, q1, q2, q3 = prune(
        tile_mask, key_weight, value_weight, queries.reshape(64, 1024), cotangent.reshape(64, 1024)
    )
    e1, e2, m1, m2 = together(e1, e2, m1, m2)
    z2, z1 = along(m2, 2), along(m1, 1)
    e3 = along(e2, 1)
    x1, x2 = flip(e1, 2), flip(e2, 2)
    x1, x2, m3, q1, q2, q3 = together(x1, x2, m3, q1, q2, q3)
    z3 = along(m3, 3)
    q1, q2, q3 = along(q1, 1), along(q2, 2), along(q3, 3)
    x1, z2 = together(x1, z2)
    x2, e3 = together(x2, e3)
    y2 = across(z2)
    x3 = flip(e3, 2)
    y2, z1 = together(y2, z1)
    y1 = across(z1)
    z3, x3, w_own = together(z3, x3, w_own)
    y3 = across(z3)
    packed = pack_call(w_own, z1, z2, y1, y2, q0, q1, q2, q3)
    packed_there = flip(packed, 1)
    early = early_call([encoder, e1, e2, e3, x1, x2, x3, packed, packed_there])
    z3_there = flip(z3, 1)
    y3, *early = together(y3, *early)
    y3_there = flip(y3, 1)
    outs = main_call(lengths, early + [packed, z3, y3, packed_there, z3_there, y3_there])
    att, qgrad, own = outs[:3]
    a3, b3, a2, b2, b10, a10, to_core = outs[3:]
    from_core = flip(to_core, 1)
    front = jnp.stack([att, qgrad], axis=1)
    other = flip(front[1], 1)
    back = jnp.stack([front[0], other]).reshape(2, 2, 2, SEQ, 16, 256).transpose(3, 0, 1, 2, 4, 5)
    b3, a3 = flip(b3, 3), flip(a3, 2)
    b3, core, b2, a2, back = together(b3, from_core, b2, a2, back)
    back = lax.all_to_all(back, "seq", split_axis=0, concat_axis=0, tiled=True)
    b2, a2 = flip(b2, 3), flip(a2, 2)
    far3, own = together(summed(core[3], b3), own)
    far3 = along(far3, 1)
    near3, core = together(summed(own[3], a3), core)
    near3 = along(near3, 1)
    b2, b10, a10 = together(b2, b10, a10)
    b10, a10 = flip(b10, 3), flip(a10, 2)
    core, back = together(core, back)
    far2, own = together(summed(core[2], b2, far3), own)
    far2 = along(far2, 2)
    near2, core = together(summed(own[2], a2, near3), core)
    near2 = along(near2, 2)
    near1, core = together(summed(own[1], a10[0]), core)
    near1 = along(near1, 1)
    b10, near2, far2 = together(b10, near2, far2)
    far1 = along(summed(core[1], b10[0]), 1)
    from_core = core
    back = back.transpose(2, 3, 1, 4, 0, 5).reshape(2, 2, 2, 16, 1024)
    back = jnp.where(c == 0, back, back[:, :, ::-1])
    back = back.reshape(2, DOCS, 16, 1024)
    a10, back = together(a10, back)
    encoder_grad = small_call(
        final_kernel, (DOCS, 64, 1024), "final", own, from_core, a10, b10, near1, near2, far1, far2
    )
    return (back[0], back[1], encoder_grad)


def solution(mesh):
    placed = (
        P("grp", "seq", None),
        P("seq", "head"),
        P("seq", "head"),
        P(None, "seq", "head"),
        P("grp"),
        P("grp", "seq", "head"),
        P("grp", "seq", "head"),
    )

    def step(*arrays):
        plan = body if fits(mesh, arrays[0], arrays[1], arrays[5]) else general_body
        return jax.shard_map(
            plan,
            mesh=mesh,
            in_specs=placed,
            out_specs=(P("grp", "seq", "head"),) * 3,
            check_vma=False,
        )(*arrays)

    return step
```

```python
import functools

import jax
import jax.numpy as jnp
from jax import lax
from jax.experimental import pallas as pl
from jax.experimental.pallas import tpu as pltpu
from jax.sharding import PartitionSpec as P

DH = 64
TILE = 64
DOCS = 4


SCALE = 0.125
FLOOR_SCORE = -1e30

BF = jnp.bfloat16
F32 = jnp.float32


def expand(tile_grid, tile_edge):
    return jnp.repeat(jnp.repeat(tile_grid, tile_edge, axis=0), tile_edge, axis=1)


def attend(keys, values, queries, cotangent, length):
    position = jnp.arange(keys.shape[0])[None, :]
    live = position < length
    scores = jnp.dot(queries, keys.T, preferred_element_type=jnp.float32) * SCALE
    scores = jnp.where(live, scores, FLOOR_SCORE)
    row_max = jnp.max(scores, axis=1, keepdims=True)
    weights = jnp.where(live, jnp.exp(scores - row_max), 0.0)
    probs = weights / jnp.sum(weights, axis=1, keepdims=True)
    probs_low = probs.astype(jnp.bfloat16)
    output = jnp.dot(probs_low, values, preferred_element_type=jnp.float32)
    delta = jnp.sum(cotangent.astype(jnp.float32) * output, axis=1, keepdims=True)
    prob_grad = jnp.dot(cotangent, values.T, preferred_element_type=jnp.float32)
    score_grad = (probs * (prob_grad - delta) * SCALE).astype(jnp.bfloat16)
    query_grad = jnp.dot(score_grad, keys, preferred_element_type=jnp.float32)
    key_grad = jnp.dot(score_grad.T, queries, preferred_element_type=jnp.float32)
    value_grad = jnp.dot(probs_low.T, cotangent, preferred_element_type=jnp.float32)
    return (
        output.astype(jnp.bfloat16),
        query_grad.astype(jnp.bfloat16),
        key_grad.astype(jnp.bfloat16),
        value_grad.astype(jnp.bfloat16),
    )


def project(encoder, key_piece, value_piece):
    count = key_piece.shape[0]
    flat = encoder.reshape(DOCS * encoder.shape[1], count)
    key_flat = jnp.dot(flat, key_piece, preferred_element_type=jnp.float32)
    value_flat = jnp.dot(flat, value_piece, preferred_element_type=jnp.float32)
    shape_out = (DOCS, encoder.shape[1], key_piece.shape[1])
    return (key_flat.reshape(shape_out), value_flat.reshape(shape_out))


def back_product(key_rows, value_rows, key_piece, value_piece):
    contract = (((1,), (1,)), ((), ()))
    total = lax.dot_general(key_rows, key_piece, contract, preferred_element_type=jnp.float32)
    return total + lax.dot_general(
        value_rows, value_piece, contract, preferred_element_type=jnp.float32
    )


def general_body(encoder, key_weight, value_weight, tile_mask, lengths, queries, cotangent):
    seq_count = lax.axis_size("seq")
    enc_rows = encoder.shape[1]
    dec_rows = queries.shape[1]
    group_heads = queries.shape[2] // DH
    pair_count = DOCS * group_heads
    local_pairs = pair_count // seq_count
    key_masked = key_weight * expand(tile_mask[0], TILE).astype(jnp.bfloat16)
    value_masked = value_weight * expand(tile_mask[1], TILE).astype(jnp.bfloat16)
    full_key, full_value = (
        lax.all_gather(key_masked, "seq", axis=0, tiled=True),
        lax.all_gather(value_masked, "seq", axis=0, tiled=True),
    )
    key_sum, value_sum = project(encoder, full_key, full_value)

    def to_pairs(first, second, rows):
        joined = jnp.concatenate(
            [
                first.reshape(DOCS, rows, group_heads, DH),
                second.reshape(DOCS, rows, group_heads, DH),
            ],
            axis=3,
        )
        return joined.transpose(0, 2, 1, 3).reshape(pair_count, rows, 2 * DH)

    def from_pairs(block, rows):
        shaped = block.reshape(DOCS, group_heads, rows, 2 * DH).transpose(0, 2, 1, 3)
        first = shaped[..., :DH].reshape(DOCS, rows, group_heads * DH)
        second = shaped[..., DH:].reshape(DOCS, rows, group_heads * DH)
        return (first, second)

    query_pairs = to_pairs(queries, cotangent, dec_rows)
    query_owned = lax.all_to_all(query_pairs, "seq", split_axis=0, concat_axis=1, tiled=True)
    kv_pairs = to_pairs(key_sum.astype(jnp.bfloat16), value_sum.astype(jnp.bfloat16), enc_rows)
    kv_owned = lax.all_to_all(kv_pairs, "seq", split_axis=0, concat_axis=1, tiled=True)
    pair_ids = lax.axis_index("seq") * local_pairs + jnp.arange(local_pairs)
    doc_of_pair = pair_ids // group_heads
    pair_length = jnp.sum(
        jnp.where(doc_of_pair[:, None] == jnp.arange(DOCS)[None, :], lengths[None, :], 0), axis=1
    )

    def owner_pair(items):
        pair_kv, pair_query, length = items
        output, query_grad, key_grad, value_grad = attend(
            pair_kv[:, :DH], pair_kv[:, DH:], pair_query[:, :DH], pair_query[:, DH:], length
        )
        return (
            jnp.concatenate([output, query_grad], axis=1),
            jnp.concatenate([key_grad, value_grad], axis=1),
        )

    front, back = lax.map(owner_pair, (kv_owned, query_owned, pair_length))
    front_rows, back_rows = (
        lax.all_to_all(front, "seq", split_axis=1, concat_axis=0, tiled=True),
        lax.all_to_all(back, "seq", split_axis=1, concat_axis=0, tiled=True),
    )
    attention, query_grad = from_pairs(front_rows, dec_rows)
    key_grads, value_grads = from_pairs(back_rows, enc_rows)
    key_rows = key_grads.reshape(DOCS * enc_rows, group_heads * DH)
    value_rows = value_grads.reshape(DOCS * enc_rows, group_heads * DH)
    grad_terms = back_product(key_rows, value_rows, full_key, full_value)
    grad_share = lax.psum_scatter(grad_terms, "head", scatter_dimension=1, tiled=True)
    encoder_grad = grad_share.astype(jnp.bfloat16).reshape(DOCS, enc_rows, grad_share.shape[1])
    return (attention, query_grad, encoder_grad)


SEQ = 4
PIECE = 512


def fits(mesh, encoder, key_weight, queries):
    return (
        mesh.shape["seq"] == SEQ
        and mesh.shape["head"] == 4
        and mesh.shape["grp"] == 2
        and encoder.shape == (DOCS * 2, 256, 4096)
        and key_weight.shape == (4096, 4096)
        and queries.shape == (DOCS * 2, 64, 4096)
    )


def prune_kernel(mask_ref, key_ref, value_ref, query_ref, cot_ref, own_ref, *message_refs):
    s, g = lax.axis_index("seq"), lax.axis_index("grp")
    left = lax.broadcasted_iota(jnp.int32, (1, 128), 1) < TILE

    def write(out_ref, first_tile, tiles, column):
        for t in range(tiles):
            tile = first_tile + t
            row = pl.ds(pl.multiple_of(tile * TILE, TILE), TILE)
            for side, ref in ((0, key_ref), (1, value_ref)):
                for part in range(2):
                    at = pl.ds(pl.multiple_of(column * 256 + part * 128, 128), 128)
                    first = mask_ref[side, tile, column * 4 + part * 2]
                    second = mask_ref[side, tile, column * 4 + part * 2 + 1]
                    keep = jnp.where(left, first, second).astype(F32)
                    to = side * 256 + part * 128
                    out_ref[t * TILE : (t + 1) * TILE, to : to + 128] = (
                        ref[row, at].astype(F32) * keep
                    ).astype(BF)

    first, second, third = message_refs[:3]
    for k, ref in enumerate(message_refs[3:]):
        at = pl.ds(pl.multiple_of(lax.bitwise_xor(s, k) * 256, 256), 256)
        ref[:, 0:256] = query_ref[:, at]
        ref[:, 256:512] = cot_ref[:, at]
    write(second, g * 8, 8, lax.bitwise_xor(s, 2))
    write(first, g * 8, 8, lax.bitwise_xor(s, 1))
    write(third, g * 8, 8, lax.bitwise_xor(s, 3))
    write(own_ref, 0, 16, s)


def prune(tile_mask, key_weight, value_weight, queries, cotangent):
    whole = pl.BlockSpec(memory_space=pltpu.VMEM)
    shapes = [(2 * PIECE, 512)] + [(PIECE, 512)] * 3 + [(64, 512)] * 4
    return pl.pallas_call(
        prune_kernel,
        out_shape=[jax.ShapeDtypeStruct(shape, BF) for shape in shapes],
        in_specs=[pl.BlockSpec(memory_space=pltpu.SMEM)] + [whole] * 4,
        out_specs=[whole] * len(shapes),
        compiler_params=pltpu.CompilerParams(vmem_limit_bytes=12 * 1024 * 1024),
        name="prune",
    )(tile_mask, key_weight, value_weight, queries, cotangent)


NT = (((1,), (1,)), ((), ()))
TN = (((0,), (0,)), ((), ()))
NN = (((1,), (0,)), ((), ()))


def dot(a, b, dims=NN):
    return lax.dot_general(a, b, dims, preferred_element_type=F32)


class Mover:
    def __init__(self, sems):
        self.sems = sems
        self.used = 0

    def start(self, pairs):
        copies = []
        for src, dst in pairs:
            copy = pltpu.make_async_copy(src, dst, self.sems.at[self.used])
            copy.start()
            self.used += 1
            copies.append(copy)
        return copies


def piece_rows(w_s, core, at, first, count):
    return w_s.at[core, pl.ds(pl.multiple_of(at * 1024 + first, 256), count)]


PACKED = 3 * 2 * PIECE


def pack_kernel(own, z1, z2, y1, y2, q0, q1, q2, q3, out_ref, sems):
    g = lax.axis_index("grp")
    pairs = [(own, out_ref.at[0 : 2 * PIECE])]
    for k, z, y in ((1, z1, y1), (2, z2, y2)):
        for piece, side in ((z, g), (y, 1 - g)):
            first = pl.multiple_of(2 * PIECE * k + side * PIECE, PIECE)
            pairs.append((piece, out_ref.at[pl.ds(first, PIECE)]))
    for k, piece in enumerate((q0, q1, q2, q3)):
        first = PACKED + 64 * lax.bitwise_xor(lax.axis_index("seq"), k)
        pairs.append((piece, out_ref.at[pl.ds(pl.multiple_of(first, 64), 64)]))
    for copy in Mover(sems).start(pairs):
        copy.wait()


def pack_call(*arrays):
    here = pl.BlockSpec(memory_space=pl.ANY)
    return pl.pallas_call(
        pack_kernel,
        out_shape=jax.ShapeDtypeStruct((PACKED + 256, 512), BF),
        in_specs=[here] * len(arrays),
        out_specs=pl.BlockSpec(memory_space=pltpu.VMEM),
        scratch_shapes=[pltpu.SemaphoreType.DMA((9,))],
        compiler_params=pltpu.CompilerParams(vmem_limit_bytes=6 * 1024 * 1024),
        cost_estimate=pl.CostEstimate(flops=1, bytes_accessed=1, transcendentals=0),
        name="pack",
    )(*arrays)


def early_weights(w_s, c, s, mine, theirs):
    pairs = []
    for core, packed in ((c, mine), (1 - c, theirs)):
        for k in range(3):
            rows = packed.at[2 * PIECE * k : 2 * PIECE * (k + 1)]
            pairs.append((rows, piece_rows(w_s, core, lax.bitwise_xor(s, k), 0, 2 * PIECE)))
    return pairs


def early_kernel(*refs):
    enc, e1, e2, e3, x1, x2, x3 = refs[:7]
    mine, theirs = refs[7:9]
    sum_ref, last_ref, enc_s, w_s, sems = refs[9:]
    s, h = lax.axis_index("seq"), lax.axis_index("head")
    c = lax.rem(h, 2)
    x = h // 2
    mover = Mover(sems)

    def rows_of(doc, at):
        return enc_s.at[pl.ds(pl.multiple_of(doc * 256 + at * 64, 64), 64)]

    pairs = [(enc.at[2 * i + c], rows_of(i, s)) for i in range(2)]
    for k, (own, other) in enumerate(((e1, x1), (e2, x2), (e3, x3))):
        at = lax.bitwise_xor(s, k + 1)
        pairs += [(own, rows_of(x, at)), (other, rows_of(1 - x, at))]
    pairs += early_weights(w_s, c, s, mine, theirs)
    for copy in mover.start(pairs):
        copy.wait()

    def columns(k):
        at = lax.bitwise_xor(s, k)
        return pl.ds(pl.multiple_of(at * 1024, 1024), 1024)

    for core in range(2):
        for half in range(2):
            row = slice(half * 256, half * 256 + 256)
            total = dot(enc_s[row, columns(0)], w_s[core, columns(0), :])
            for k in (1, 2):
                total = total + dot(enc_s[row, columns(k)], w_s[core, columns(k), :])
            sum_ref[core, row] = total
    last_ref[...] = enc_s[:, columns(3)]


def early_call(arrays):
    here = pl.BlockSpec(memory_space=pl.ANY)
    vmem = pl.BlockSpec(memory_space=pltpu.VMEM)
    return pl.pallas_call(
        early_kernel,
        out_shape=[
            jax.ShapeDtypeStruct((2, 512, 512), F32),
            jax.ShapeDtypeStruct((512, 1024), BF),
        ],
        in_specs=[here] * len(arrays),
        out_specs=[vmem] * 2,
        scratch_shapes=[
            pltpu.VMEM((512, 4096), BF),
            pltpu.VMEM((2, 4096, 512), BF),
            pltpu.SemaphoreType.DMA((18,)),
        ],
        compiler_params=pltpu.CompilerParams(vmem_limit_bytes=28 * 1024 * 1024),
        cost_estimate=pl.CostEstimate(
            flops=1, bytes_accessed=1, transcendentals=0
        ),
        name="early",
    )(*arrays)


def main_kernel(lengths, *refs):
    early_sum, last_rows = refs[:2]
    mine, theirs = refs[2:5], refs[5:8]
    (
        att_ref, qg_ref, own_ref,
        a3, b3, a2, b2, b10, a10, core_ref,
        w_s, qc_s, grad_s, sems,
    ) = refs[8:]
    s, g, h = lax.axis_index("seq"), lax.axis_index("grp"), lax.axis_index("head")
    c = lax.rem(h, 2)
    mover = Mover(sems)
    far = lax.bitwise_xor(s, 3)
    pairs = []
    for core, pieces in ((c, mine), (1 - c, theirs)):
        packed, z3, y3 = pieces
        for src, side in ((z3, g), (y3, 1 - g)):
            pairs.append((src, piece_rows(w_s, core, far, side * PIECE, PIECE)))
        for d in range(SEQ):
            pairs.append((packed.at[PACKED + 64 * d : PACKED + 64 * d + 64], qc_s.at[core, d]))
    now = mover.start(pairs)
    later = mover.start(early_weights(w_s, c, s, mine[0], theirs[0]))
    for copy in now:
        copy.wait()
    far_rows = pl.ds(pl.multiple_of(far * 1024, 1024), 1024)

    row_head = lax.broadcasted_iota(jnp.int32, (256, 256), 0) // DH
    col_head = lax.broadcasted_iota(jnp.int32, (256, 256), 1) // DH
    same = row_head == col_head
    position = lax.broadcasted_iota(jnp.int32, (256, 256), 1)

    def spread(block):
        four = jnp.concatenate([block] * 4, axis=0)
        return jnp.where(same, four, jnp.zeros_like(four))

    def gather_heads(block):
        kept = jnp.where(same, block, 0.0)
        return (kept[0:64] + kept[64:128]) + (kept[128:192] + kept[192:256])

    for core in range(2):
        slot = lax.rem(core + c, 2)
        for doc in range(2):
            row = slice(doc * 256, doc * 256 + 256)
            both = early_sum[core, row] + dot(last_rows[row], w_s[core, far_rows, :])
            keys = both[:, :256].astype(BF)
            values = both[:, 256:].astype(BF)
            at = pl.ds(pl.multiple_of((2 * doc + c) * 16, 16), 16)
            query = spread(qc_s[core, :, at, 0:256].reshape(64, 256))
            cot = spread(qc_s[core, :, at, 256:512].reshape(64, 256))
            live = position < lengths[2 * doc + c]
            scores = dot(query, keys, NT) * SCALE
            scores = jnp.where(live, scores, FLOOR_SCORE)
            row_max = jnp.max(scores, axis=1, keepdims=True)
            weights = jnp.where(live, jnp.exp(scores - row_max), 0.0)
            probs = weights / jnp.sum(weights, axis=1, keepdims=True)
            low = probs.astype(BF)
            output = dot(low, values)
            delta = jnp.sum(cot.astype(F32) * output, axis=1, keepdims=True)
            prob_grad = dot(cot, values, NT)
            score_grad = (probs * (prob_grad - delta) * SCALE).astype(BF)
            query_grad = dot(score_grad, keys)
            att_ref[slot, doc] = gather_heads(output).astype(BF)
            qg_ref[slot, doc] = gather_heads(query_grad).astype(BF)
            key_grad = dot(score_grad, query, TN).astype(BF)
            value_grad = dot(low, cot, TN).astype(BF)
            for at in range(4):
                first = lax.bitwise_xor(s, at) * 128 + doc * 64
                to = pl.ds(pl.multiple_of(first, 64), 64)
                grad_s[core, to, 0:256] = key_grad[at * 64 : at * 64 + 64]
                grad_s[core, to, 256:512] = value_grad[at * 64 : at * 64 + 64]

    for copy in later:
        copy.wait()
    cores = [core_ref.at[k] for k in range(4)]
    owns = [own_ref.at[k] for k in range(4)]
    for flip, outs in (
        (2, (a10.at[1], a10.at[0], a2, a3)),
        (3, (b10.at[1], b10.at[0], b2, b3)),
        (1, cores),
        (0, owns),
    ):
        block = lax.bitwise_xor(h, flip)
        for n in range(4):
            at = pl.ds(pl.multiple_of(block * 1024 + n * 256, 256), 256)
            total = dot(grad_s[0], w_s[0, at, :], NT) + dot(grad_s[1], w_s[1, at, :], NT)
            for k in range(4):
                for doc in range(2):
                    first = k * 128 + doc * 64
                    outs[k][doc, :, n * 256 : n * 256 + 256] = total[first : first + 64].astype(
                        outs[k].dtype
                    )


def main_call(lengths, arrays):
    here = pl.BlockSpec(memory_space=pl.ANY)
    vmem = pl.BlockSpec(memory_space=pltpu.VMEM)
    smem = pl.BlockSpec(memory_space=pltpu.SMEM)
    piece = jax.ShapeDtypeStruct((2, 64, 1024), BF)
    front = jax.ShapeDtypeStruct((2, 2, 64, 256), BF)
    return pl.pallas_call(
        main_kernel,
        out_shape=[
            front,
            front,
            jax.ShapeDtypeStruct((4, 2, 64, 1024), F32),
        ]
        + [piece] * 4
        + [jax.ShapeDtypeStruct((2, 2, 64, 1024), BF)] * 2
        + [jax.ShapeDtypeStruct((4, 2, 64, 1024), BF)],
        in_specs=[smem] + [vmem] * 2 + [here] * (len(arrays) - 2),
        out_specs=[vmem] * 10,
        scratch_shapes=[
            pltpu.VMEM((2, 4096, 512), BF),
            pltpu.VMEM((2, 4, 64, 512), BF),
            pltpu.VMEM((2, 512, 512), BF),
            pltpu.SemaphoreType.DMA((26,)),
        ],
        compiler_params=pltpu.CompilerParams(vmem_limit_bytes=34 * 1024 * 1024),
        cost_estimate=pl.CostEstimate(
            flops=6 * 10**9, bytes_accessed=24 * 2**20, transcendentals=2**18
        ),
        name="attend",
    )(lengths, *arrays)


def final_kernel(own, core, near, far, near1, near2, far1, far2, out_ref):
    c = lax.rem(lax.axis_index("head"), 2)
    for i in range(2):
        mine = (own[0, i] + near[1, i].astype(F32)) + (near1[i].astype(F32) + near2[i].astype(F32))
        theirs = (core[0, i].astype(F32) + far[1, i].astype(F32)) + (
            far1[i].astype(F32) + far2[i].astype(F32)
        )
        out_ref[2 * i + c] = mine.astype(BF)
        out_ref[2 * i + 1 - c] = theirs.astype(BF)


def small_call(kernel, shape, name, *arrays):
    vmem = pl.BlockSpec(memory_space=pltpu.VMEM)
    return pl.pallas_call(
        kernel,
        out_shape=jax.ShapeDtypeStruct(shape, BF),
        in_specs=[vmem] * len(arrays),
        out_specs=vmem,
        compiler_params=pltpu.CompilerParams(vmem_limit_bytes=12 * 1024 * 1024),
        name=name,
    )(*arrays)


def together(*values):
    return lax.optimization_barrier(values)


def summed(*parts):
    total = parts[0].astype(F32)
    for part in parts[1:]:
        total = total + part.astype(F32)
    return total.astype(BF)


def body(encoder, key_weight, value_weight, tile_mask, lengths, queries, cotangent):
    h = lax.axis_index("head")
    c = lax.rem(h, 2)

    def along(value, k):
        return lax.ppermute(value, "seq", [(a, a ^ k) for a in range(SEQ)])

    def flip(value, bits):
        return lax.ppermute(value, "head", [(a, a ^ bits) for a in range(4)])

    def across(value):
        return lax.ppermute(value, "grp", [(0, 1), (1, 0)])

    e0 = lax.dynamic_index_in_dim(encoder, h, 0, keepdims=False)
    e2 = along(e0, 2)
    e1 = along(e0, 1)
    w_own, m1, m2, m3, q0, q1, q2, q3 = prune(
        tile_mask, key_weight, value_weight, queries.reshape(64, 1024), cotangent.reshape(64, 1024)
    )
    e1, e2, m1, m2 = together(e1, e2, m1, m2)
    z2, z1 = along(m2, 2), along(m1, 1)
    x1, x2 = flip(e1, 2), flip(e2, 2)
    x1, e2 = together(x1, e2)
    e3 = along(e2, 1)
    x1, x2, m3, q1, q2, q3 = together(x1, x2, m3, q1, q2, q3)
    z3 = along(m3, 3)
    q1, q2, q3 = along(q1, 1), along(q2, 2), along(q3, 3)
    x1, z2 = together(x1, z2)
    x2, e3 = together(x2, e3)
    y2 = across(z2)
    x3 = flip(e3, 2)
    y2, z1 = together(y2, z1)
    y1 = across(z1)
    z3, x3, w_own = together(z3, x3, w_own)
    y3 = across(z3)
    packed = pack_call(w_own, z1, z2, y1, y2, q0, q1, q2, q3)
    packed_there = flip(packed, 1)
    early = early_call([encoder, e1, e2, e3, x1, x2, x3, packed, packed_there])
    z3_there = flip(z3, 1)
    y3, *early = together(y3, *early)
    y3_there = flip(y3, 1)
    outs = main_call(lengths, early + [packed, z3, y3, packed_there, z3_there, y3_there])
    att, qgrad, own = outs[:3]
    a3, b3, a2, b2, b10, a10, to_core = outs[3:]
    from_core = flip(to_core, 1)
    front = jnp.stack([att, qgrad], axis=1)
    other = flip(front[1], 1)
    back = jnp.stack([front[0], other]).reshape(2, 2, 2, SEQ, 16, 256).transpose(3, 0, 1, 2, 4, 5)
    b3, a3 = flip(b3, 3), flip(a3, 2)
    b3, core, b2, a2, back = together(b3, from_core, b2, a2, back)
    back = lax.all_to_all(back, "seq", split_axis=0, concat_axis=0, tiled=True)
    b2, a2 = flip(b2, 3), flip(a2, 2)
    far3, own = together(summed(core[3], b3), own)
    far3 = along(far3, 1)
    near3, core = together(summed(own[3], a3), core)
    near3 = along(near3, 1)
    b2, b10, a10 = together(b2, b10, a10)
    b10, a10 = flip(b10, 3), flip(a10, 2)
    core, back = together(core, back)
    far2, own = together(summed(core[2], b2, far3), own)
    far2 = along(far2, 2)
    near2, core = together(summed(own[2], a2, near3), core)
    near2 = along(near2, 2)
    near1, core = together(summed(own[1], a10[0]), core)
    near1 = along(near1, 1)
    b10, near2, far2 = together(b10, near2, far2)
    far1 = along(summed(core[1], b10[0]), 1)
    from_core = core
    back = back.transpose(2, 3, 1, 4, 0, 5).reshape(2, 2, 2, 16, 1024)
    back = jnp.where(c == 0, back, back[:, :, ::-1])
    back = back.reshape(2, DOCS, 16, 1024)
    a10, back = together(a10, back)
    encoder_grad = small_call(
        final_kernel, (DOCS, 64, 1024), "final", own, from_core, a10, b10, near1, near2, far1, far2
    )
    return (back[0], back[1], encoder_grad)


def solution(mesh):
    placed = (
        P("grp", "seq", None),
        P("seq", "head"),
        P("seq", "head"),
        P(None, "seq", "head"),
        P("grp"),
        P("grp", "seq", "head"),
        P("grp", "seq", "head"),
    )

    def step(*arrays):
        plan = body if fits(mesh, arrays[0], arrays[1], arrays[5]) else general_body
        return jax.shard_map(
            plan,
            mesh=mesh,
            in_specs=placed,
            out_specs=(P("grp", "seq", "head"),) * 3,
            check_vma=False,
        )(*arrays)

    return step
```

```python
import functools

import jax
import jax.numpy as jnp
from jax import lax
from jax.experimental import pallas as pl
from jax.experimental.pallas import tpu as pltpu
from jax.sharding import PartitionSpec as P

DH = 64
TILE = 64
DOCS = 4


SCALE = 0.125
FLOOR_SCORE = -1e30

BF = jnp.bfloat16
F32 = jnp.float32


def expand(tile_grid, tile_edge):
    return jnp.repeat(jnp.repeat(tile_grid, tile_edge, axis=0), tile_edge, axis=1)


def attend(keys, values, queries, cotangent, length):
    position = jnp.arange(keys.shape[0])[None, :]
    live = position < length
    scores = jnp.dot(queries, keys.T, preferred_element_type=jnp.float32) * SCALE
    scores = jnp.where(live, scores, FLOOR_SCORE)
    row_max = jnp.max(scores, axis=1, keepdims=True)
    weights = jnp.where(live, jnp.exp(scores - row_max), 0.0)
    probs = weights / jnp.sum(weights, axis=1, keepdims=True)
    probs_low = probs.astype(jnp.bfloat16)
    output = jnp.dot(probs_low, values, preferred_element_type=jnp.float32)
    delta = jnp.sum(cotangent.astype(jnp.float32) * output, axis=1, keepdims=True)
    prob_grad = jnp.dot(cotangent, values.T, preferred_element_type=jnp.float32)
    score_grad = (probs * (prob_grad - delta) * SCALE).astype(jnp.bfloat16)
    query_grad = jnp.dot(score_grad, keys, preferred_element_type=jnp.float32)
    key_grad = jnp.dot(score_grad.T, queries, preferred_element_type=jnp.float32)
    value_grad = jnp.dot(probs_low.T, cotangent, preferred_element_type=jnp.float32)
    return (
        output.astype(jnp.bfloat16),
        query_grad.astype(jnp.bfloat16),
        key_grad.astype(jnp.bfloat16),
        value_grad.astype(jnp.bfloat16),
    )


def project(encoder, key_piece, value_piece):
    count = key_piece.shape[0]
    flat = encoder.reshape(DOCS * encoder.shape[1], count)
    key_flat = jnp.dot(flat, key_piece, preferred_element_type=jnp.float32)
    value_flat = jnp.dot(flat, value_piece, preferred_element_type=jnp.float32)
    shape_out = (DOCS, encoder.shape[1], key_piece.shape[1])
    return (key_flat.reshape(shape_out), value_flat.reshape(shape_out))


def back_product(key_rows, value_rows, key_piece, value_piece):
    contract = (((1,), (1,)), ((), ()))
    total = lax.dot_general(key_rows, key_piece, contract, preferred_element_type=jnp.float32)
    return total + lax.dot_general(
        value_rows, value_piece, contract, preferred_element_type=jnp.float32
    )


def general_body(encoder, key_weight, value_weight, tile_mask, lengths, queries, cotangent):
    seq_count = lax.axis_size("seq")
    enc_rows = encoder.shape[1]
    dec_rows = queries.shape[1]
    group_heads = queries.shape[2] // DH
    pair_count = DOCS * group_heads
    local_pairs = pair_count // seq_count
    key_masked = key_weight * expand(tile_mask[0], TILE).astype(jnp.bfloat16)
    value_masked = value_weight * expand(tile_mask[1], TILE).astype(jnp.bfloat16)
    full_key, full_value = (
        lax.all_gather(key_masked, "seq", axis=0, tiled=True),
        lax.all_gather(value_masked, "seq", axis=0, tiled=True),
    )
    key_sum, value_sum = project(encoder, full_key, full_value)

    def to_pairs(first, second, rows):
        joined = jnp.concatenate(
            [
                first.reshape(DOCS, rows, group_heads, DH),
                second.reshape(DOCS, rows, group_heads, DH),
            ],
            axis=3,
        )
        return joined.transpose(0, 2, 1, 3).reshape(pair_count, rows, 2 * DH)

    def from_pairs(block, rows):
        shaped = block.reshape(DOCS, group_heads, rows, 2 * DH).transpose(0, 2, 1, 3)
        first = shaped[..., :DH].reshape(DOCS, rows, group_heads * DH)
        second = shaped[..., DH:].reshape(DOCS, rows, group_heads * DH)
        return (first, second)

    query_pairs = to_pairs(queries, cotangent, dec_rows)
    query_owned = lax.all_to_all(query_pairs, "seq", split_axis=0, concat_axis=1, tiled=True)
    kv_pairs = to_pairs(key_sum.astype(jnp.bfloat16), value_sum.astype(jnp.bfloat16), enc_rows)
    kv_owned = lax.all_to_all(kv_pairs, "seq", split_axis=0, concat_axis=1, tiled=True)
    pair_ids = lax.axis_index("seq") * local_pairs + jnp.arange(local_pairs)
    doc_of_pair = pair_ids // group_heads
    pair_length = jnp.sum(
        jnp.where(doc_of_pair[:, None] == jnp.arange(DOCS)[None, :], lengths[None, :], 0), axis=1
    )

    def owner_pair(items):
        pair_kv, pair_query, length = items
        output, query_grad, key_grad, value_grad = attend(
            pair_kv[:, :DH], pair_kv[:, DH:], pair_query[:, :DH], pair_query[:, DH:], length
        )
        return (
            jnp.concatenate([output, query_grad], axis=1),
            jnp.concatenate([key_grad, value_grad], axis=1),
        )

    front, back = lax.map(owner_pair, (kv_owned, query_owned, pair_length))
    front_rows, back_rows = (
        lax.all_to_all(front, "seq", split_axis=1, concat_axis=0, tiled=True),
        lax.all_to_all(back, "seq", split_axis=1, concat_axis=0, tiled=True),
    )
    attention, query_grad = from_pairs(front_rows, dec_rows)
    key_grads, value_grads = from_pairs(back_rows, enc_rows)
    key_rows = key_grads.reshape(DOCS * enc_rows, group_heads * DH)
    value_rows = value_grads.reshape(DOCS * enc_rows, group_heads * DH)
    grad_terms = back_product(key_rows, value_rows, full_key, full_value)
    grad_share = lax.psum_scatter(grad_terms, "head", scatter_dimension=1, tiled=True)
    encoder_grad = grad_share.astype(jnp.bfloat16).reshape(DOCS, enc_rows, grad_share.shape[1])
    return (attention, query_grad, encoder_grad)


SEQ = 4
PIECE = 512


def fits(mesh, encoder, key_weight, queries):
    return (
        mesh.shape["seq"] == SEQ
        and mesh.shape["head"] == 4
        and mesh.shape["grp"] == 2
        and encoder.shape == (DOCS * 2, 256, 4096)
        and key_weight.shape == (4096, 4096)
        and queries.shape == (DOCS * 2, 64, 4096)
    )


def prune_kernel(mask_ref, key_ref, value_ref, query_ref, cot_ref, own_ref, *message_refs):
    s, g = lax.axis_index("seq"), lax.axis_index("grp")
    left = lax.broadcasted_iota(jnp.int32, (1, 128), 1) < TILE

    def write(out_ref, first_tile, tiles, column):
        for t in range(tiles):
            tile = first_tile + t
            row = pl.ds(pl.multiple_of(tile * TILE, TILE), TILE)
            for side, ref in ((0, key_ref), (1, value_ref)):
                for part in range(2):
                    at = pl.ds(pl.multiple_of(column * 256 + part * 128, 128), 128)
                    first = mask_ref[side, tile, column * 4 + part * 2]
                    second = mask_ref[side, tile, column * 4 + part * 2 + 1]
                    keep = jnp.where(left, first, second).astype(F32)
                    to = side * 256 + part * 128
                    out_ref[t * TILE : (t + 1) * TILE, to : to + 128] = (
                        ref[row, at].astype(F32) * keep
                    ).astype(BF)

    first, second, third = message_refs[:3]
    for k, ref in enumerate(message_refs[3:]):
        at = pl.ds(pl.multiple_of(lax.bitwise_xor(s, k) * 256, 256), 256)
        ref[:, 0:256] = query_ref[:, at]
        ref[:, 256:512] = cot_ref[:, at]
    write(second, g * 8, 8, lax.bitwise_xor(s, 2))
    write(first, g * 8, 8, lax.bitwise_xor(s, 1))
    write(third, g * 8, 8, lax.bitwise_xor(s, 3))
    write(own_ref, 0, 16, s)


def prune(tile_mask, key_weight, value_weight, queries, cotangent):
    whole = pl.BlockSpec(memory_space=pltpu.VMEM)
    shapes = [(2 * PIECE, 512)] + [(PIECE, 512)] * 3 + [(64, 512)] * 4
    return pl.pallas_call(
        prune_kernel,
        out_shape=[jax.ShapeDtypeStruct(shape, BF) for shape in shapes],
        in_specs=[pl.BlockSpec(memory_space=pltpu.SMEM)] + [whole] * 4,
        out_specs=[whole] * len(shapes),
        compiler_params=pltpu.CompilerParams(vmem_limit_bytes=12 * 1024 * 1024),
        name="prune",
    )(tile_mask, key_weight, value_weight, queries, cotangent)


NT = (((1,), (1,)), ((), ()))
TN = (((0,), (0,)), ((), ()))
NN = (((1,), (0,)), ((), ()))


def dot(a, b, dims=NN):
    return lax.dot_general(a, b, dims, preferred_element_type=F32)


class Mover:
    def __init__(self, sems):
        self.sems = sems
        self.used = 0

    def start(self, pairs):
        copies = []
        for src, dst in pairs:
            copy = pltpu.make_async_copy(src, dst, self.sems.at[self.used])
            copy.start()
            self.used += 1
            copies.append(copy)
        return copies


def piece_rows(w_s, core, at, first, count):
    return w_s.at[core, pl.ds(pl.multiple_of(at * 1024 + first, 256), count)]


PACKED = 3 * 2 * PIECE


def pack_kernel(own, z1, z2, y1, y2, q0, q1, q2, q3, out_ref, sems):
    g = lax.axis_index("grp")
    pairs = [(own, out_ref.at[0 : 2 * PIECE])]
    for k, z, y in ((1, z1, y1), (2, z2, y2)):
        for piece, side in ((z, g), (y, 1 - g)):
            first = pl.multiple_of(2 * PIECE * k + side * PIECE, PIECE)
            pairs.append((piece, out_ref.at[pl.ds(first, PIECE)]))
    for k, piece in enumerate((q0, q1, q2, q3)):
        first = PACKED + 64 * lax.bitwise_xor(lax.axis_index("seq"), k)
        pairs.append((piece, out_ref.at[pl.ds(pl.multiple_of(first, 64), 64)]))
    for copy in Mover(sems).start(pairs):
        copy.wait()


def pack_call(*arrays):
    here = pl.BlockSpec(memory_space=pl.ANY)
    return pl.pallas_call(
        pack_kernel,
        out_shape=jax.ShapeDtypeStruct((PACKED + 256, 512), BF),
        in_specs=[here] * len(arrays),
        out_specs=pl.BlockSpec(memory_space=pltpu.VMEM),
        scratch_shapes=[pltpu.SemaphoreType.DMA((9,))],
        compiler_params=pltpu.CompilerParams(vmem_limit_bytes=6 * 1024 * 1024),
        cost_estimate=pl.CostEstimate(flops=1, bytes_accessed=1, transcendentals=0),
        name="pack",
    )(*arrays)


def early_weights(w_s, c, s, mine, theirs):
    pairs = []
    for core, packed in ((c, mine), (1 - c, theirs)):
        for k in range(3):
            rows = packed.at[2 * PIECE * k : 2 * PIECE * (k + 1)]
            pairs.append((rows, piece_rows(w_s, core, lax.bitwise_xor(s, k), 0, 2 * PIECE)))
    return pairs


def early_kernel(*refs):
    enc, e1, e2, e3, x1, x2, x3 = refs[:7]
    mine, theirs = refs[7:9]
    sum_ref, last_ref, enc_s, w_s, sems = refs[9:]
    s, h = lax.axis_index("seq"), lax.axis_index("head")
    c = lax.rem(h, 2)
    x = h // 2
    mover = Mover(sems)

    def rows_of(doc, at):
        return enc_s.at[pl.ds(pl.multiple_of(doc * 256 + at * 64, 64), 64)]

    pairs = [(enc.at[2 * i + c], rows_of(i, s)) for i in range(2)]
    for k, (own, other) in enumerate(((e1, x1), (e2, x2), (e3, x3))):
        at = lax.bitwise_xor(s, k + 1)
        pairs += [(own, rows_of(x, at)), (other, rows_of(1 - x, at))]
    pairs += early_weights(w_s, c, s, mine, theirs)
    for copy in mover.start(pairs):
        copy.wait()

    def columns(k):
        at = lax.bitwise_xor(s, k)
        return pl.ds(pl.multiple_of(at * 1024, 1024), 1024)

    for core in range(2):
        for half in range(2):
            row = slice(half * 256, half * 256 + 256)
            total = dot(enc_s[row, columns(0)], w_s[core, columns(0), :])
            for k in (1, 2):
                total = total + dot(enc_s[row, columns(k)], w_s[core, columns(k), :])
            sum_ref[core, row] = total
    last_ref[...] = enc_s[:, columns(3)]


def early_call(arrays):
    here = pl.BlockSpec(memory_space=pl.ANY)
    vmem = pl.BlockSpec(memory_space=pltpu.VMEM)
    return pl.pallas_call(
        early_kernel,
        out_shape=[
            jax.ShapeDtypeStruct((2, 512, 512), F32),
            jax.ShapeDtypeStruct((512, 1024), BF),
        ],
        in_specs=[here] * len(arrays),
        out_specs=[vmem] * 2,
        scratch_shapes=[
            pltpu.VMEM((512, 4096), BF),
            pltpu.VMEM((2, 4096, 512), BF),
            pltpu.SemaphoreType.DMA((18,)),
        ],
        compiler_params=pltpu.CompilerParams(vmem_limit_bytes=28 * 1024 * 1024),
        cost_estimate=pl.CostEstimate(
            flops=1, bytes_accessed=1, transcendentals=0
        ),
        name="early",
    )(*arrays)


def main_kernel(lengths, *refs):
    early_sum, last_rows = refs[:2]
    mine, theirs = refs[2:5], refs[5:8]
    (
        att_ref, qg_ref, own_ref,
        a3, b3, a2, b2, b10, a10, core_ref,
        w_s, qc_s, grad_s, sems,
    ) = refs[8:]
    s, g, h = lax.axis_index("seq"), lax.axis_index("grp"), lax.axis_index("head")
    c = lax.rem(h, 2)
    mover = Mover(sems)
    far = lax.bitwise_xor(s, 3)
    pairs = []
    for core, pieces in ((c, mine), (1 - c, theirs)):
        packed, z3, y3 = pieces
        for src, side in ((z3, g), (y3, 1 - g)):
            pairs.append((src, piece_rows(w_s, core, far, side * PIECE, PIECE)))
        for d in range(SEQ):
            pairs.append((packed.at[PACKED + 64 * d : PACKED + 64 * d + 64], qc_s.at[core, d]))
    now = mover.start(pairs)
    later = mover.start(early_weights(w_s, c, s, mine[0], theirs[0]))
    for copy in now:
        copy.wait()
    far_rows = pl.ds(pl.multiple_of(far * 1024, 1024), 1024)

    row_head = lax.broadcasted_iota(jnp.int32, (256, 256), 0) // DH
    col_head = lax.broadcasted_iota(jnp.int32, (256, 256), 1) // DH
    same = row_head == col_head
    position = lax.broadcasted_iota(jnp.int32, (256, 256), 1)

    def spread(block):
        four = jnp.concatenate([block] * 4, axis=0)
        return jnp.where(same, four, jnp.zeros_like(four))

    def gather_heads(block):
        kept = jnp.where(same, block, 0.0)
        return (kept[0:64] + kept[64:128]) + (kept[128:192] + kept[192:256])

    for core in range(2):
        slot = lax.rem(core + c, 2)
        for doc in range(2):
            row = slice(doc * 256, doc * 256 + 256)
            both = early_sum[core, row] + dot(last_rows[row], w_s[core, far_rows, :])
            keys = both[:, :256].astype(BF)
            values = both[:, 256:].astype(BF)
            at = pl.ds(pl.multiple_of((2 * doc + c) * 16, 16), 16)
            query = spread(qc_s[core, :, at, 0:256].reshape(64, 256))
            cot = spread(qc_s[core, :, at, 256:512].reshape(64, 256))
            live = position < lengths[2 * doc + c]
            scores = dot(query, keys, NT) * SCALE
            scores = jnp.where(live, scores, FLOOR_SCORE)
            row_max = jnp.max(scores, axis=1, keepdims=True)
            weights = jnp.where(live, jnp.exp(scores - row_max), 0.0)
            probs = weights / jnp.sum(weights, axis=1, keepdims=True)
            low = probs.astype(BF)
            output = dot(low, values)
            delta = jnp.sum(cot.astype(F32) * output, axis=1, keepdims=True)
            prob_grad = dot(cot, values, NT)
            score_grad = (probs * (prob_grad - delta) * SCALE).astype(BF)
            query_grad = dot(score_grad, keys)
            att_ref[slot, doc] = gather_heads(output).astype(BF)
            qg_ref[slot, doc] = gather_heads(query_grad).astype(BF)
            key_grad = dot(score_grad, query, TN).astype(BF)
            value_grad = dot(low, cot, TN).astype(BF)
            for at in range(4):
                first = lax.bitwise_xor(s, at) * 128 + doc * 64
                to = pl.ds(pl.multiple_of(first, 64), 64)
                grad_s[core, to, 0:256] = key_grad[at * 64 : at * 64 + 64]
                grad_s[core, to, 256:512] = value_grad[at * 64 : at * 64 + 64]

    for copy in later:
        copy.wait()
    cores = [core_ref.at[k] for k in range(4)]
    owns = [own_ref.at[k] for k in range(4)]
    for flip, outs in (
        (2, (a10.at[1], a10.at[0], a2, a3)),
        (3, (b10.at[1], b10.at[0], b2, b3)),
        (1, cores),
        (0, owns),
    ):
        block = lax.bitwise_xor(h, flip)
        for n in range(4):
            at = pl.ds(pl.multiple_of(block * 1024 + n * 256, 256), 256)
            total = dot(grad_s[0], w_s[0, at, :], NT) + dot(grad_s[1], w_s[1, at, :], NT)
            for k in range(4):
                for doc in range(2):
                    first = k * 128 + doc * 64
                    outs[k][doc, :, n * 256 : n * 256 + 256] = total[first : first + 64].astype(
                        outs[k].dtype
                    )


def main_call(lengths, arrays):
    here = pl.BlockSpec(memory_space=pl.ANY)
    vmem = pl.BlockSpec(memory_space=pltpu.VMEM)
    smem = pl.BlockSpec(memory_space=pltpu.SMEM)
    piece = jax.ShapeDtypeStruct((2, 64, 1024), BF)
    front = jax.ShapeDtypeStruct((2, 2, 64, 256), BF)
    return pl.pallas_call(
        main_kernel,
        out_shape=[
            front,
            front,
            jax.ShapeDtypeStruct((4, 2, 64, 1024), F32),
        ]
        + [piece] * 4
        + [jax.ShapeDtypeStruct((2, 2, 64, 1024), BF)] * 2
        + [jax.ShapeDtypeStruct((4, 2, 64, 1024), BF)],
        in_specs=[smem] + [vmem] * 2 + [here] * (len(arrays) - 2),
        out_specs=[vmem] * 10,
        scratch_shapes=[
            pltpu.VMEM((2, 4096, 512), BF),
            pltpu.VMEM((2, 4, 64, 512), BF),
            pltpu.VMEM((2, 512, 512), BF),
            pltpu.SemaphoreType.DMA((26,)),
        ],
        compiler_params=pltpu.CompilerParams(vmem_limit_bytes=34 * 1024 * 1024),
        cost_estimate=pl.CostEstimate(
            flops=6 * 10**9, bytes_accessed=24 * 2**20, transcendentals=2**18
        ),
        name="attend",
    )(lengths, *arrays)


def final_kernel(own, core, near, far, near1, near2, far1, far2, out_ref):
    c = lax.rem(lax.axis_index("head"), 2)
    for i in range(2):
        mine = (own[0, i] + near[1, i].astype(F32)) + (near1[i].astype(F32) + near2[i].astype(F32))
        theirs = (core[0, i].astype(F32) + far[1, i].astype(F32)) + (
            far1[i].astype(F32) + far2[i].astype(F32)
        )
        out_ref[2 * i + c] = mine.astype(BF)
        out_ref[2 * i + 1 - c] = theirs.astype(BF)


def small_call(kernel, shape, name, *arrays):
    vmem = pl.BlockSpec(memory_space=pltpu.VMEM)
    return pl.pallas_call(
        kernel,
        out_shape=jax.ShapeDtypeStruct(shape, BF),
        in_specs=[vmem] * len(arrays),
        out_specs=vmem,
        compiler_params=pltpu.CompilerParams(vmem_limit_bytes=12 * 1024 * 1024),
        name=name,
    )(*arrays)


def together(*values):
    return lax.optimization_barrier(values)


def summed(*parts):
    total = parts[0].astype(F32)
    for part in parts[1:]:
        total = total + part.astype(F32)
    return total.astype(BF)


def body(encoder, key_weight, value_weight, tile_mask, lengths, queries, cotangent):
    h = lax.axis_index("head")
    c = lax.rem(h, 2)

    def along(value, k):
        return lax.ppermute(value, "seq", [(a, a ^ k) for a in range(SEQ)])

    def flip(value, bits):
        return lax.ppermute(value, "head", [(a, a ^ bits) for a in range(4)])

    def across(value):
        return lax.ppermute(value, "grp", [(0, 1), (1, 0)])

    e0 = lax.dynamic_index_in_dim(encoder, h, 0, keepdims=False)
    e2 = along(e0, 2)
    e1 = along(e0, 1)
    w_own, m1, m2, m3, q0, q1, q2, q3 = prune(
        tile_mask, key_weight, value_weight, queries.reshape(64, 1024), cotangent.reshape(64, 1024)
    )
    e1, e2, m1, m2 = together(e1, e2, m1, m2)
    z2, z1 = along(m2, 2), along(m1, 1)
    e3 = along(e2, 1)
    x1, x2 = flip(e1, 2), flip(e2, 2)
    x1, x2, m3, q1, q2, q3 = together(x1, x2, m3, q1, q2, q3)
    z3 = along(m3, 3)
    q1, q2, q3 = along(q1, 1), along(q2, 2), along(q3, 3)
    x1, z2 = together(x1, z2)
    x2, e3 = together(x2, e3)
    y2 = across(z2)
    x3 = flip(e3, 2)
    y2, z1 = together(y2, z1)
    y1 = across(z1)
    z3, x3, w_own = together(z3, x3, w_own)
    y3 = across(z3)
    packed = pack_call(w_own, z1, z2, y1, y2, q0, q1, q2, q3)
    packed_there = flip(packed, 1)
    early = early_call([encoder, e1, e2, e3, x1, x2, x3, packed, packed_there])
    z3_there = flip(z3, 1)
    y3, *early = together(y3, *early)
    y3_there = flip(y3, 1)
    outs = main_call(lengths, early + [packed, z3, y3, packed_there, z3_there, y3_there])
    att, qgrad, own = outs[:3]
    a3, b3, a2, b2, b10, a10, to_core = outs[3:]
    from_core = flip(to_core, 1)
    front = jnp.stack([att, qgrad], axis=1)
    other = flip(front[1], 1)
    back = jnp.stack([front[0], other]).reshape(2, 2, 2, SEQ, 16, 256).transpose(3, 0, 1, 2, 4, 5)
    b3, a3 = flip(b3, 3), flip(a3, 2)
    b3, b2, a2 = together(b3, b2, a2)
    b3, core, back = together(b3, from_core, back)
    back = lax.all_to_all(back, "seq", split_axis=0, concat_axis=0, tiled=True)
    b2, a2 = flip(b2, 3), flip(a2, 2)
    far3, own = together(summed(core[3], b3), own)
    far3 = along(far3, 1)
    near3, core = together(summed(own[3], a3), core)
    near3 = along(near3, 1)
    b2, b10, a10 = together(b2, b10, a10)
    b10, a10 = flip(b10, 3), flip(a10, 2)
    core, back = together(core, back)
    far2, own = together(summed(core[2], b2, far3), own)
    far2 = along(far2, 2)
    near2, core = together(summed(own[2], a2, near3), core)
    near2 = along(near2, 2)
    near1, core = together(summed(own[1], a10[0]), core)
    near1 = along(near1, 1)
    b10, near2, far2 = together(b10, near2, far2)
    far1 = along(summed(core[1], b10[0]), 1)
    from_core = core
    back = back.transpose(2, 3, 1, 4, 0, 5).reshape(2, 2, 2, 16, 1024)
    back = jnp.where(c == 0, back, back[:, :, ::-1])
    back = back.reshape(2, DOCS, 16, 1024)
    a10, back = together(a10, back)
    encoder_grad = small_call(
        final_kernel, (DOCS, 64, 1024), "final", own, from_core, a10, b10, near1, near2, far1, far2
    )
    return (back[0], back[1], encoder_grad)


def solution(mesh):
    placed = (
        P("grp", "seq", None),
        P("seq", "head"),
        P("seq", "head"),
        P(None, "seq", "head"),
        P("grp"),
        P("grp", "seq", "head"),
        P("grp", "seq", "head"),
    )

    def step(*arrays):
        plan = body if fits(mesh, arrays[0], arrays[1], arrays[5]) else general_body
        return jax.shard_map(
            plan,
            mesh=mesh,
            in_specs=placed,
            out_specs=(P("grp", "seq", "head"),) * 3,
            check_vma=False,
        )(*arrays)

    return step
```
